512 devices in a mesh: page: 16 (over z_lo, core), tensor: 32 (over x, y, z_hi).
Axes of the slice: x: 4, y: 4, z: 16 (z_hi: 2, z_lo: 8; z = z_hi * 8 + z_lo), core: 2. Of those that a mesh axis runs over, the one named last changes fastest.
Arguments:
- tokens: bfloat16 [2048, 2560], P('tensor'), may hold values from -6 to 6
- norm_gain: float32 [2560], replicated, may hold values from 0.1 to 1.9
- w_query: bfloat16 [2560, 2560], P(None, 'tensor'), may hold values from -0.125 to 0.125
- w_keyvalue: bfloat16 [2560, 1280], P(None, 'tensor'), may hold values from -0.125 to 0.125
- cache: bfloat16 [128, 32, 128, 1280], P('page', 'tensor'), may hold values from -180 to 180, as said below
- page_count: int32 [16, 32], P('page', 'tensor'), may hold values from 1 to 8, as said below
- page_owner: int32 [128, 32], P('page', 'tensor'), may hold values from 0 to 63
- keep_rows: int32 [128, 32, 32], P('page', 'tensor'), may hold values from 0 to 127, as said below
- dest_slot: int32 [128, 32], P('page', 'tensor'), may hold values from 0 to 15, as said below
Outputs:
- attended: bfloat16 [2048, 2560], P('tensor')
- compacted: bfloat16 [256, 32, 32, 1280], P('page', 'tensor')
The draws below stay inside these ranges and needn't reach their ends.
Inputs may be any that keep to these rules, and one draw needn't show every extreme that they name: `cache`: normal values within 4.5; keys may carry a row scale. `page_count`: in every tensor index some holder has all 8 slots live. `keep_rows`: distinct within each page. `dest_slot`: value q * 1 + c names position c of holder q (with 1 = 1, c = 0); the live slots of one holder and tensor index name distinct destinations, and every holder's first slot of a tensor index goes to position 0 of one common holder of that index.
All inputs are finite; a program needn't handle non-finite values.
Results may differ from the reference program's by a relative error of at most 0.012.
Values may be sent and summed in bfloat16 or wider, within the bound.
No kernel may reach another device: no remote copies, remote signals or barrier semaphores. Data moves between devices by JAX's collectives and lax.ppermute only.
A program may use at most 64 MiB of HBM per device.

```python
import math
import jax
import jax.numpy as jnp
import numpy as np
from jax import lax

D = 2560
HEADS = 32
KV_HEADS = 8
HEAD_DIM = 80
RT = 64
SRC = 8
ROWS = 128
KEEP = 32
GROUPS = 32
HOLDERS = 16
REQUESTS = 2048
SLOTS = 128
CAP = 1
DST = 16
KVW = 1280


def draw_cache(key, part):
    base = jnp.clip(jax.random.normal(key, (SLOTS, GROUPS, ROWS, KVW), jnp.float32), -4.5, 4.5)
    return base.astype(jnp.bfloat16)


def draw_page_count(key, part):
    first_draw = jax.random.randint(jax.random.fold_in(key, 1), (HOLDERS, GROUPS), 0, SRC)
    second_draw = jax.random.randint(jax.random.fold_in(key, 2), (HOLDERS, GROUPS), 0, SRC)
    counts = 1 + first_draw * (second_draw + SRC - 1) // max(2 * (SRC - 1), 1)
    busiest = jax.random.randint(jax.random.fold_in(key, 3), (GROUPS,), 0, HOLDERS)
    counts = jnp.where(jnp.arange(HOLDERS)[:, None] == busiest[None, :], SRC, counts)
    return counts.astype(jnp.int32)


def draw_keep_rows(key, part):
    noise = jax.random.randint(key, (SLOTS, GROUPS, ROWS), 0, 1 << 20)
    scores_int = noise * ROWS + jnp.arange(ROWS, dtype=jnp.int32)
    order = jnp.argsort(scores_int, axis=-1)
    return order[:, :, :KEEP].astype(jnp.int32)


def draw_dest_slot(key, part):
    common = jax.random.randint(jax.random.fold_in(key, 11), (GROUPS,), 0, HOLDERS)
    noise = jax.random.randint(jax.random.fold_in(key, 12), (HOLDERS, GROUPS, DST), 0, 1 << 20)
    pair_index = jnp.arange(DST, dtype=jnp.int32)
    pair_holder = pair_index // CAP
    pair_place = pair_index % CAP
    ranked = noise * DST + pair_index
    ranked = jnp.where(pair_holder[None, None, :] == common[None, :, None], pair_place[None, None, :] - CAP, ranked)
    order = jnp.argsort(ranked, axis=-1)[:, :, :SRC]
    return jnp.transpose(order, (0, 2, 1)).reshape(SLOTS, GROUPS).astype(jnp.int32)


def touch_ends(result, stream_key, smallest, high):
    shape = result.shape
    spot = [jax.random.randint(jax.random.fold_in(stream_key, axis), (), 0, shape[axis]) for axis in range(len(shape))]
    result = result.at[tuple(spot)].set(smallest)
    longest = shape.index(max(shape))
    spot[longest] = (spot[longest] + 1) % shape[longest]
    return result.at[tuple(spot)].set(high)


def level_of(rng, shape, cuts, smallest, high):
    gain, own = 1.0, jax.random.fold_in(rng, 6)
    for position, parts in cuts:
        draws = jnp.exp(jax.random.uniform(jax.random.fold_in(own, position), (parts,), jnp.float32, smallest / len(cuts), high / len(cuts)))
        gain = gain * jnp.repeat(draws, shape[position] // parts).reshape([-1 if axis == position else 1 for axis in range(len(shape))])
    return gain


def rank_bounds(amount, lean):
    loads = [(1 << 20) // math.isqrt(standing ** lean) + 1 for standing in range(1, amount + 1)]
    width = 1 + sum(loads) // (1 << 30)
    return np.cumsum(np.array([max(1, weight // width) for weight in loads]))


def ranked_ids(key, shape, count, slope):
    table = rank_bounds(count, slope)
    ticket = jax.random.randint(jax.random.fold_in(key, 1), shape, 0, int(table[count - 1]))
    standing = jnp.searchsorted(jnp.asarray(table, jnp.int32), ticket, side="right")
    return jax.random.permutation(jax.random.fold_in(key, 2), count)[standing].astype(jnp.int32)


def gaussian(rng, extent, deviation, bound, split=(), kind=jnp.bfloat16):
    values = jax.random.normal(rng, extent, jnp.float32) * deviation
    if len(split) > 0:
        values = level_of(rng, extent, split, -0.22, 0.18) * values
    return jnp.clip(values, min=-bound, max=bound).astype(kind)


def setup_inputs(seed: int = 0) -> dict:
    key_of = jax.random.split(jax.random.key(seed), 10)
    tokens = gaussian(key_of[0], (REQUESTS, D), 1.0, 6.0, ((0, 32),))
    norm_gain = jnp.clip(1.0 + 0.18 * jax.random.normal(key_of[1], (D,), jnp.float32), 0.1, 1.9)
    w_query = gaussian(key_of[2], (D, HEADS * HEAD_DIM), D ** -0.5, 0.125, ((1, 32),))
    w_keyvalue = gaussian(key_of[3], (D, KVW), D ** -0.5, 0.125, ((1, 32),))
    cache = draw_cache(jax.random.fold_in(key_of[9], 71), 0)
    page_count = draw_page_count(jax.random.fold_in(key_of[9], 71), 0)
    page_owner = touch_ends(ranked_ids(key_of[6], (SLOTS, GROUPS), RT, 2), jax.random.fold_in(key_of[6], 3), 0, RT - 1).astype(jnp.int32)
    keep_rows = draw_keep_rows(jax.random.fold_in(key_of[9], 71), 0)
    dest_slot = draw_dest_slot(jax.random.fold_in(key_of[9], 71), 0)
    return {"tokens": tokens, "norm_gain": norm_gain, "w_query": w_query, "w_keyvalue": w_keyvalue, "cache": cache, "page_count": page_count, "page_owner": page_owner, "keep_rows": keep_rows, "dest_slot": dest_slot}


EPSILON = 1e-05
NEGATIVE = -1e+30

def reference(tokens, norm_gain, w_query, w_keyvalue, cache, page_count, page_owner, keep_rows, dest_slot):
    widened = tokens.astype(jnp.float32)
    normed = (widened * lax.rsqrt(lax.optimization_barrier(jnp.mean(widened * widened, axis=-1, keepdims=True)) + EPSILON) * norm_gain).astype(jnp.bfloat16)
    queries = jnp.dot(normed, w_query, preferred_element_type=jnp.float32).astype(jnp.bfloat16)
    keyvalues = jnp.dot(normed, w_keyvalue, preferred_element_type=jnp.float32).astype(jnp.bfloat16)
    retained = jax.vmap(jax.vmap(lambda one_page, row_picks: one_page[row_picks]))(cache, keep_rows)
    slot_index = jnp.arange(SLOTS, dtype=jnp.int32)
    sender = slot_index // SRC
    is_live = (slot_index % SRC)[:, None] < page_count[sender]
    target = dest_slot // CAP * DST + sender[:, None] * CAP + dest_slot % CAP
    target = jnp.where(is_live, target, HOLDERS * DST).astype(jnp.int32)
    group_ids = jnp.broadcast_to(jnp.arange(GROUPS, dtype=jnp.int32)[None, :], target.shape)
    compacted = jnp.zeros((HOLDERS * DST, GROUPS, KEEP, KVW), cache.dtype).at[target, group_ids].set(retained, mode='drop')
    score_scale = HEAD_DIM ** (-0.5)
    repeat_count = HEADS // KV_HEADS

    def one_group(group_index):
        rows_q = lax.dynamic_slice_in_dim(queries, group_index * RT, RT, 0).astype(jnp.float32)
        rows_q = rows_q.reshape(RT, KV_HEADS, repeat_count, HEAD_DIM)
        rows_kv = lax.dynamic_slice_in_dim(keyvalues, group_index * RT, RT, 0).astype(jnp.float32)
        rows_kv = rows_kv.reshape(RT, 2, KV_HEADS, HEAD_DIM)
        group_pages = lax.dynamic_index_in_dim(retained, group_index, 1, keepdims=False).astype(jnp.float32)
        slot_keys = group_pages[:, :, :KV_HEADS * HEAD_DIM].reshape(SLOTS, KEEP, KV_HEADS, HEAD_DIM)
        slot_values = group_pages[:, :, KV_HEADS * HEAD_DIM:].reshape(SLOTS, KEEP, KV_HEADS, HEAD_DIM)
        owners = lax.dynamic_index_in_dim(page_owner, group_index, 1, keepdims=False)
        alive = lax.dynamic_index_in_dim(is_live, group_index, 1, keepdims=False)
        member = (owners[None, :] == jnp.arange(RT, dtype=jnp.int32)[:, None]) & alive[None, :]
        valid = member[:, None, None, :, None]
        scores = jnp.einsum('rgkd,sjgd->rgksj', rows_q, slot_keys) * score_scale
        own_score = jnp.einsum('rgkd,rgd->rgk', rows_q, rows_kv[:, 0]) * score_scale
        row_peak = jnp.maximum(lax.optimization_barrier(jnp.max(jnp.where(valid, scores, NEGATIVE), axis=(3, 4))), own_score)
        weights = jnp.where(valid, jnp.exp(scores - row_peak[..., None, None]), 0.0)
        own_weight = jnp.exp(own_score - row_peak)
        total = lax.optimization_barrier(jnp.sum(weights, axis=(3, 4))) + own_weight
        rounded = lax.optimization_barrier(weights.astype(jnp.bfloat16)).astype(jnp.float32)
        mixed = jnp.einsum('rgksj,sjgd->rgkd', rounded, slot_values)
        mixed = mixed + own_weight[..., None] * rows_kv[:, 1][:, :, None, :]
        return (mixed / total[..., None]).reshape(RT, HEADS * HEAD_DIM).astype(jnp.bfloat16)
    attended = lax.map(one_group, jnp.arange(GROUPS, dtype=jnp.int32)).reshape(REQUESTS, HEADS * HEAD_DIM)
    return (attended, compacted)
```

```python
import functools

import jax
import jax.numpy as jnp
from jax import lax
from jax.experimental import pallas as pl
from jax.experimental.pallas import tpu as pltpu
from jax.sharding import PartitionSpec as P

HEADS = 32
KV_HEADS = 8
HEAD_DIM = 80
EPSILON = 1e-05
NEGATIVE = -1e30

CHIPS = 8
PLANE = 16
SOURCES = 8
KEEP = 32
LANES = SOURCES * KEEP
BLOCK = 2 * HEAD_DIM + 16

PLANE_GROUPS = [[2 * i + half for i in range(PLANE)] for half in range(2)]
RUN_GROUPS = [[2 * z + core for z in range(CHIPS)] for core in range(2)]
OTHER_HALF = [(i, i ^ 1) for i in range(2 * PLANE)]
OTHER_CORE = [(i, i ^ 1) for i in range(2 * CHIPS)]


def select_kernel(count_ref, owner_ref, dest_ref, keep_ref, page_ref, out_ref, kv_ref, kept_ref):
    slot = pl.program_id(0)

    @pl.when(slot == 0)
    def _():
        out_ref[...] = jnp.zeros_like(out_ref)

    rows = page_ref.shape[1]
    picks = jnp.broadcast_to(keep_ref[0], (rows, KEEP))
    chosen = (picks == lax.broadcasted_iota(jnp.int32, (rows, KEEP), 0)).astype(jnp.float32)
    kept = jnp.dot(
        chosen.T.astype(jnp.bfloat16), page_ref[0], preferred_element_type=jnp.float32
    ).astype(jnp.bfloat16)
    kept_ref[pl.ds(pl.multiple_of(slot * KEEP, KEEP), KEEP), :] = kept

    @pl.when(slot < count_ref[0])
    def _():
        out_ref[dest_ref[slot]] = kept

    @pl.when(slot == SOURCES - 1)
    def _():
        turned = kept_ref[...].T
        lane_slot = lax.broadcasted_iota(jnp.int32, (16, LANES), 1) // KEEP
        tags = jnp.full((16, LANES), -1, jnp.int32)
        for s in range(SOURCES):
            tag = jnp.where(s < count_ref[0], owner_ref[s], -1)
            tags = jnp.where(lane_slot == s, tag, tags)
        tags = tags.astype(jnp.float32).astype(jnp.bfloat16)
        values_at = KV_HEADS * HEAD_DIM
        for g in range(KV_HEADS):
            low = g * HEAD_DIM
            kv_ref[g, 0:HEAD_DIM] = turned[low : low + HEAD_DIM]
            kv_ref[g, HEAD_DIM : 2 * HEAD_DIM] = turned[values_at + low : values_at + low + HEAD_DIM]
            kv_ref[g, 2 * HEAD_DIM :] = tags


def select_rows(page_count, page_owner, dest_slot, keep_rows, cache):
    sources, _, rows, width = cache.shape
    holders = 2 * CHIPS
    return pl.pallas_call(
        select_kernel,
        out_shape=(
            jax.ShapeDtypeStruct((holders, KEEP, width), cache.dtype),
            jax.ShapeDtypeStruct((KV_HEADS, BLOCK, LANES), cache.dtype),
        ),
        grid_spec=pltpu.PrefetchScalarGridSpec(
            num_scalar_prefetch=3,
            grid=(sources,),
            in_specs=[
                pl.BlockSpec((1, 1, KEEP), lambda s, *_: (s, 0, 0)),
                pl.BlockSpec((1, rows, width), lambda s, *_: (s, 0, 0)),
            ],
            out_specs=[
                pl.BlockSpec((holders, KEEP, width), lambda s, *_: (0, 0, 0)),
                pl.BlockSpec((KV_HEADS, BLOCK, LANES), lambda s, *_: (0, 0, 0)),
            ],
            scratch_shapes=[pltpu.VMEM((LANES, width), cache.dtype)],
        ),
        name="select_rows",
    )(
        page_count.reshape(1),
        page_owner.reshape(sources),
        dest_slot.reshape(sources),
        keep_rows,
        cache.reshape(sources, rows, width),
    )


def attend_kernel(own_ref, near_ref, far_ref, out_ref, score_ref):
    scale = HEAD_DIM ** (-0.5)
    requests = own_ref.shape[1]
    query = jnp.concatenate([own_ref[0, :, :HEAD_DIM], own_ref[1, :, :HEAD_DIM]], axis=0)
    new_key = own_ref[0, :, HEAD_DIM:].astype(jnp.float32)
    new_value = own_ref[1, :, HEAD_DIM:].astype(jnp.float32)
    new_key = jnp.concatenate([new_key, new_key], axis=0)
    new_value = jnp.concatenate([new_value, new_value], axis=0)
    own = jnp.sum(query.astype(jnp.float32) * new_key, axis=1, keepdims=True) * scale
    request = lax.broadcasted_iota(jnp.int32, (2 * requests, 1), 0) % requests
    request = request.astype(jnp.float32)
    blocks = [near_ref.at[i] for i in range(CHIPS)] + [far_ref.at[i] for i in range(CHIPS)]
    top = jnp.full((2 * requests, LANES), NEGATIVE, jnp.float32)
    for b, block in enumerate(blocks):
        score = jnp.dot(query, block[0:HEAD_DIM, :], preferred_element_type=jnp.float32) * scale
        tag = block[2 * HEAD_DIM : BLOCK, :].astype(jnp.float32)[0:1]
        score = jnp.where(tag == request, score, NEGATIVE)
        score_ref[:, b * LANES : (b + 1) * LANES] = score
        top = jnp.maximum(top, score)
    peak = jnp.maximum(jnp.max(top, axis=1, keepdims=True), own)
    own_weight = jnp.exp(own - peak)
    total = jnp.zeros((2 * requests, LANES), jnp.float32)
    mixed = jnp.zeros((2 * requests, HEAD_DIM), jnp.float32)
    for b, block in enumerate(blocks):
        weight = jnp.exp(score_ref[:, b * LANES : (b + 1) * LANES] - peak)
        total = total + weight
        mixed = mixed + lax.dot_general(
            weight.astype(jnp.bfloat16),
            block[HEAD_DIM : 2 * HEAD_DIM, :],
            (((1,), (1,)), ((), ())),
            preferred_element_type=jnp.float32,
        )
    total = jnp.sum(total, axis=1, keepdims=True) + own_weight
    result = (mixed + own_weight * new_value) / total
    out_ref[...] = result.T.astype(jnp.bfloat16)


def attend(own, near, far):
    requests = own.shape[1]
    return pl.pallas_call(
        attend_kernel,
        out_shape=jax.ShapeDtypeStruct((HEAD_DIM, 2 * requests), jnp.bfloat16),
        in_specs=[pl.BlockSpec(memory_space=pltpu.VMEM)] * 3,
        out_specs=pl.BlockSpec(memory_space=pltpu.VMEM),
        scratch_shapes=[pltpu.VMEM((2 * requests, 2 * CHIPS * LANES), jnp.float32)],
        name="attend",
    )(own, near, far)


def assemble_kernel(core_ref, near_ref, far_ref, out_ref):
    first = core_ref[0] == 0
    requests = out_ref.shape[0]
    for z in range(CHIPS):
        near = near_ref[z].astype(jnp.float32)
        far = far_ref[z].astype(jnp.float32)
        for core in range(2):
            piece = jnp.where(first == (core == 0), near, far).T.astype(jnp.bfloat16)
            for j in range(2):
                at = (4 * z + 2 * core + j) * HEAD_DIM
                out_ref[:, at : at + HEAD_DIM] = piece[j * requests : (j + 1) * requests]


def assemble(core, near, far):
    requests = near.shape[2] // 2
    return pl.pallas_call(
        assemble_kernel,
        out_shape=jax.ShapeDtypeStruct((requests, HEADS * HEAD_DIM), jnp.bfloat16),
        in_specs=[pl.BlockSpec(memory_space=pltpu.SMEM)] + [pl.BlockSpec(memory_space=pltpu.VMEM)] * 2,
        out_specs=pl.BlockSpec(memory_space=pltpu.VMEM),
        name="assemble",
    )(core.reshape(1), near, far)


def per_device(
    tokens, norm_gain, w_query, w_keyvalue, cache, page_count, page_owner, keep_rows, dest_slot
):
    holders = lax.axis_size("page")
    groups = lax.axis_size("tensor")
    holder = lax.axis_index("page")
    half = lax.axis_index("tensor") % 2
    share = tokens.shape[0] // holders

    mine = lax.dynamic_slice_in_dim(tokens, holder * share, share, 0)
    widened = mine.astype(jnp.float32)
    normed = (
        widened
        * lax.rsqrt(jnp.mean(widened * widened, axis=-1, keepdims=True) + EPSILON)
        * norm_gain
    ).astype(jnp.bfloat16)
    across = lax.ppermute(normed, "tensor", OTHER_HALF)

    compact, by_head = select_rows(page_count, page_owner, dest_slot, keep_rows, cache)
    near = lax.all_to_all(
        by_head, "page", 0, 0, axis_index_groups=RUN_GROUPS, tiled=True
    )
    far = lax.ppermute(near, "page", OTHER_CORE)
    arrived = lax.all_to_all(compact, "page", 0, 0, tiled=True)

    both = jnp.where(
        half == 0, jnp.stack([normed, across]), jnp.stack([across, normed])
    )
    rows = lax.all_to_all(
        jnp.broadcast_to(both[None], (PLANE,) + both.shape),
        "tensor",
        0,
        0,
        axis_index_groups=PLANE_GROUPS,
        tiled=True,
    ).reshape(groups * share, -1)
    query_part = jnp.dot(rows, w_query, preferred_element_type=jnp.float32)
    pair_part = jnp.dot(rows, w_keyvalue, preferred_element_type=jnp.float32)
    projected = jnp.concatenate([query_part, pair_part], axis=1).astype(jnp.bfloat16)
    back = lax.all_to_all(
        projected.reshape(groups, share, -1), "tensor", 0, 0, tiled=True
    )
    query = back[:, :, :HEAD_DIM].reshape(CHIPS, 2, 2, share, HEAD_DIM)
    pair = back[:, :, HEAD_DIM:].reshape(2, CHIPS, 2, share, HEAD_DIM // 2)
    pair = jnp.transpose(pair, (1, 0, 3, 2, 4)).reshape(CHIPS, 1, 2, share, HEAD_DIM)
    pair = jnp.broadcast_to(pair, query.shape)
    outgoing = jnp.concatenate([query, pair], axis=-1).reshape(holders, 2, share, 2 * HEAD_DIM)
    own = lax.all_to_all(outgoing, "page", 0, 0, tiled=True)
    own = jnp.transpose(own, (1, 0, 2, 3)).reshape(2, holders * share, 2 * HEAD_DIM)

    piece = attend(own, near, far)
    near_out = lax.all_to_all(
        jnp.broadcast_to(piece[None], (CHIPS,) + piece.shape),
        "page",
        0,
        0,
        axis_index_groups=RUN_GROUPS,
        tiled=True,
    )
    far_out = lax.ppermute(near_out, "page", OTHER_CORE)
    attended = assemble(holder % 2, near_out, far_out)
    return attended, arrived[:, None]


def solution(mesh):
    return jax.shard_map(
        per_device,
        mesh=mesh,
        in_specs=(
            P("tensor", None),
            P(),
            P(None, "tensor"),
            P(None, "tensor"),
            P("page", "tensor", None, None),
            P("page", "tensor"),
            P("page", "tensor"),
            P("page", "tensor", None),
            P("page", "tensor"),
        ),
        out_specs=(P("tensor", None), P("page", "tensor", None, None)),
        check_vma=False,
    )
```

```python
import functools

import jax
import jax.numpy as jnp
from jax import lax
from jax.experimental import pallas as pl
from jax.experimental.pallas import tpu as pltpu
from jax.sharding import PartitionSpec as P

HEADS = 32
KV_HEADS = 8
HEAD_DIM = 80
EPSILON = 1e-05
NEGATIVE = -1e30

CHIPS = 8
PLANE = 16
SOURCES = 8
KEEP = 32
LANES = SOURCES * KEEP
BLOCK = 2 * HEAD_DIM + 16

PLANE_GROUPS = [[2 * i + half for i in range(PLANE)] for half in range(2)]
RUN_GROUPS = [[2 * z + core for z in range(CHIPS)] for core in range(2)]
OTHER_HALF = [(i, i ^ 1) for i in range(2 * PLANE)]
OTHER_CORE = [(i, i ^ 1) for i in range(2 * CHIPS)]
OTHER_CHIP = [[(i, i ^ (2 * d)) for i in range(2 * CHIPS)] for d in range(CHIPS)]


def select_kernel(
    place_ref, count_ref, owner_ref, dest_ref, keep_ref, page_ref, *refs
):
    out_refs, kv_refs = refs[:CHIPS], refs[CHIPS : 2 * CHIPS]
    kept_ref, turned_ref = refs[2 * CHIPS :]
    slot = pl.program_id(0)
    chip, core = place_ref[0], place_ref[1]

    @pl.when(slot == 0)
    def _():
        for ref in out_refs:
            ref[...] = jnp.zeros_like(ref)

    rows = page_ref.shape[1]
    picks = jnp.broadcast_to(keep_ref[0], (rows, KEEP))
    chosen = (picks == lax.broadcasted_iota(jnp.int32, (rows, KEEP), 0)).astype(jnp.float32)
    kept = jnp.dot(
        chosen.T.astype(jnp.bfloat16), page_ref[0], preferred_element_type=jnp.float32
    ).astype(jnp.bfloat16)
    kept_ref[pl.ds(pl.multiple_of(slot * KEEP, KEEP), KEEP), :] = kept
    target = dest_ref[slot]
    step = (target // 2) ^ chip
    cross = (target % 2) ^ core
    live = slot < count_ref[0]
    for d in range(CHIPS):

        @pl.when(live & (step == d))
        def _():
            out_refs[d][cross] = kept

    @pl.when(slot == SOURCES - 1)
    def _():
        turned_ref[...] = kept_ref[...].T
        lane_slot = lax.broadcasted_iota(jnp.int32, (16, LANES), 1) // KEEP
        tags = jnp.full((16, LANES), -1, jnp.int32)
        for s in range(SOURCES):
            tag = jnp.where(s < count_ref[0], owner_ref[s], -1)
            tags = jnp.where(lane_slot == s, tag, tags)
        tags = tags.astype(jnp.float32).astype(jnp.bfloat16)
        values_at = KV_HEADS * HEAD_DIM
        for d in range(CHIPS):
            low = pl.multiple_of((chip ^ d) * HEAD_DIM, HEAD_DIM)
            kv_refs[d][0:HEAD_DIM] = turned_ref[pl.ds(low, HEAD_DIM), :]
            kv_refs[d][HEAD_DIM : 2 * HEAD_DIM] = turned_ref[
                pl.ds(pl.multiple_of(values_at + low, HEAD_DIM), HEAD_DIM), :
            ]
            kv_refs[d][2 * HEAD_DIM :] = tags


def select_rows(place, page_count, page_owner, dest_slot, keep_rows, cache):
    sources, _, rows, width = cache.shape
    out = jax.ShapeDtypeStruct((2, KEEP, width), cache.dtype)
    kv = jax.ShapeDtypeStruct((BLOCK, LANES), cache.dtype)
    results = pl.pallas_call(
        select_kernel,
        out_shape=[out] * CHIPS + [kv] * CHIPS,
        grid_spec=pltpu.PrefetchScalarGridSpec(
            num_scalar_prefetch=4,
            grid=(sources,),
            in_specs=[
                pl.BlockSpec((1, 1, KEEP), lambda s, *_: (s, 0, 0)),
                pl.BlockSpec((1, rows, width), lambda s, *_: (s, 0, 0)),
            ],
            out_specs=[pl.BlockSpec(out.shape, lambda s, *_: (0, 0, 0))] * CHIPS
            + [pl.BlockSpec(kv.shape, lambda s, *_: (0, 0))] * CHIPS,
            scratch_shapes=[
                pltpu.VMEM((LANES, width), cache.dtype),
                pltpu.VMEM((width, LANES), cache.dtype),
            ],
        ),
        name="select_rows",
    )(
        place,
        page_count.reshape(1),
        page_owner.reshape(sources),
        dest_slot.reshape(sources),
        keep_rows,
        cache.reshape(sources, rows, width),
    )
    return results[:CHIPS], results[CHIPS:]


def place_kernel(place_ref, *refs):
    got_refs, cross_ref, out_ref = refs[:CHIPS], refs[CHIPS], refs[CHIPS + 1]
    chip, core = place_ref[0], place_ref[1]
    for d in range(CHIPS):
        at = 2 * (chip ^ d)
        out_ref[at + core] = got_refs[d][0]
        out_ref[at + 1 - core] = cross_ref[d]


def place_pages(place, got, cross):
    return pl.pallas_call(
        place_kernel,
        out_shape=jax.ShapeDtypeStruct((2 * CHIPS,) + cross.shape[1:], cross.dtype),
        in_specs=[pl.BlockSpec(memory_space=pltpu.SMEM)]
        + [pl.BlockSpec(memory_space=pltpu.VMEM)] * (CHIPS + 1),
        out_specs=pl.BlockSpec(memory_space=pltpu.VMEM),
        name="place_pages",
    )(place, *got, cross)


def attend_kernel(own_ref, *refs):
    near_refs = refs[:CHIPS]
    far_ref, out_ref, score_ref = refs[CHIPS:]
    scale = HEAD_DIM ** (-0.5)
    requests = own_ref.shape[1]
    query = jnp.concatenate([own_ref[0, :, :HEAD_DIM], own_ref[1, :, :HEAD_DIM]], axis=0)
    new_key = own_ref[0, :, HEAD_DIM:].astype(jnp.float32)
    new_value = own_ref[1, :, HEAD_DIM:].astype(jnp.float32)
    new_key = jnp.concatenate([new_key, new_key], axis=0)
    new_value = jnp.concatenate([new_value, new_value], axis=0)
    own = jnp.sum(query.astype(jnp.float32) * new_key, axis=1, keepdims=True) * scale
    request = lax.broadcasted_iota(jnp.int32, (2 * requests, 1), 0) % requests
    request = request.astype(jnp.float32)
    blocks = list(near_refs) + [far_ref.at[i] for i in range(CHIPS)]
    top = jnp.full((2 * requests, LANES), NEGATIVE, jnp.float32)
    for b, block in enumerate(blocks):
        score = jnp.dot(query, block[0:HEAD_DIM, :], preferred_element_type=jnp.float32) * scale
        tag = block[2 * HEAD_DIM : BLOCK, :].astype(jnp.float32)[0:1]
        score = jnp.where(tag == request, score, NEGATIVE)
        score_ref[:, b * LANES : (b + 1) * LANES] = score
        top = jnp.maximum(top, score)
    peak = jnp.maximum(jnp.max(top, axis=1, keepdims=True), own)
    own_weight = jnp.exp(own - peak)
    total = jnp.zeros((2 * requests, LANES), jnp.float32)
    mixed = jnp.zeros((2 * requests, HEAD_DIM), jnp.float32)
    for b, block in enumerate(blocks):
        weight = jnp.exp(score_ref[:, b * LANES : (b + 1) * LANES] - peak)
        total = total + weight
        mixed = mixed + lax.dot_general(
            weight.astype(jnp.bfloat16),
            block[HEAD_DIM : 2 * HEAD_DIM, :],
            (((1,), (1,)), ((), ())),
            preferred_element_type=jnp.float32,
        )
    total = jnp.sum(total, axis=1, keepdims=True) + own_weight
    result = (mixed + own_weight * new_value) / total
    out_ref[...] = result.T.astype(jnp.bfloat16)


def attend(own, near, far):
    requests = own.shape[1]
    return pl.pallas_call(
        attend_kernel,
        out_shape=jax.ShapeDtypeStruct((HEAD_DIM, 2 * requests), jnp.bfloat16),
        in_specs=[pl.BlockSpec(memory_space=pltpu.VMEM)] * (2 + CHIPS),
        out_specs=pl.BlockSpec(memory_space=pltpu.VMEM),
        scratch_shapes=[pltpu.VMEM((2 * requests, 2 * CHIPS * LANES), jnp.float32)],
        name="attend",
    )(own, *near, far)


def assemble_kernel(core_ref, near_ref, far_ref, out_ref):
    first = core_ref[0] == 0
    requests = out_ref.shape[0]
    for z in range(CHIPS):
        near = near_ref[z].astype(jnp.float32)
        far = far_ref[z].astype(jnp.float32)
        for core in range(2):
            piece = jnp.where(first == (core == 0), near, far).T.astype(jnp.bfloat16)
            for j in range(2):
                at = (4 * z + 2 * core + j) * HEAD_DIM
                out_ref[:, at : at + HEAD_DIM] = piece[j * requests : (j + 1) * requests]


def assemble(core, near, far):
    requests = near.shape[2] // 2
    return pl.pallas_call(
        assemble_kernel,
        out_shape=jax.ShapeDtypeStruct((requests, HEADS * HEAD_DIM), jnp.bfloat16),
        in_specs=[pl.BlockSpec(memory_space=pltpu.SMEM)] + [pl.BlockSpec(memory_space=pltpu.VMEM)] * 2,
        out_specs=pl.BlockSpec(memory_space=pltpu.VMEM),
        name="assemble",
    )(core.reshape(1), near, far)


def per_device(
    tokens, norm_gain, w_query, w_keyvalue, cache, page_count, page_owner, keep_rows, dest_slot
):
    holders = lax.axis_size("page")
    groups = lax.axis_size("tensor")
    holder = lax.axis_index("page")
    half = lax.axis_index("tensor") % 2
    share = tokens.shape[0] // holders

    mine = lax.dynamic_slice_in_dim(tokens, holder * share, share, 0)
    widened = mine.astype(jnp.float32)
    normed = (
        widened
        * lax.rsqrt(jnp.mean(widened * widened, axis=-1, keepdims=True) + EPSILON)
        * norm_gain
    ).astype(jnp.bfloat16)
    across = lax.ppermute(normed, "tensor", OTHER_HALF)

    place = jnp.stack([holder // 2, holder % 2])
    compact, by_head = select_rows(place, page_count, page_owner, dest_slot, keep_rows, cache)
    near, got = [by_head[0]] + [None] * (CHIPS - 1), [compact[0]] + [None] * (CHIPS - 1)

    def send(after, heads, pages):
        blocks = [by_head[d] for d in heads] + [compact[d] for d in pages]
        blocks, after = lax.optimization_barrier((blocks, after))
        for d in heads:
            near[d] = lax.ppermute(blocks.pop(0), "page", OTHER_CHIP[d])
        for d in pages:
            got[d] = lax.ppermute(blocks.pop(0), "page", OTHER_CHIP[d])
        return after

    normed = send(normed, (4, 5, 6, 1), ())
    both = jnp.where(
        half == 0, jnp.stack([normed, across]), jnp.stack([across, normed])
    )
    rows = lax.all_to_all(
        jnp.broadcast_to(both[None], (PLANE,) + both.shape),
        "tensor",
        0,
        0,
        axis_index_groups=PLANE_GROUPS,
        tiled=True,
    ).reshape(groups * share, -1)
    rows = send(rows, (7, 2, 3), (4, 1))
    query_part = jnp.dot(rows, w_query, preferred_element_type=jnp.float32)
    pair_part = jnp.dot(rows, w_keyvalue, preferred_element_type=jnp.float32)
    projected = jnp.concatenate([query_part, pair_part], axis=1).astype(jnp.bfloat16)
    back = lax.all_to_all(
        projected.reshape(groups, share, -1), "tensor", 0, 0, tiled=True
    )
    back = send(back, (), (5, 2))
    query = back[:, :, :HEAD_DIM].reshape(CHIPS, 2, 2, share, HEAD_DIM)
    pair = back[:, :, HEAD_DIM:].reshape(2, CHIPS, 2, share, HEAD_DIM // 2)
    pair = jnp.transpose(pair, (1, 0, 3, 2, 4)).reshape(CHIPS, 1, 2, share, HEAD_DIM)
    pair = jnp.broadcast_to(pair, query.shape)
    outgoing = jnp.concatenate([query, pair], axis=-1).reshape(holders, 2, share, 2 * HEAD_DIM)
    own = lax.all_to_all(outgoing, "page", 0, 0, tiled=True)
    own = jnp.transpose(own, (1, 0, 2, 3)).reshape(2, holders * share, 2 * HEAD_DIM)

    far = lax.ppermute(jnp.stack(near), "page", OTHER_CORE)
    piece = attend(own, near, far)
    piece = send(piece, (), (6, 7, 3))
    near_out = lax.all_to_all(
        jnp.broadcast_to(piece[None], (CHIPS,) + piece.shape),
        "page",
        0,
        0,
        axis_index_groups=RUN_GROUPS,
        tiled=True,
    )
    far_out = lax.ppermute(near_out, "page", OTHER_CORE)
    attended = assemble(holder % 2, near_out, far_out)
    cross = lax.ppermute(jnp.stack([block[1] for block in got]), "page", OTHER_CORE)
    arrived = place_pages(place, got, cross)
    return attended, arrived[:, None]


def solution(mesh):
    return jax.shard_map(
        per_device,
        mesh=mesh,
        in_specs=(
            P("tensor", None),
            P(),
            P(None, "tensor"),
            P(None, "tensor"),
            P("page", "tensor", None, None),
            P("page", "tensor"),
            P("page", "tensor"),
            P("page", "tensor", None),
            P("page", "tensor"),
        ),
        out_specs=(P("tensor", None), P("page", "tensor", None, None)),
        check_vma=False,
    )
```

```python
import jax
import jax.numpy as jnp
from jax import lax
from jax.experimental import pallas as pl
from jax.experimental.pallas import tpu as pltpu
from jax.sharding import PartitionSpec as P

HEADS = 32
KV_HEADS = 8
REPEAT = HEADS // KV_HEADS
HEAD_DIM = 80
KEYS = KV_HEADS * HEAD_DIM
QUERIES = HEADS * HEAD_DIM
EPSILON = 1e-05
NEGATIVE = -1e30

PLANE = 16
HOLDERS = 16
SOURCES = 8
KEEP = 32
EXTRA = 256

PLANE_GROUPS = [[2 * i + half for i in range(PLANE)] for half in range(2)]
OTHER_HALF = [
    (p * 2 * PLANE + t, (p ^ 8) * 2 * PLANE + (t ^ 1)) for p in range(HOLDERS) for t in range(2 * PLANE)
]

VMEM = pl.BlockSpec(memory_space=pltpu.VMEM)
SMEM = pl.BlockSpec(memory_space=pltpu.SMEM)


def select_kernel(count_ref, dest_ref, keep_ref, page_ref, out_ref, kept_ref):
    slot = pl.program_id(0)

    @pl.when(slot == 0)
    def _():
        out_ref[...] = jnp.zeros_like(out_ref)

    rows = page_ref.shape[1]
    picks = jnp.broadcast_to(keep_ref[0], (rows, KEEP))
    chosen = (picks == lax.broadcasted_iota(jnp.int32, (rows, KEEP), 0)).astype(jnp.float32)
    kept = jnp.dot(
        chosen.T.astype(jnp.bfloat16), page_ref[0], preferred_element_type=jnp.float32
    ).astype(jnp.bfloat16)
    kept_ref[...] = kept

    @pl.when(slot < count_ref[0])
    def _():
        out_ref[dest_ref[slot]] = kept


def select_rows(page_count, dest_slot, keep_rows, cache):
    sources, _, rows, width = cache.shape
    return pl.pallas_call(
        select_kernel,
        out_shape=(
            jax.ShapeDtypeStruct((HOLDERS, KEEP, width), cache.dtype),
            jax.ShapeDtypeStruct((sources * KEEP, width), cache.dtype),
        ),
        grid_spec=pltpu.PrefetchScalarGridSpec(
            num_scalar_prefetch=2,
            grid=(sources,),
            in_specs=[
                pl.BlockSpec((1, 1, KEEP), lambda s, *_: (s, 0, 0)),
                pl.BlockSpec((1, rows, width), lambda s, *_: (s, 0, 0)),
            ],
            out_specs=[
                pl.BlockSpec((HOLDERS, KEEP, width), lambda s, *_: (0, 0, 0)),
                pl.BlockSpec((KEEP, width), lambda s, *_: (s, 0)),
            ],
        ),
        name="select_rows",
    )(page_count, dest_slot, keep_rows, cache.reshape(sources, rows, width))


def arrange_kernel(back_ref, out_ref):
    half = HEAD_DIM // 2
    for h in range(HEADS):
        at = (h % REPEAT * KV_HEADS + h // REPEAT) * HEAD_DIM
        out_ref[:, at : at + HEAD_DIM] = back_ref[h, :, :HEAD_DIM]
        at = QUERIES + h * half
        out_ref[:, at : at + half] = back_ref[h, :, HEAD_DIM:]


def arrange(back):
    return pl.pallas_call(
        arrange_kernel,
        out_shape=jax.ShapeDtypeStruct((back.shape[1], QUERIES + 2 * KEYS), back.dtype),
        in_specs=[VMEM],
        out_specs=VMEM,
        name="arrange",
    )(back)


def pieces(value, count):
    parts = []
    for _ in range(count):
        part = value.astype(jnp.bfloat16)
        parts.append(part)
        value = value - part.astype(jnp.float32)
    return parts


def attend_kernel(count_ref, owner_ref, kept_ref, rows_ref, out_ref, sum_ref, peak_ref, total_ref):
    scale = HEAD_DIM ** (-0.5)
    requests = rows_ref.shape[0]
    slot = lax.broadcasted_iota(jnp.int32, (SOURCES, requests), 0)
    owner = jnp.zeros((SOURCES, requests), jnp.int32)
    for s in range(SOURCES):
        owner = jnp.where(slot == s, owner_ref[s], owner)
    picked = (owner == lax.broadcasted_iota(jnp.int32, (SOURCES, requests), 1)).astype(jnp.float32)
    query = jnp.dot(
        picked.astype(jnp.bfloat16), rows_ref[:, :QUERIES], preferred_element_type=jnp.float32
    )
    head = lax.broadcasted_iota(jnp.int32, (KV_HEADS, KEYS), 0) * HEAD_DIM
    lane = lax.broadcasted_iota(jnp.int32, (KV_HEADS, KEYS), 1)
    mask = ((lane >= head) & (lane < head + HEAD_DIM)).astype(jnp.float32)
    for s in range(SOURCES):
        spread = jnp.concatenate(
            [query[s : s + 1, k * KEYS : (k + 1) * KEYS] * mask for k in range(REPEAT)], axis=0
        ).astype(jnp.bfloat16)
        keys = kept_ref[s * KEEP : (s + 1) * KEEP, :KEYS]
        values = kept_ref[s * KEEP : (s + 1) * KEEP, KEYS:]
        score = scale * lax.dot_general(
            keys, spread, (((1,), (1,)), ((), ())), preferred_element_type=jnp.float32
        )
        peak = jnp.max(score, axis=0, keepdims=True)
        weight = jnp.exp(score - peak)
        total_ref[s : s + 1, :] = jnp.sum(weight, axis=0, keepdims=True)
        peak_ref[s : s + 1, :] = jnp.where(s < count_ref[0], peak, NEGATIVE)
        mixed = lax.dot_general(
            weight.astype(jnp.bfloat16),
            values,
            (((0,), (0,)), ((), ())),
            preferred_element_type=jnp.float32,
        )
        for k in range(REPEAT):
            sum_ref[s : s + 1, k * KEYS : (k + 1) * KEYS] = jnp.sum(
                mixed[k * KV_HEADS : (k + 1) * KV_HEADS] * mask, axis=0, keepdims=True
            )
    out_ref[:, :QUERIES] = sum_ref[...].astype(jnp.bfloat16)
    slots = lax.broadcasted_iota(jnp.int32, (SOURCES, HEADS), 0)
    tag = jnp.full((SOURCES, HEADS), -1, jnp.int32)
    for s in range(SOURCES):
        tag = jnp.where((slots == s) & (s < count_ref[0]), owner_ref[s], tag)
    tag = tag.astype(jnp.float32).astype(jnp.bfloat16)
    columns = pieces(peak_ref[...], 3) + pieces(total_ref[...], 3) + [tag, tag]
    columns = [column.astype(jnp.float32) for column in columns]
    out_ref[:, QUERIES:] = jnp.concatenate(columns, axis=1).astype(jnp.bfloat16)


def attend(page_count, page_owner, kept, rows):
    return pl.pallas_call(
        attend_kernel,
        out_shape=jax.ShapeDtypeStruct((SOURCES, QUERIES + EXTRA), jnp.bfloat16),
        in_specs=[SMEM, SMEM, VMEM, VMEM],
        out_specs=VMEM,
        scratch_shapes=[
            pltpu.VMEM((SOURCES, QUERIES), jnp.float32),
            pltpu.VMEM((SOURCES, HEADS), jnp.float32),
            pltpu.VMEM((SOURCES, HEADS), jnp.float32),
        ],
        name="attend",
    )(page_count, page_owner, kept, rows)


def spread_dot(value, chosen, contract, count, chosen_first=False):
    total = None
    for part in pieces(value, count):
        operands = (chosen, part) if chosen_first else (part, chosen)
        term = lax.dot_general(
            *operands, (contract, ((), ())), preferred_element_type=jnp.float32
        )
        total = term if total is None else total + term
    return total


def combine_kernel(part_ref, rows_ref, out_ref):
    scale = HEAD_DIM ** (-0.5)
    requests = rows_ref.shape[0]
    slots = part_ref.shape[0]
    extra = part_ref[:, QUERIES:].astype(jnp.float32)
    column = [extra[:, i * HEADS : (i + 1) * HEADS] for i in range(7)]
    peaks = column[0] + column[1] + column[2]
    totals = column[3] + column[4] + column[5]
    tag = column[6][:, :1]
    row = lax.broadcasted_iota(jnp.int32, (requests, 1), 0).astype(jnp.float32)
    member = (
        tag == lax.broadcasted_iota(jnp.int32, (slots, requests), 1).astype(jnp.float32)
    ).astype(jnp.float32).astype(jnp.bfloat16)
    head = lax.broadcasted_iota(jnp.int32, (HEADS, QUERIES), 0) * HEAD_DIM
    lane = lax.broadcasted_iota(jnp.int32, (HEADS, QUERIES), 1)
    expand = ((lane >= head) & (lane < head + HEAD_DIM)).astype(jnp.float32).astype(jnp.bfloat16)

    query = rows_ref[:, :QUERIES].astype(jnp.float32)
    key = rows_ref[:, QUERIES : QUERIES + KEYS].astype(jnp.float32)
    value = rows_ref[:, QUERIES + KEYS :].astype(jnp.float32)
    product = query * jnp.concatenate([key] * REPEAT, axis=1)
    own = scale * spread_dot(product, expand, ((1,), (1,)), 3)
    top = own
    for s in range(slots):
        top = jnp.maximum(
            top, jnp.where(tag[s : s + 1] == row, peaks[s : s + 1], NEGATIVE)
        )
    own_weight = jnp.exp(own - top)
    weight = jnp.exp(peaks - spread_dot(top, member, ((1,), (0,)), 3, True))
    total = spread_dot(weight * totals, member, ((0,), (0,)), 3, True) + own_weight
    inverse = 1.0 / total
    weight = weight * spread_dot(inverse, member, ((1,), (0,)), 3, True)
    scaled = part_ref[:, :QUERIES].astype(jnp.float32) * spread_dot(
        weight, expand, ((1,), (0,)), 2
    )
    mixed = spread_dot(scaled, member, ((0,), (0,)), 2, True)
    own_share = spread_dot(own_weight * inverse, expand, ((1,), (0,)), 2)
    mixed = (mixed + own_share * jnp.concatenate([value] * REPEAT, axis=1)).astype(jnp.bfloat16)
    for h in range(HEADS):
        at = (h % REPEAT * KV_HEADS + h // REPEAT) * HEAD_DIM
        out_ref[:, h * HEAD_DIM : (h + 1) * HEAD_DIM] = mixed[:, at : at + HEAD_DIM]


def combine(parts, rows):
    return pl.pallas_call(
        combine_kernel,
        out_shape=jax.ShapeDtypeStruct((rows.shape[0], QUERIES), jnp.bfloat16),
        in_specs=[VMEM] * 2,
        out_specs=VMEM,
        compiler_params=pltpu.CompilerParams(vmem_limit_bytes=48 * 1024 * 1024),
        name="combine",
    )(parts, rows)


def per_device(
    tokens, norm_gain, w_query, w_keyvalue, cache, page_count, page_owner, keep_rows, dest_slot
):
    groups = lax.axis_size("tensor")
    holder = lax.axis_index("page")
    half = lax.axis_index("tensor") % 2
    share = tokens.shape[0] // HOLDERS

    def normalise(rows):
        widened = rows.astype(jnp.float32)
        return (
            widened
            * lax.rsqrt(jnp.mean(widened * widened, axis=-1, keepdims=True) + EPSILON)
            * norm_gain
        ).astype(jnp.bfloat16)

    theirs = lax.dynamic_slice_in_dim(tokens, (holder ^ 8) * share, share, 0)
    across = lax.ppermute(normalise(theirs), ("page", "tensor"), OTHER_HALF)
    mine = normalise(lax.dynamic_slice_in_dim(tokens, holder * share, share, 0))

    page_count = page_count.reshape(1)
    page_owner = page_owner.reshape(SOURCES)
    compact, kept = select_rows(page_count, dest_slot.reshape(SOURCES), keep_rows, cache)

    both = jnp.where(half == 0, jnp.stack([mine, across]), jnp.stack([across, mine]))
    rows = lax.all_to_all(
        jnp.broadcast_to(both[None], (PLANE,) + both.shape),
        "tensor",
        0,
        0,
        axis_index_groups=PLANE_GROUPS,
        tiled=True,
    ).reshape(groups * share, -1)
    query_part = jnp.dot(rows, w_query, preferred_element_type=jnp.float32)
    pair_part = jnp.dot(rows, w_keyvalue, preferred_element_type=jnp.float32)
    projected = jnp.concatenate([query_part, pair_part], axis=1).astype(jnp.bfloat16)
    back = lax.all_to_all(
        projected.reshape(groups, share, -1), "tensor", 0, 0, tiled=True
    )
    back, compact = lax.optimization_barrier((back, compact))
    arrived = lax.all_to_all(compact, "page", 0, 0, tiled=True)
    own_rows = lax.all_gather(arrange(back), "page", axis=0, tiled=True)
    part = attend(page_count, page_owner, kept, own_rows)
    parts = lax.all_gather(part, "page", axis=0, tiled=True)
    return combine(parts, own_rows), arrived[:, None]


def solution(mesh):
    return jax.shard_map(
        per_device,
        mesh=mesh,
        in_specs=(
            P("tensor", None),
            P(),
            P(None, "tensor"),
            P(None, "tensor"),
            P("page", "tensor", None, None),
            P("page", "tensor"),
            P("page", "tensor"),
            P("page", "tensor", None),
            P("page", "tensor"),
        ),
        out_specs=(P("tensor", None), P("page", "tensor", None, None)),
        check_vma=False,
    )
```

```python
import jax
import jax.numpy as jnp
from jax import lax
from jax.experimental import pallas as pl
from jax.experimental.pallas import tpu as pltpu
from jax.sharding import PartitionSpec as P

HEADS = 32
KV_HEADS = 8
REPEAT = HEADS // KV_HEADS
HEAD_DIM = 80
KEYS = KV_HEADS * HEAD_DIM
QUERIES = HEADS * HEAD_DIM
EPSILON = 1e-05
NEGATIVE = -1e30

PLANE = 16
HOLDERS = 16
SOURCES = 8
KEEP = 32
EXTRA = 256

CHIPS = 8
PLANE_GROUPS = [[2 * i + half for i in range(PLANE)] for half in range(2)]
OTHER_HALF = [
    (p * 2 * PLANE + t, (p ^ 8) * 2 * PLANE + (t ^ 1)) for p in range(HOLDERS) for t in range(2 * PLANE)
]

RUN_GROUPS = [[2 * z + core for z in range(CHIPS)] for core in range(2)]
OTHER_CORE = [(i, i ^ 1) for i in range(HOLDERS)]
STEP = 4

VMEM = pl.BlockSpec(memory_space=pltpu.VMEM)
SMEM = pl.BlockSpec(memory_space=pltpu.SMEM)


def select_kernel(count_ref, dest_ref, keep_ref, page_ref, out_ref, kept_ref):
    step = pl.program_id(0)

    @pl.when(step == 0)
    def _():
        out_ref[...] = jnp.zeros_like(out_ref)

    rows = page_ref.shape[1]
    for i in range(STEP):
        slot = step * STEP + i
        picks = jnp.broadcast_to(keep_ref[i], (rows, KEEP))
        chosen = (picks == lax.broadcasted_iota(jnp.int32, (rows, KEEP), 0)).astype(jnp.float32)
        kept = jnp.dot(
            chosen.T.astype(jnp.bfloat16), page_ref[i], preferred_element_type=jnp.float32
        ).astype(jnp.bfloat16)
        kept_ref[i * KEEP : (i + 1) * KEEP] = kept

        @pl.when(slot < count_ref[0])
        def _():
            out_ref[dest_ref[slot]] = kept


def select_rows(page_count, dest_slot, keep_rows, cache):
    sources, _, rows, width = cache.shape
    return pl.pallas_call(
        select_kernel,
        out_shape=(
            jax.ShapeDtypeStruct((HOLDERS, KEEP, width), cache.dtype),
            jax.ShapeDtypeStruct((sources * KEEP, width), cache.dtype),
        ),
        grid_spec=pltpu.PrefetchScalarGridSpec(
            num_scalar_prefetch=2,
            grid=(sources // STEP,),
            in_specs=[
                pl.BlockSpec((STEP, 1, KEEP), lambda s, *_: (s, 0, 0)),
                pl.BlockSpec((STEP, rows, width), lambda s, *_: (s, 0, 0)),
            ],
            out_specs=[
                pl.BlockSpec((HOLDERS, KEEP, width), lambda s, *_: (0, 0, 0)),
                pl.BlockSpec((STEP * KEEP, width), lambda s, *_: (s, 0)),
            ],
        ),
        name="select_rows",
    )(page_count, dest_slot, keep_rows, cache.reshape(sources, rows, width))


def project_kernel(rows_ref, query_ref, pair_ref, out_ref):
    rows = rows_ref[...]
    for ref, low, high in ((query_ref, 0, HEAD_DIM), (pair_ref, HEAD_DIM, HEAD_DIM * 3 // 2)):
        out_ref[:, low:high] = lax.dot_general(
            rows, ref[...], (((1,), (1,)), ((), ())), preferred_element_type=jnp.float32
        ).astype(jnp.bfloat16)


def project(rows, w_query, w_keyvalue):
    return pl.pallas_call(
        project_kernel,
        out_shape=jax.ShapeDtypeStruct((rows.shape[0], HEAD_DIM * 3 // 2), jnp.bfloat16),
        in_specs=[VMEM] * 3,
        out_specs=VMEM,
        name="project",
    )(rows, w_query.T, w_keyvalue.T)


def pick_kernel(place_ref, all_ref, own_ref, other_ref):
    block = all_ref[...].astype(jnp.float32)
    share = own_ref.shape[1]
    low, high = block[:, :share], block[:, share:]
    first = place_ref[1] == 0
    own_ref[...] = jnp.where(first, low, high).astype(jnp.bfloat16)
    other_ref[...] = jnp.where(first, high, low).astype(jnp.bfloat16)


def pick(place, everyone):
    count, rows, width = everyone.shape
    both = rows // PLANE
    piece = jax.ShapeDtypeStruct((count, both // 2, width), everyone.dtype)
    whole = pl.BlockSpec(piece.shape, lambda i, *_: (0, 0, 0))
    return pl.pallas_call(
        pick_kernel,
        out_shape=(piece, piece),
        grid_spec=pltpu.PrefetchScalarGridSpec(
            num_scalar_prefetch=1,
            grid=(1,),
            in_specs=[pl.BlockSpec((count, both, width), lambda i, place: (0, place[0], 0))],
            out_specs=[whole, whole],
        ),
        name="pick",
    )(place, everyone)


def arrange_kernel(place_ref, own_ref, got_ref, out_ref):
    half = HEAD_DIM // 2
    for h in range(HEADS):
        block = jnp.where(
            place_ref[1] == h % 2,
            own_ref[h // 2].astype(jnp.float32),
            got_ref[h // 2].astype(jnp.float32),
        ).astype(jnp.bfloat16)
        at = (h % REPEAT * KV_HEADS + h // REPEAT) * HEAD_DIM
        out_ref[:, at : at + HEAD_DIM] = block[:, :HEAD_DIM]
        at = QUERIES + h * half
        out_ref[:, at : at + half] = block[:, HEAD_DIM:]


def arrange(place, own, got):
    return pl.pallas_call(
        arrange_kernel,
        out_shape=jax.ShapeDtypeStruct((own.shape[1], QUERIES + 2 * KEYS), own.dtype),
        in_specs=[SMEM, VMEM, VMEM],
        out_specs=VMEM,
        name="arrange",
    )(place, own, got)


def pieces(value, count):
    parts = []
    for _ in range(count):
        part = value.astype(jnp.bfloat16)
        parts.append(part)
        value = value - part.astype(jnp.float32)
    return parts


def from_runs(request, core, near, far):
    count = near.shape[0]
    per_holder = count // CHIPS
    holder = request // per_holder
    place = holder // 2 * per_holder + request % per_holder
    spot = lax.broadcasted_iota(jnp.int32, (request.shape[0], count), 1)
    total = None
    for rows, same in ((near, True), (far, False)):
        chosen = (spot == place) & ((holder % 2 == core) == same)
        term = jnp.dot(
            chosen.astype(jnp.float32).astype(jnp.bfloat16), rows, preferred_element_type=jnp.float32
        )
        total = term if total is None else total + term
    return total


def attend_kernel(
    place_ref, count_ref, owner_ref, kept_ref, near_ref, far_ref, out_ref, sum_ref, peak_ref, total_ref
):
    scale = HEAD_DIM ** (-0.5)
    slot = lax.broadcasted_iota(jnp.int32, (SOURCES, near_ref.shape[0]), 0)
    owner = jnp.zeros(slot.shape, jnp.int32)
    for s in range(SOURCES):
        owner = jnp.where(slot == s, owner_ref[s], owner)
    query = from_runs(owner, place_ref[2], near_ref[:, :QUERIES], far_ref[:, :QUERIES])
    head = lax.broadcasted_iota(jnp.int32, (KV_HEADS, KEYS), 0) * HEAD_DIM
    lane = lax.broadcasted_iota(jnp.int32, (KV_HEADS, KEYS), 1)
    mask = ((lane >= head) & (lane < head + HEAD_DIM)).astype(jnp.float32)
    for s in range(SOURCES):
        spread = jnp.concatenate(
            [query[s : s + 1, k * KEYS : (k + 1) * KEYS] * mask for k in range(REPEAT)], axis=0
        ).astype(jnp.bfloat16)
        keys = kept_ref[s * KEEP : (s + 1) * KEEP, :KEYS]
        values = kept_ref[s * KEEP : (s + 1) * KEEP, KEYS:]
        score = scale * lax.dot_general(
            keys, spread, (((1,), (1,)), ((), ())), preferred_element_type=jnp.float32
        )
        peak = jnp.max(score, axis=0, keepdims=True)
        weight = jnp.exp(score - peak)
        total_ref[s : s + 1, :] = jnp.sum(weight, axis=0, keepdims=True)
        peak_ref[s : s + 1, :] = jnp.where(s < count_ref[0], peak, NEGATIVE)
        mixed = lax.dot_general(
            weight.astype(jnp.bfloat16),
            values,
            (((0,), (0,)), ((), ())),
            preferred_element_type=jnp.float32,
        )
        for k in range(REPEAT):
            sum_ref[s : s + 1, k * KEYS : (k + 1) * KEYS] = jnp.sum(
                mixed[k * KV_HEADS : (k + 1) * KV_HEADS] * mask, axis=0, keepdims=True
            )
    out_ref[:, :QUERIES] = sum_ref[...].astype(jnp.bfloat16)
    slots = lax.broadcasted_iota(jnp.int32, (SOURCES, HEADS), 0)
    tag = jnp.full((SOURCES, HEADS), -1, jnp.int32)
    for s in range(SOURCES):
        tag = jnp.where((slots == s) & (s < count_ref[0]), owner_ref[s], tag)
    tag = tag.astype(jnp.float32).astype(jnp.bfloat16)
    columns = pieces(peak_ref[...], 3) + pieces(total_ref[...], 3) + [tag, tag]
    columns = [column.astype(jnp.float32) for column in columns]
    out_ref[:, QUERIES:] = jnp.concatenate(columns, axis=1).astype(jnp.bfloat16)


def attend(place, page_count, page_owner, kept, near, far):
    return pl.pallas_call(
        attend_kernel,
        out_shape=jax.ShapeDtypeStruct((SOURCES, QUERIES + EXTRA), jnp.bfloat16),
        in_specs=[SMEM] * 3 + [VMEM] * 3,
        out_specs=VMEM,
        scratch_shapes=[
            pltpu.VMEM((SOURCES, QUERIES), jnp.float32),
            pltpu.VMEM((SOURCES, HEADS), jnp.float32),
            pltpu.VMEM((SOURCES, HEADS), jnp.float32),
        ],
        name="attend",
    )(place, page_count, page_owner, kept, near, far)


def spread_dot(value, chosen, contract, count, chosen_first=False):
    total = None
    for part in pieces(value, count):
        operands = (chosen, part) if chosen_first else (part, chosen)
        term = lax.dot_general(
            *operands, (contract, ((), ())), preferred_element_type=jnp.float32
        )
        total = term if total is None else total + term
    return total


def combine_kernel(place_ref, near_part_ref, far_part_ref, near_ref, far_ref, out_ref):
    scale = HEAD_DIM ** (-0.5)
    requests = out_ref.shape[0]
    part = jnp.concatenate(
        [near_part_ref[...].astype(jnp.float32), far_part_ref[...].astype(jnp.float32)], axis=0
    )
    slots = part.shape[0]
    extra = part[:, QUERIES:]
    column = [extra[:, i * HEADS : (i + 1) * HEADS] for i in range(7)]
    peaks = column[0] + column[1] + column[2]
    totals = column[3] + column[4] + column[5]
    tag = column[6][:, :1]
    row = lax.broadcasted_iota(jnp.int32, (requests, 1), 0).astype(jnp.float32)
    member = (
        tag == lax.broadcasted_iota(jnp.int32, (slots, requests), 1).astype(jnp.float32)
    ).astype(jnp.float32).astype(jnp.bfloat16)
    head = lax.broadcasted_iota(jnp.int32, (HEADS, QUERIES), 0) * HEAD_DIM
    lane = lax.broadcasted_iota(jnp.int32, (HEADS, QUERIES), 1)
    expand = ((lane >= head) & (lane < head + HEAD_DIM)).astype(jnp.float32).astype(jnp.bfloat16)

    number = lax.broadcasted_iota(jnp.int32, (requests, near_ref.shape[0]), 0)
    rows = from_runs(number, place_ref[2], near_ref[...], far_ref[...])
    query = rows[:, :QUERIES]
    key = rows[:, QUERIES : QUERIES + KEYS]
    value = rows[:, QUERIES + KEYS :]
    product = query * jnp.concatenate([key] * REPEAT, axis=1)
    own = scale * spread_dot(product, expand, ((1,), (1,)), 3)
    top = own
    for s in range(slots):
        top = jnp.maximum(
            top, jnp.where(tag[s : s + 1] == row, peaks[s : s + 1], NEGATIVE)
        )
    own_weight = jnp.exp(own - top)
    weight = jnp.exp(peaks - spread_dot(top, member, ((1,), (0,)), 3, True))
    total = spread_dot(weight * totals, member, ((0,), (0,)), 3, True) + own_weight
    inverse = 1.0 / total
    weight = weight * spread_dot(inverse, member, ((1,), (0,)), 3, True)
    scaled = part[:, :QUERIES] * spread_dot(
        weight, expand, ((1,), (0,)), 2
    )
    mixed = spread_dot(scaled, member, ((0,), (0,)), 2, True)
    own_share = spread_dot(own_weight * inverse, expand, ((1,), (0,)), 2)
    mixed = (mixed + own_share * jnp.concatenate([value] * REPEAT, axis=1)).astype(jnp.bfloat16)
    for h in range(HEADS):
        at = (h % REPEAT * KV_HEADS + h // REPEAT) * HEAD_DIM
        out_ref[:, h * HEAD_DIM : (h + 1) * HEAD_DIM] = mixed[:, at : at + HEAD_DIM]


def combine(place, near_part, far_part, near, far):
    return pl.pallas_call(
        combine_kernel,
        out_shape=jax.ShapeDtypeStruct((2 * near.shape[0], QUERIES), jnp.bfloat16),
        in_specs=[SMEM] + [VMEM] * 4,
        out_specs=VMEM,
        compiler_params=pltpu.CompilerParams(vmem_limit_bytes=48 * 1024 * 1024),
        name="combine",
    )(place, near_part, far_part, near, far)


def to_all_holders(block):
    near = lax.all_to_all(
        jnp.broadcast_to(block[None], (CHIPS,) + block.shape),
        "page",
        0,
        0,
        axis_index_groups=RUN_GROUPS,
        tiled=True,
    )
    far = lax.ppermute(near, "page", OTHER_CORE)
    shape = (CHIPS * block.shape[0], block.shape[1])
    return near.reshape(shape), far.reshape(shape)


def per_device(
    tokens, norm_gain, w_query, w_keyvalue, cache, page_count, page_owner, keep_rows, dest_slot
):
    holder = lax.axis_index("page")
    group = lax.axis_index("tensor")
    half = group % 2
    place = jnp.stack([group // 2, half, holder % 2])
    share = tokens.shape[0] // HOLDERS

    def normalise(rows):
        widened = rows.astype(jnp.float32)
        return (
            widened
            * lax.rsqrt(jnp.mean(widened * widened, axis=-1, keepdims=True) + EPSILON)
            * norm_gain
        ).astype(jnp.bfloat16)

    page_count = page_count.reshape(1)
    page_owner = page_owner.reshape(SOURCES)
    compact, kept = select_rows(page_count, dest_slot.reshape(SOURCES), keep_rows, cache)

    mine = normalise(lax.dynamic_slice_in_dim(tokens, holder * share, share, 0))
    mine, compact = lax.optimization_barrier((mine, compact))
    across = lax.ppermute(mine, ("page", "tensor"), OTHER_HALF)
    arrived = lax.all_to_all(compact, "page", 0, 0, tiled=True)

    both = jnp.where(
        half == 0,
        jnp.concatenate([mine, across], axis=0),
        jnp.concatenate([across, mine], axis=0),
    )
    rows = lax.all_gather(
        both, "tensor", axis=0, axis_index_groups=PLANE_GROUPS, tiled=True
    )
    projected = project(rows, w_query, w_keyvalue)
    everyone = lax.all_gather(
        projected, "tensor", axis=0, axis_index_groups=PLANE_GROUPS, tiled=False
    )
    own, other = pick(place, everyone)
    got = lax.ppermute(other, ("page", "tensor"), OTHER_HALF)
    ordered, arrived = lax.optimization_barrier((arrange(place, own, got), arrived))
    near, far = to_all_holders(ordered)
    part = attend(place, page_count, page_owner, kept, near, far)
    near_part, far_part = to_all_holders(part)
    attended = combine(place, near_part, far_part, near, far)
    return attended, arrived[:, None]


def solution(mesh):
    return jax.shard_map(
        per_device,
        mesh=mesh,
        in_specs=(
            P("tensor", None),
            P(),
            P(None, "tensor"),
            P(None, "tensor"),
            P("page", "tensor", None, None),
            P("page", "tensor"),
            P("page", "tensor"),
            P("page", "tensor", None),
            P("page", "tensor"),
        ),
        out_specs=(P("tensor", None), P("page", "tensor", None, None)),
        check_vma=False,
    )
```

```python
import jax
import jax.numpy as jnp
from jax import lax
from jax.experimental import pallas as pl
from jax.experimental.pallas import tpu as pltpu
from jax.sharding import PartitionSpec as P

HEADS = 32
KV_HEADS = 8
REPEAT = HEADS // KV_HEADS
HEAD_DIM = 80
KEYS = KV_HEADS * HEAD_DIM
QUERIES = HEADS * HEAD_DIM
EPSILON = 1e-05
NEGATIVE = -1e30

PLANE = 16
HOLDERS = 16
SOURCES = 8
KEEP = 32
EXTRA = 256

CHIPS = 8
PLANE_GROUPS = [[2 * i + half for i in range(PLANE)] for half in range(2)]
OTHER_HALF = [
    (p * 2 * PLANE + t, (p ^ 8) * 2 * PLANE + (t ^ 1)) for p in range(HOLDERS) for t in range(2 * PLANE)
]

COLUMN_GROUPS = [
    [(2 * z + core) * 2 * PLANE + 2 * xy + half for half in range(2) for z in range(CHIPS)]
    for xy in range(PLANE)
    for core in range(2)
]
HALF_COLUMNS = (QUERIES + 2 * KEYS) // 2
RUN_GROUPS = [[2 * z + core for z in range(CHIPS)] for core in range(2)]
OTHER_CORE = [(i, i ^ 1) for i in range(HOLDERS)]
STEP = 4

VMEM = pl.BlockSpec(memory_space=pltpu.VMEM)
SMEM = pl.BlockSpec(memory_space=pltpu.SMEM)


def select_kernel(count_ref, dest_ref, keep_ref, page_ref, out_ref, kept_ref):
    step = pl.program_id(0)

    @pl.when(step == 0)
    def _():
        out_ref[...] = jnp.zeros_like(out_ref)

    rows = page_ref.shape[1]
    for i in range(STEP):
        slot = step * STEP + i
        picks = jnp.broadcast_to(keep_ref[i], (rows, KEEP))
        chosen = (picks == lax.broadcasted_iota(jnp.int32, (rows, KEEP), 0)).astype(jnp.float32)
        kept = jnp.dot(
            chosen.T.astype(jnp.bfloat16), page_ref[i], preferred_element_type=jnp.float32
        ).astype(jnp.bfloat16)
        kept_ref[i * KEEP : (i + 1) * KEEP] = kept

        @pl.when(slot < count_ref[0])
        def _():
            out_ref[dest_ref[slot]] = kept


def select_rows(page_count, dest_slot, keep_rows, cache):
    sources, _, rows, width = cache.shape
    return pl.pallas_call(
        select_kernel,
        out_shape=(
            jax.ShapeDtypeStruct((HOLDERS, KEEP, width), cache.dtype),
            jax.ShapeDtypeStruct((sources * KEEP, width), cache.dtype),
        ),
        grid_spec=pltpu.PrefetchScalarGridSpec(
            num_scalar_prefetch=2,
            grid=(sources // STEP,),
            in_specs=[
                pl.BlockSpec((STEP, 1, KEEP), lambda s, *_: (s, 0, 0)),
                pl.BlockSpec((STEP, rows, width), lambda s, *_: (s, 0, 0)),
            ],
            out_specs=[
                pl.BlockSpec((HOLDERS, KEEP, width), lambda s, *_: (0, 0, 0)),
                pl.BlockSpec((STEP * KEEP, width), lambda s, *_: (s, 0)),
            ],
        ),
        name="select_rows",
    )(page_count, dest_slot, keep_rows, cache.reshape(sources, rows, width))


def project_kernel(rows_ref, query_ref, pair_ref, out_ref):
    rows = rows_ref[...]
    for ref, low, high in ((query_ref, 0, HEAD_DIM), (pair_ref, HEAD_DIM, HEAD_DIM * 3 // 2)):
        out_ref[:, low:high] = lax.dot_general(
            rows, ref[...], (((1,), (1,)), ((), ())), preferred_element_type=jnp.float32
        ).astype(jnp.bfloat16)


def project(rows, w_query, w_keyvalue):
    return pl.pallas_call(
        project_kernel,
        out_shape=jax.ShapeDtypeStruct((rows.shape[0], HEAD_DIM * 3 // 2), jnp.bfloat16),
        in_specs=[VMEM] * 3,
        out_specs=VMEM,
        name="project",
    )(rows, w_query.T, w_keyvalue.T)


def pick_kernel(place_ref, all_ref, out_ref, rows_ref):
    half = HEAD_DIM // 2
    for i in range(PLANE):
        block = all_ref[i].astype(jnp.float32)
        at = (i % 2 * KV_HEADS + i // 2) * HEAD_DIM
        rows_ref[:, at : at + HEAD_DIM] = block[:, :HEAD_DIM]
        at = QUERIES // 2 + i * half
        rows_ref[:, at : at + half] = block[:, HEAD_DIM:]
    share = out_ref.shape[1]
    for h in range(2):
        piece = rows_ref[h * share : (h + 1) * share].astype(jnp.bfloat16)
        for z in range(CHIPS):
            out_ref[h * CHIPS + z] = piece


def pick(place, everyone):
    count, rows, width = everyone.shape
    both = rows // PLANE
    piece = jax.ShapeDtypeStruct((2 * CHIPS, both // 2, HALF_COLUMNS), everyone.dtype)
    return pl.pallas_call(
        pick_kernel,
        out_shape=piece,
        grid_spec=pltpu.PrefetchScalarGridSpec(
            num_scalar_prefetch=1,
            grid=(1,),
            in_specs=[pl.BlockSpec((count, both, width), lambda i, place: (0, place[0], 0))],
            out_specs=pl.BlockSpec(piece.shape, lambda i, *_: (0, 0, 0)),
            scratch_shapes=[pltpu.VMEM((both, HALF_COLUMNS), jnp.float32)],
        ),
        name="pick",
    )(place, everyone)


def held(place_ref, near_ref, far_ref, chip, core, half, columns):
    spot = half * CHIPS + jnp.where(place_ref[1] == half, chip, chip ^ 4)
    near = near_ref[spot, :, columns].astype(jnp.float32)
    far = far_ref[spot, :, columns].astype(jnp.float32)
    return jnp.where(place_ref[2] == core, near, far)


def pieces(value, count):
    parts = []
    for _ in range(count):
        part = value.astype(jnp.bfloat16)
        parts.append(part)
        value = value - part.astype(jnp.float32)
    return parts


def attend_kernel(
    place_ref, count_ref, owner_ref, kept_ref, near_ref, far_ref, out_ref, sum_ref, peak_ref, total_ref
):
    scale = HEAD_DIM ** (-0.5)
    share = near_ref.shape[1]
    line = lax.broadcasted_iota(jnp.int32, (share, QUERIES // 2), 0)
    head = lax.broadcasted_iota(jnp.int32, (KV_HEADS, KEYS), 0) * HEAD_DIM
    lane = lax.broadcasted_iota(jnp.int32, (KV_HEADS, KEYS), 1)
    mask = ((lane >= head) & (lane < head + HEAD_DIM)).astype(jnp.float32)
    for s in range(SOURCES):
        request = owner_ref[s]
        holder = request // share
        query = []
        for half in range(2):
            block = held(
                place_ref, near_ref, far_ref, holder // 2, holder % 2, half, pl.ds(0, QUERIES // 2)
            )
            query.append(
                jnp.sum(jnp.where(line == request % share, block, 0.0), axis=0, keepdims=True)
            )
        spread = jnp.concatenate(
            [
                query[k % 2][:, k // 2 * KEYS : (k // 2 + 1) * KEYS] * mask
                for k in range(REPEAT)
            ],
            axis=0,
        ).astype(jnp.bfloat16)
        keys = kept_ref[s * KEEP : (s + 1) * KEEP, :KEYS]
        values = kept_ref[s * KEEP : (s + 1) * KEEP, KEYS:]
        score = scale * lax.dot_general(
            keys, spread, (((1,), (1,)), ((), ())), preferred_element_type=jnp.float32
        )
        peak = jnp.max(score, axis=0, keepdims=True)
        weight = jnp.exp(score - peak)
        total_ref[s : s + 1, :] = jnp.sum(weight, axis=0, keepdims=True)
        peak_ref[s : s + 1, :] = jnp.where(s < count_ref[0], peak, NEGATIVE)
        mixed = lax.dot_general(
            weight.astype(jnp.bfloat16),
            values,
            (((0,), (0,)), ((), ())),
            preferred_element_type=jnp.float32,
        )
        for k in range(REPEAT):
            sum_ref[s : s + 1, k * KEYS : (k + 1) * KEYS] = jnp.sum(
                mixed[k * KV_HEADS : (k + 1) * KV_HEADS] * mask, axis=0, keepdims=True
            )
    sums = sum_ref[...].astype(jnp.bfloat16)
    slots = lax.broadcasted_iota(jnp.int32, (SOURCES, HEADS), 0)
    tag = jnp.full((SOURCES, HEADS), -1, jnp.int32)
    for s in range(SOURCES):
        tag = jnp.where((slots == s) & (s < count_ref[0]), owner_ref[s], tag)
    tag = tag.astype(jnp.float32).astype(jnp.bfloat16)
    columns = pieces(peak_ref[...], 3) + pieces(total_ref[...], 3) + [tag, tag]
    columns = [column.astype(jnp.float32) for column in columns]
    columns = jnp.concatenate(columns, axis=1).astype(jnp.bfloat16)
    for z in range(CHIPS):
        out_ref[z, :, :QUERIES] = sums
        out_ref[z, :, QUERIES:] = columns


def attend(place, page_count, page_owner, kept, near, far):
    return pl.pallas_call(
        attend_kernel,
        out_shape=jax.ShapeDtypeStruct((CHIPS, SOURCES, QUERIES + EXTRA), jnp.bfloat16),
        in_specs=[SMEM] * 3 + [VMEM] * 3,
        out_specs=VMEM,
        scratch_shapes=[
            pltpu.VMEM((SOURCES, QUERIES), jnp.float32),
            pltpu.VMEM((SOURCES, HEADS), jnp.float32),
            pltpu.VMEM((SOURCES, HEADS), jnp.float32),
        ],
        name="attend",
    )(place, page_count, page_owner, kept, near, far)


def spread_dot(value, chosen, contract, count, chosen_first=False):
    total = None
    for part in pieces(value, count):
        operands = (chosen, part) if chosen_first else (part, chosen)
        term = lax.dot_general(
            *operands, (contract, ((), ())), preferred_element_type=jnp.float32
        )
        total = term if total is None else total + term
    return total


def head_columns():
    head = lax.broadcasted_iota(jnp.int32, (HEADS, QUERIES), 0) * HEAD_DIM
    lane = lax.broadcasted_iota(jnp.int32, (HEADS, QUERIES), 1)
    return ((lane >= head) & (lane < head + HEAD_DIM)).astype(jnp.float32).astype(jnp.bfloat16)


def own_kernel(place_ref, near_ref, far_ref, score_ref, value_ref, query_ref, pair_ref):
    scale = HEAD_DIM ** (-0.5)
    share = near_ref.shape[1]
    piece = HEAD_DIM // 2
    for holder in range(HOLDERS):
        rows = slice(holder * share, (holder + 1) * share)
        for half in range(2):
            block = held(
                place_ref, near_ref, far_ref, holder // 2, holder % 2, half, pl.ds(0, HALF_COLUMNS)
            )
            for k in range(2):
                at = (2 * k + half) * KEYS
                query_ref[rows, at : at + KEYS] = block[:, k * KEYS : (k + 1) * KEYS]
            pair_ref[half, rows, :] = block[:, QUERIES // 2 :]
    keys, values = [], []
    for g in range(KV_HEADS):
        for half in range(2):
            keys.append(pair_ref[half, :, g * piece : (g + 1) * piece])
            at = KEYS // 2 + g * piece
            values.append(pair_ref[half, :, at : at + piece])
    key = jnp.concatenate(keys, axis=1)
    value_ref[...] = jnp.concatenate(values, axis=1)
    product = query_ref[...] * jnp.concatenate([key] * REPEAT, axis=1)
    score_ref[...] = scale * spread_dot(product, head_columns(), ((1,), (1,)), 3)


def own_part(place, near, far):
    requests = HOLDERS * near.shape[1]
    return pl.pallas_call(
        own_kernel,
        out_shape=(
            jax.ShapeDtypeStruct((requests, HEADS), jnp.float32),
            jax.ShapeDtypeStruct((requests, KEYS), jnp.float32),
        ),
        in_specs=[SMEM, VMEM, VMEM],
        out_specs=(VMEM, VMEM),
        scratch_shapes=[
            pltpu.VMEM((requests, QUERIES), jnp.float32),
            pltpu.VMEM((2, requests, KEYS), jnp.float32),
        ],
        name="own_part",
    )(place, near, far)


def combine_kernel(near_ref, far_ref, own_ref, value_ref, out_ref):
    requests = out_ref.shape[0]
    part = jnp.concatenate(
        [near_ref[...].astype(jnp.float32), far_ref[...].astype(jnp.float32)], axis=0
    )
    slots = part.shape[0]
    extra = part[:, QUERIES:]
    column = [extra[:, i * HEADS : (i + 1) * HEADS] for i in range(7)]
    peaks = column[0] + column[1] + column[2]
    totals = column[3] + column[4] + column[5]
    tag = column[6][:, :1]
    row = lax.broadcasted_iota(jnp.int32, (requests, 1), 0).astype(jnp.float32)
    member = (
        tag == lax.broadcasted_iota(jnp.int32, (slots, requests), 1).astype(jnp.float32)
    ).astype(jnp.float32).astype(jnp.bfloat16)
    expand = head_columns()
    own = own_ref[...]
    tops = [own] + [jnp.full(own.shape, NEGATIVE, jnp.float32)] * 3
    for s in range(slots):
        tops[s % 4] = jnp.maximum(
            tops[s % 4], jnp.where(tag[s : s + 1] == row, peaks[s : s + 1], NEGATIVE)
        )
    top = jnp.maximum(jnp.maximum(tops[0], tops[1]), jnp.maximum(tops[2], tops[3]))
    own_weight = jnp.exp(own - top)
    weight = jnp.exp(peaks - spread_dot(top, member, ((1,), (0,)), 3, True))
    total = spread_dot(weight * totals, member, ((0,), (0,)), 3, True) + own_weight
    inverse = 1.0 / total
    weight = weight * spread_dot(inverse, member, ((1,), (0,)), 3, True)
    scaled = part[:, :QUERIES] * spread_dot(weight, expand, ((1,), (0,)), 2)
    mixed = spread_dot(scaled, member, ((0,), (0,)), 2, True)
    own_share = spread_dot(own_weight * inverse, expand, ((1,), (0,)), 2)
    mixed = mixed + own_share * jnp.concatenate([value_ref[...]] * REPEAT, axis=1)
    mixed = mixed.astype(jnp.bfloat16)
    for h in range(HEADS):
        at = (h % REPEAT * KV_HEADS + h // REPEAT) * HEAD_DIM
        out_ref[:, h * HEAD_DIM : (h + 1) * HEAD_DIM] = mixed[:, at : at + HEAD_DIM]


def combine(near, far, own, value):
    return pl.pallas_call(
        combine_kernel,
        out_shape=jax.ShapeDtypeStruct((own.shape[0], QUERIES), jnp.bfloat16),
        in_specs=[VMEM] * 4,
        out_specs=VMEM,
        compiler_params=pltpu.CompilerParams(vmem_limit_bytes=48 * 1024 * 1024),
        name="combine",
    )(near, far, own, value)


def per_device(
    tokens, norm_gain, w_query, w_keyvalue, cache, page_count, page_owner, keep_rows, dest_slot
):
    holder = lax.axis_index("page")
    group = lax.axis_index("tensor")
    half = group % 2
    place = jnp.stack([group // 2, half, holder % 2])
    share = tokens.shape[0] // HOLDERS

    def normalise(rows):
        widened = rows.astype(jnp.float32)
        return (
            widened
            * lax.rsqrt(jnp.mean(widened * widened, axis=-1, keepdims=True) + EPSILON)
            * norm_gain
        ).astype(jnp.bfloat16)

    page_count = page_count.reshape(1)
    page_owner = page_owner.reshape(SOURCES)
    compact, kept = select_rows(page_count, dest_slot.reshape(SOURCES), keep_rows, cache)

    mine = normalise(lax.dynamic_slice_in_dim(tokens, holder * share, share, 0))
    across = lax.ppermute(mine, ("page", "tensor"), OTHER_HALF)
    across, compact = lax.optimization_barrier((across, compact))
    arrived = lax.all_to_all(compact, "page", 0, 0, tiled=True)

    both = jnp.where(
        half == 0,
        jnp.concatenate([mine, across], axis=0),
        jnp.concatenate([across, mine], axis=0),
    )
    rows = lax.all_gather(
        both, "tensor", axis=0, axis_index_groups=PLANE_GROUPS, tiled=True
    )
    projected = project(rows, w_query, w_keyvalue)
    everyone = lax.all_gather(
        projected, "tensor", axis=0, axis_index_groups=PLANE_GROUPS, tiled=False
    )
    halves, arrived = lax.optimization_barrier((pick(place, everyone), arrived))
    near = lax.all_to_all(
        halves, ("page", "tensor"), 0, 0, axis_index_groups=COLUMN_GROUPS, tiled=True
    )
    far = lax.ppermute(near, "page", OTHER_CORE)
    part = attend(place, page_count, page_owner, kept, near, far)
    near_part = lax.all_to_all(
        part, "page", 0, 0, axis_index_groups=RUN_GROUPS, tiled=True
    )
    own, value = own_part(place, near, far)
    near_part, own, value = lax.optimization_barrier((near_part, own, value))
    far_part = lax.ppermute(near_part, "page", OTHER_CORE)
    flat = (CHIPS * SOURCES, QUERIES + EXTRA)
    attended = combine(near_part.reshape(flat), far_part.reshape(flat), own, value)
    return attended, arrived[:, None]


def solution(mesh):
    return jax.shard_map(
        per_device,
        mesh=mesh,
        in_specs=(
            P("tensor", None),
            P(),
            P(None, "tensor"),
            P(None, "tensor"),
            P("page", "tensor", None, None),
            P("page", "tensor"),
            P("page", "tensor"),
            P("page", "tensor", None),
            P("page", "tensor"),
        ),
        out_specs=(P("tensor", None), P("page", "tensor", None, None)),
        check_vma=False,
    )
```

```python
import jax
import jax.numpy as jnp
from jax import lax
from jax.experimental import pallas as pl
from jax.experimental.pallas import tpu as pltpu
from jax.sharding import PartitionSpec as P

HEADS = 32
KV_HEADS = 8
REPEAT = HEADS // KV_HEADS
HEAD_DIM = 80
KEYS = KV_HEADS * HEAD_DIM
QUERIES = HEADS * HEAD_DIM
EPSILON = 1e-05
NEGATIVE = -1e30

PLANE = 16
HOLDERS = 16
SOURCES = 8
KEEP = 32
EXTRA = 256

CHIPS = 8
PLANE_GROUPS = [[2 * i + half for i in range(PLANE)] for half in range(2)]
OTHER_HALF = [
    (p * 2 * PLANE + t, (p ^ 8) * 2 * PLANE + (t ^ 1)) for p in range(HOLDERS) for t in range(2 * PLANE)
]

FOUR_GROUPS = [
    [
        (2 * (4 * quad + z) + core) * 2 * PLANE + 2 * xy + half
        for half in range(2)
        for quad in range(2)
    ]
    for xy in range(PLANE)
    for z in range(CHIPS // 2)
    for core in range(2)
]
QUAD_GROUPS = [[CHIPS * quad + i for i in range(CHIPS)] for quad in range(2)]
OTHER_QUAD = [(i, i ^ CHIPS) for i in range(HOLDERS)]
HALF_COLUMNS = (QUERIES + 2 * KEYS) // 2
STEP = 4

VMEM = pl.BlockSpec(memory_space=pltpu.VMEM)
SMEM = pl.BlockSpec(memory_space=pltpu.SMEM)


def select_kernel(count_ref, dest_ref, keep_ref, page_ref, out_ref, kept_ref):
    step = pl.program_id(0)

    @pl.when(step == 0)
    def _():
        out_ref[...] = jnp.zeros_like(out_ref)

    rows = page_ref.shape[1]
    for i in range(STEP):
        slot = step * STEP + i
        picks = jnp.broadcast_to(keep_ref[i], (rows, KEEP))
        chosen = (picks == lax.broadcasted_iota(jnp.int32, (rows, KEEP), 0)).astype(jnp.float32)
        kept = jnp.dot(
            chosen.T.astype(jnp.bfloat16), page_ref[i], preferred_element_type=jnp.float32
        ).astype(jnp.bfloat16)
        kept_ref[i * KEEP : (i + 1) * KEEP] = kept

        @pl.when(slot < count_ref[0])
        def _():
            out_ref[dest_ref[slot]] = kept


def select_rows(page_count, dest_slot, keep_rows, cache):
    sources, _, rows, width = cache.shape
    return pl.pallas_call(
        select_kernel,
        out_shape=(
            jax.ShapeDtypeStruct((HOLDERS, KEEP, width), cache.dtype),
            jax.ShapeDtypeStruct((sources * KEEP, width), cache.dtype),
        ),
        grid_spec=pltpu.PrefetchScalarGridSpec(
            num_scalar_prefetch=2,
            grid=(sources // STEP,),
            in_specs=[
                pl.BlockSpec((STEP, 1, KEEP), lambda s, *_: (s, 0, 0)),
                pl.BlockSpec((STEP, rows, width), lambda s, *_: (s, 0, 0)),
            ],
            out_specs=[
                pl.BlockSpec((HOLDERS, KEEP, width), lambda s, *_: (0, 0, 0)),
                pl.BlockSpec((STEP * KEEP, width), lambda s, *_: (s, 0)),
            ],
        ),
        name="select_rows",
    )(page_count, dest_slot, keep_rows, cache.reshape(sources, rows, width))


def project_kernel(rows_ref, query_ref, pair_ref, out_ref):
    rows = rows_ref[...]
    for ref, low, high in ((query_ref, 0, HEAD_DIM), (pair_ref, HEAD_DIM, HEAD_DIM * 3 // 2)):
        out_ref[:, low:high] = lax.dot_general(
            rows, ref[...], (((1,), (1,)), ((), ())), preferred_element_type=jnp.float32
        ).astype(jnp.bfloat16)


def project(rows, w_query, w_keyvalue):
    return pl.pallas_call(
        project_kernel,
        out_shape=jax.ShapeDtypeStruct((rows.shape[0], HEAD_DIM * 3 // 2), jnp.bfloat16),
        in_specs=[VMEM] * 3,
        out_specs=VMEM,
        name="project",
    )(rows, w_query.T, w_keyvalue.T)


def pick_kernel(plane_ref, all_ref, out_ref, rows_ref):
    half = HEAD_DIM // 2
    for i in range(PLANE):
        block = all_ref[i].astype(jnp.float32)
        at = (i % 2 * KV_HEADS + i // 2) * HEAD_DIM
        rows_ref[:, at : at + HEAD_DIM] = block[:, :HEAD_DIM]
        at = QUERIES // 2 + i * half
        rows_ref[:, at : at + half] = block[:, HEAD_DIM:]
    share = out_ref.shape[1]
    for h in range(2):
        piece = rows_ref[h * share : (h + 1) * share].astype(jnp.bfloat16)
        for quad in range(2):
            out_ref[2 * h + quad] = piece


def pick(plane, everyone):
    count, rows, width = everyone.shape
    both = rows // PLANE
    piece = jax.ShapeDtypeStruct((4, both // 2, HALF_COLUMNS), everyone.dtype)
    return pl.pallas_call(
        pick_kernel,
        out_shape=piece,
        grid_spec=pltpu.PrefetchScalarGridSpec(
            num_scalar_prefetch=1,
            grid=(1,),
            in_specs=[pl.BlockSpec((count, both, width), lambda i, plane: (0, plane[0], 0))],
            out_specs=pl.BlockSpec(piece.shape, lambda i, *_: (0, 0, 0)),
            scratch_shapes=[pltpu.VMEM((both, HALF_COLUMNS), jnp.float32)],
        ),
        name="pick",
    )(plane, everyone)


def held(rows_ref, holder, half, columns):
    quad, inside = holder // CHIPS, holder % CHIPS
    same = lax.axis_index("tensor") % 2 == half
    spot = inside * 4 + 2 * half + jnp.where(same, quad, 1 - quad)
    return rows_ref[spot, :, columns].astype(jnp.float32)


def pieces(value, count):
    parts = []
    for _ in range(count):
        part = value.astype(jnp.bfloat16)
        parts.append(part)
        value = value - part.astype(jnp.float32)
    return parts


def attend_kernel(
    count_ref, owner_ref, kept_ref, rows_ref, out_ref, sum_ref, peak_ref, total_ref
):
    scale = HEAD_DIM ** (-0.5)
    share = rows_ref.shape[1]
    line = lax.broadcasted_iota(jnp.int32, (share, QUERIES // 2), 0)
    head = lax.broadcasted_iota(jnp.int32, (KV_HEADS, KEYS), 0) * HEAD_DIM
    lane = lax.broadcasted_iota(jnp.int32, (KV_HEADS, KEYS), 1)
    mask = ((lane >= head) & (lane < head + HEAD_DIM)).astype(jnp.float32)
    for s in range(SOURCES):
        request = owner_ref[s]
        holder = request // share
        query = []
        for half in range(2):
            block = held(rows_ref, holder, half, pl.ds(0, QUERIES // 2))
            query.append(
                jnp.sum(jnp.where(line == request % share, block, 0.0), axis=0, keepdims=True)
            )
        spread = jnp.concatenate(
            [
                query[k % 2][:, k // 2 * KEYS : (k // 2 + 1) * KEYS] * mask
                for k in range(REPEAT)
            ],
            axis=0,
        ).astype(jnp.bfloat16)
        keys = kept_ref[s * KEEP : (s + 1) * KEEP, :KEYS]
        values = kept_ref[s * KEEP : (s + 1) * KEEP, KEYS:]
        score = scale * lax.dot_general(
            keys, spread, (((1,), (1,)), ((), ())), preferred_element_type=jnp.float32
        )
        peak = jnp.max(score, axis=0, keepdims=True)
        weight = jnp.exp(score - peak)
        total_ref[s : s + 1, :] = jnp.sum(weight, axis=0, keepdims=True)
        peak_ref[s : s + 1, :] = jnp.where(s < count_ref[0], peak, NEGATIVE)
        mixed = lax.dot_general(
            weight.astype(jnp.bfloat16),
            values,
            (((0,), (0,)), ((), ())),
            preferred_element_type=jnp.float32,
        )
        for k in range(REPEAT):
            sum_ref[s : s + 1, k * KEYS : (k + 1) * KEYS] = jnp.sum(
                mixed[k * KV_HEADS : (k + 1) * KV_HEADS] * mask, axis=0, keepdims=True
            )
    sums = sum_ref[...].astype(jnp.bfloat16)
    slots = lax.broadcasted_iota(jnp.int32, (SOURCES, HEADS), 0)
    tag = jnp.full((SOURCES, HEADS), -1, jnp.int32)
    for s in range(SOURCES):
        tag = jnp.where((slots == s) & (s < count_ref[0]), owner_ref[s], tag)
    tag = tag.astype(jnp.float32).astype(jnp.bfloat16)
    columns = pieces(peak_ref[...], 3) + pieces(total_ref[...], 3) + [tag, tag]
    columns = [column.astype(jnp.float32) for column in columns]
    columns = jnp.concatenate(columns, axis=1).astype(jnp.bfloat16)
    out_ref[:, :QUERIES] = sums
    out_ref[:, QUERIES:] = columns


def attend(page_count, page_owner, kept, rows):
    return pl.pallas_call(
        attend_kernel,
        out_shape=jax.ShapeDtypeStruct((SOURCES, QUERIES + EXTRA), jnp.bfloat16),
        in_specs=[SMEM] * 2 + [VMEM] * 2,
        out_specs=VMEM,
        scratch_shapes=[
            pltpu.VMEM((SOURCES, QUERIES), jnp.float32),
            pltpu.VMEM((SOURCES, HEADS), jnp.float32),
            pltpu.VMEM((SOURCES, HEADS), jnp.float32),
        ],
        name="attend",
    )(page_count, page_owner, kept, rows)


def spread_dot(value, chosen, contract, count, chosen_first=False):
    total = None
    for part in pieces(value, count):
        operands = (chosen, part) if chosen_first else (part, chosen)
        term = lax.dot_general(
            *operands, (contract, ((), ())), preferred_element_type=jnp.float32
        )
        total = term if total is None else total + term
    return total


def head_columns():
    head = lax.broadcasted_iota(jnp.int32, (HEADS, QUERIES), 0) * HEAD_DIM
    lane = lax.broadcasted_iota(jnp.int32, (HEADS, QUERIES), 1)
    return ((lane >= head) & (lane < head + HEAD_DIM)).astype(jnp.float32).astype(jnp.bfloat16)


def own_kernel(rows_ref, score_ref, value_ref, query_ref, pair_ref):
    scale = HEAD_DIM ** (-0.5)
    share = rows_ref.shape[1]
    piece = HEAD_DIM // 2
    for holder in range(HOLDERS):
        rows = slice(holder * share, (holder + 1) * share)
        for half in range(2):
            block = held(rows_ref, holder, half, pl.ds(0, HALF_COLUMNS))
            for k in range(2):
                at = (2 * k + half) * KEYS
                query_ref[rows, at : at + KEYS] = block[:, k * KEYS : (k + 1) * KEYS]
            pair_ref[half, rows, :] = block[:, QUERIES // 2 :]
    keys, values = [], []
    for g in range(KV_HEADS):
        for half in range(2):
            keys.append(pair_ref[half, :, g * piece : (g + 1) * piece])
            at = KEYS // 2 + g * piece
            values.append(pair_ref[half, :, at : at + piece])
    key = jnp.concatenate(keys, axis=1)
    value_ref[...] = jnp.concatenate(values, axis=1)
    product = query_ref[...] * jnp.concatenate([key] * REPEAT, axis=1)
    score_ref[...] = scale * spread_dot(product, head_columns(), ((1,), (1,)), 3)


def own_part(rows):
    requests = HOLDERS * rows.shape[1]
    return pl.pallas_call(
        own_kernel,
        out_shape=(
            jax.ShapeDtypeStruct((requests, HEADS), jnp.float32),
            jax.ShapeDtypeStruct((requests, KEYS), jnp.float32),
        ),
        in_specs=[VMEM],
        out_specs=(VMEM, VMEM),
        scratch_shapes=[
            pltpu.VMEM((requests, QUERIES), jnp.float32),
            pltpu.VMEM((2, requests, KEYS), jnp.float32),
        ],
        name="own_part",
    )(rows)


def combine_kernel(part_ref, own_ref, value_ref, out_ref):
    requests = out_ref.shape[0]
    slots = part_ref.shape[0]
    extra = part_ref[:, QUERIES:].astype(jnp.float32)
    column = [extra[:, i * HEADS : (i + 1) * HEADS] for i in range(7)]
    peaks = column[0] + column[1] + column[2]
    totals = column[3] + column[4] + column[5]
    tag = column[6][:, :1]
    row = lax.broadcasted_iota(jnp.int32, (requests, 1), 0).astype(jnp.float32)
    member = (
        tag == lax.broadcasted_iota(jnp.int32, (slots, requests), 1).astype(jnp.float32)
    ).astype(jnp.float32).astype(jnp.bfloat16)
    expand = head_columns()
    own = own_ref[...]
    tops = [own] + [jnp.full(own.shape, NEGATIVE, jnp.float32)] * 3
    for s in range(slots):
        tops[s % 4] = jnp.maximum(
            tops[s % 4], jnp.where(tag[s : s + 1] == row, peaks[s : s + 1], NEGATIVE)
        )
    top = jnp.maximum(jnp.maximum(tops[0], tops[1]), jnp.maximum(tops[2], tops[3]))
    own_weight = jnp.exp(own - top)
    weight = jnp.exp(peaks - spread_dot(top, member, ((1,), (0,)), 3, True))
    total = spread_dot(weight * totals, member, ((0,), (0,)), 3, True) + own_weight
    inverse = 1.0 / total
    weight = weight * spread_dot(inverse, member, ((1,), (0,)), 3, True)
    scaled = part_ref[:, :QUERIES].astype(jnp.float32) * spread_dot(weight, expand, ((1,), (0,)), 2)
    mixed = spread_dot(scaled, member, ((0,), (0,)), 2, True)
    own_share = spread_dot(own_weight * inverse, expand, ((1,), (0,)), 2)
    mixed = mixed + own_share * jnp.concatenate([value_ref[...]] * REPEAT, axis=1)
    mixed = mixed.astype(jnp.bfloat16)
    for h in range(HEADS):
        at = (h % REPEAT * KV_HEADS + h // REPEAT) * HEAD_DIM
        out_ref[:, h * HEAD_DIM : (h + 1) * HEAD_DIM] = mixed[:, at : at + HEAD_DIM]


def combine(parts, own, value):
    return pl.pallas_call(
        combine_kernel,
        out_shape=jax.ShapeDtypeStruct((own.shape[0], QUERIES), jnp.bfloat16),
        in_specs=[VMEM] * 3,
        out_specs=VMEM,
        compiler_params=pltpu.CompilerParams(vmem_limit_bytes=48 * 1024 * 1024),
        name="combine",
    )(parts, own, value)


def settle_kernel(in_ref, out_ref):
    out_ref[...] = in_ref[...]


def settle(pages):
    block = pl.BlockSpec((4,) + pages.shape[1:], lambda i: (i, 0, 0))
    return pl.pallas_call(
        settle_kernel,
        out_shape=jax.ShapeDtypeStruct(pages.shape, pages.dtype),
        grid=(pages.shape[0] // 4,),
        in_specs=[block],
        out_specs=block,
        name="settle",
    )(pages)


def per_device(
    tokens, norm_gain, w_query, w_keyvalue, cache, page_count, page_owner, keep_rows, dest_slot
):
    holder = lax.axis_index("page")
    group = lax.axis_index("tensor")
    half = group % 2
    share = tokens.shape[0] // HOLDERS

    def normalise(rows):
        widened = rows.astype(jnp.float32)
        return (
            widened
            * lax.rsqrt(jnp.mean(widened * widened, axis=-1, keepdims=True) + EPSILON)
            * norm_gain
        ).astype(jnp.bfloat16)

    page_count = page_count.reshape(1)
    page_owner = page_owner.reshape(SOURCES)
    compact, kept = select_rows(page_count, dest_slot.reshape(SOURCES), keep_rows, cache)

    mine = normalise(lax.dynamic_slice_in_dim(tokens, holder * share, share, 0))
    across = lax.ppermute(mine, ("page", "tensor"), OTHER_HALF)
    across, compact = lax.optimization_barrier((across, compact))
    arrived = lax.all_to_all(compact, "page", 0, 0, tiled=True)

    both = jnp.where(
        half == 0,
        jnp.concatenate([mine, across], axis=0),
        jnp.concatenate([across, mine], axis=0),
    )
    rows = lax.all_gather(
        both, "tensor", axis=0, axis_index_groups=PLANE_GROUPS, tiled=True
    )
    projected = project(rows, w_query, w_keyvalue)
    everyone = lax.all_gather(
        projected, "tensor", axis=0, axis_index_groups=PLANE_GROUPS, tiled=False
    )
    halves = pick((group // 2).reshape(1), everyone)
    halves, arrived = lax.optimization_barrier((halves, arrived))
    quarter = lax.all_to_all(
        halves, ("page", "tensor"), 0, 0, axis_index_groups=FOUR_GROUPS, tiled=True
    )
    rows = lax.all_gather(quarter, "page", axis=0, axis_index_groups=QUAD_GROUPS, tiled=True)
    part = attend(page_count, page_owner, kept, rows)
    far = lax.ppermute(part, "page", OTHER_QUAD)
    own, value = own_part(rows)
    settled = settle(arrived)
    far, own, value, settled = lax.optimization_barrier((far, own, value, settled))
    parts = lax.all_gather(
        jnp.concatenate([part, far], axis=0),
        "page",
        axis=0,
        axis_index_groups=QUAD_GROUPS,
        tiled=True,
    )
    return combine(parts, own, value), settled[:, None]


def solution(mesh):
    return jax.shard_map(
        per_device,
        mesh=mesh,
        in_specs=(
            P("tensor", None),
            P(),
            P(None, "tensor"),
            P(None, "tensor"),
            P("page", "tensor", None, None),
            P("page", "tensor"),
            P("page", "tensor"),
            P("page", "tensor", None),
            P("page", "tensor"),
        ),
        out_specs=(P("tensor", None), P("page", "tensor", None, None)),
        check_vma=False,
    )
```

```python
import jax
import jax.numpy as jnp
from jax import lax
from jax.experimental import pallas as pl
from jax.experimental.pallas import tpu as pltpu
from jax.sharding import PartitionSpec as P

HEADS = 32
KV_HEADS = 8
REPEAT = HEADS // KV_HEADS
HEAD_DIM = 80
KEYS = KV_HEADS * HEAD_DIM
QUERIES = HEADS * HEAD_DIM
EPSILON = 1e-05
NEGATIVE = -1e30

PLANE = 16
HOLDERS = 16
SOURCES = 8
KEEP = 32
EXTRA = 256

CHIPS = 8
PLANE_GROUPS = [[2 * i + half for i in range(PLANE)] for half in range(2)]
OTHER_HALF = [
    (p * 2 * PLANE + t, (p ^ 8) * 2 * PLANE + (t ^ 1)) for p in range(HOLDERS) for t in range(2 * PLANE)
]

FOUR_GROUPS = [
    [
        (2 * (4 * quad + z) + core) * 2 * PLANE + 2 * xy + half
        for half in range(2)
        for quad in range(2)
    ]
    for xy in range(PLANE)
    for z in range(CHIPS // 2)
    for core in range(2)
]
QUAD_GROUPS = [[CHIPS * quad + i for i in range(CHIPS)] for quad in range(2)]
OTHER_CORE = [(i, i ^ 1) for i in range(HOLDERS)]
OTHER_CHIP = [[(i, i ^ (2 * d)) for i in range(HOLDERS)] for d in range(CHIPS)]
OTHER_QUAD = [(i, i ^ CHIPS) for i in range(HOLDERS)]
HALF_COLUMNS = (QUERIES + 2 * KEYS) // 2
STEP = 4

VMEM = pl.BlockSpec(memory_space=pltpu.VMEM)
SMEM = pl.BlockSpec(memory_space=pltpu.SMEM)


def select_kernel(count_ref, dest_ref, keep_ref, page_ref, *refs):
    out_refs, kept_ref = refs[:CHIPS], refs[CHIPS]
    grid_step = pl.program_id(0)
    holder = lax.axis_index("page")

    @pl.when(grid_step == 0)
    def _():
        for ref in out_refs:
            ref[...] = jnp.zeros_like(ref)

    rows = page_ref.shape[1]
    for i in range(STEP):
        slot = grid_step * STEP + i
        picks = jnp.broadcast_to(keep_ref[i], (rows, KEEP))
        chosen = (picks == lax.broadcasted_iota(jnp.int32, (rows, KEEP), 0)).astype(jnp.float32)
        kept = jnp.dot(
            chosen.T.astype(jnp.bfloat16), page_ref[i], preferred_element_type=jnp.float32
        ).astype(jnp.bfloat16)
        kept_ref[i * KEEP : (i + 1) * KEEP] = kept
        target = dest_ref[slot] ^ holder
        live = slot < count_ref[0]
        for d in range(CHIPS):

            @pl.when(live & (target // 2 == d))
            def _():
                out_refs[d][target % 2] = kept_ref[i * KEEP : (i + 1) * KEEP]


def select_rows(page_count, dest_slot, keep_rows, cache):
    sources, _, rows, width = cache.shape
    block = jax.ShapeDtypeStruct((2, KEEP, width), cache.dtype)
    results = pl.pallas_call(
        select_kernel,
        out_shape=[block] * CHIPS + [jax.ShapeDtypeStruct((sources * KEEP, width), cache.dtype)],
        grid_spec=pltpu.PrefetchScalarGridSpec(
            num_scalar_prefetch=2,
            grid=(sources // STEP,),
            in_specs=[
                pl.BlockSpec((STEP, 1, KEEP), lambda s, *_: (s, 0, 0)),
                pl.BlockSpec((STEP, rows, width), lambda s, *_: (s, 0, 0)),
            ],
            out_specs=[pl.BlockSpec(block.shape, lambda s, *_: (0, 0, 0))] * CHIPS
            + [pl.BlockSpec((STEP * KEEP, width), lambda s, *_: (s, 0))],
        ),
        name="select_rows",
    )(page_count, dest_slot, keep_rows, cache.reshape(sources, rows, width))
    return results[:CHIPS], results[CHIPS]


def pack_kernel(*refs):
    for d in range(CHIPS):
        refs[CHIPS][d] = refs[d][1]


def pack(got):
    return pl.pallas_call(
        pack_kernel,
        out_shape=jax.ShapeDtypeStruct((CHIPS,) + got[0].shape[1:], got[0].dtype),
        in_specs=[VMEM] * CHIPS,
        out_specs=VMEM,
        name="pack",
    )(*got)


def place_kernel(*refs):
    got_refs, cross_ref, out_ref = refs[:CHIPS], refs[CHIPS], refs[CHIPS + 1]
    holder = lax.axis_index("page")
    for d in range(CHIPS):
        out_ref[holder ^ (2 * d)] = got_refs[d][0]
        out_ref[holder ^ (2 * d + 1)] = cross_ref[d]


def place_pages(got, cross):
    return pl.pallas_call(
        place_kernel,
        out_shape=jax.ShapeDtypeStruct((HOLDERS,) + cross.shape[1:], cross.dtype),
        in_specs=[VMEM] * (CHIPS + 1),
        out_specs=VMEM,
        name="place_pages",
    )(*got, cross)


def project_kernel(rows_ref, query_ref, pair_ref, out_ref):
    rows = rows_ref[...]
    for ref, low, high in ((query_ref, 0, HEAD_DIM), (pair_ref, HEAD_DIM, HEAD_DIM * 3 // 2)):
        out_ref[:, low:high] = lax.dot_general(
            rows, ref[...], (((1,), (1,)), ((), ())), preferred_element_type=jnp.float32
        ).astype(jnp.bfloat16)


def project(rows, w_query, w_keyvalue):
    return pl.pallas_call(
        project_kernel,
        out_shape=jax.ShapeDtypeStruct((rows.shape[0], HEAD_DIM * 3 // 2), jnp.bfloat16),
        in_specs=[VMEM] * 3,
        out_specs=VMEM,
        name="project",
    )(rows, w_query.T, w_keyvalue.T)


def pick_kernel(all_ref, out_ref, rows_ref):
    half = HEAD_DIM // 2
    for i in range(PLANE):
        block = all_ref[i].astype(jnp.float32)
        at = (i % 2 * KV_HEADS + i // 2) * HEAD_DIM
        rows_ref[:, at : at + HEAD_DIM] = block[:, :HEAD_DIM]
        at = QUERIES // 2 + i * half
        rows_ref[:, at : at + half] = block[:, HEAD_DIM:]
    share = out_ref.shape[1]
    for h in range(2):
        piece = rows_ref[h * share : (h + 1) * share].astype(jnp.bfloat16)
        for quad in range(2):
            out_ref[2 * h + quad] = piece


def pick(block):
    count, both, _ = block.shape
    return pl.pallas_call(
        pick_kernel,
        out_shape=jax.ShapeDtypeStruct((4, both // 2, HALF_COLUMNS), block.dtype),
        in_specs=[VMEM],
        out_specs=VMEM,
        scratch_shapes=[pltpu.VMEM((both, HALF_COLUMNS), jnp.float32)],
        name="pick",
    )(block)


def held(rows_ref, holder, half, columns):
    quad, inside = holder // CHIPS, holder % CHIPS
    same = lax.axis_index("tensor") % 2 == half
    spot = inside * 4 + 2 * half + jnp.where(same, quad, 1 - quad)
    return rows_ref[spot, :, columns].astype(jnp.float32)


def pieces(value, count):
    parts = []
    for _ in range(count):
        part = value.astype(jnp.bfloat16)
        parts.append(part)
        value = value - part.astype(jnp.float32)
    return parts


def attend_kernel(
    count_ref, owner_ref, kept_ref, rows_ref, out_ref, sum_ref, peak_ref, total_ref
):
    scale = HEAD_DIM ** (-0.5)
    share = rows_ref.shape[1]
    line = lax.broadcasted_iota(jnp.int32, (share, QUERIES // 2), 0)
    head = lax.broadcasted_iota(jnp.int32, (KV_HEADS, KEYS), 0) * HEAD_DIM
    lane = lax.broadcasted_iota(jnp.int32, (KV_HEADS, KEYS), 1)
    mask = ((lane >= head) & (lane < head + HEAD_DIM)).astype(jnp.float32)
    for s in range(SOURCES):
        request = owner_ref[s]
        holder = request // share
        query = []
        for half in range(2):
            block = held(rows_ref, holder, half, pl.ds(0, QUERIES // 2))
            query.append(
                jnp.sum(jnp.where(line == request % share, block, 0.0), axis=0, keepdims=True)
            )
        spread = jnp.concatenate(
            [
                query[k % 2][:, k // 2 * KEYS : (k // 2 + 1) * KEYS] * mask
                for k in range(REPEAT)
            ],
            axis=0,
        ).astype(jnp.bfloat16)
        keys = kept_ref[s * KEEP : (s + 1) * KEEP, :KEYS]
        values = kept_ref[s * KEEP : (s + 1) * KEEP, KEYS:]
        score = scale * lax.dot_general(
            keys, spread, (((1,), (1,)), ((), ())), preferred_element_type=jnp.float32
        )
        peak = jnp.max(score, axis=0, keepdims=True)
        weight = jnp.exp(score - peak)
        total_ref[s : s + 1, :] = jnp.sum(weight, axis=0, keepdims=True)
        peak_ref[s : s + 1, :] = jnp.where(s < count_ref[0], peak, NEGATIVE)
        mixed = lax.dot_general(
            weight.astype(jnp.bfloat16),
            values,
            (((0,), (0,)), ((), ())),
            preferred_element_type=jnp.float32,
        )
        for k in range(REPEAT):
            sum_ref[s : s + 1, k * KEYS : (k + 1) * KEYS] = jnp.sum(
                mixed[k * KV_HEADS : (k + 1) * KV_HEADS] * mask, axis=0, keepdims=True
            )
    sums = sum_ref[...].astype(jnp.bfloat16)
    slots = lax.broadcasted_iota(jnp.int32, (SOURCES, HEADS), 0)
    tag = jnp.full((SOURCES, HEADS), -1, jnp.int32)
    for s in range(SOURCES):
        tag = jnp.where((slots == s) & (s < count_ref[0]), owner_ref[s], tag)
    tag = tag.astype(jnp.float32).astype(jnp.bfloat16)
    columns = pieces(peak_ref[...], 3) + pieces(total_ref[...], 3) + [tag, tag]
    columns = [column.astype(jnp.float32) for column in columns]
    columns = jnp.concatenate(columns, axis=1).astype(jnp.bfloat16)
    out_ref[:, :QUERIES] = sums
    out_ref[:, QUERIES:] = columns


def attend(page_count, page_owner, kept, rows):
    return pl.pallas_call(
        attend_kernel,
        out_shape=jax.ShapeDtypeStruct((SOURCES, QUERIES + EXTRA), jnp.bfloat16),
        in_specs=[SMEM] * 2 + [VMEM] * 2,
        out_specs=VMEM,
        scratch_shapes=[
            pltpu.VMEM((SOURCES, QUERIES), jnp.float32),
            pltpu.VMEM((SOURCES, HEADS), jnp.float32),
            pltpu.VMEM((SOURCES, HEADS), jnp.float32),
        ],
        name="attend",
    )(page_count, page_owner, kept, rows)


def spread_dot(value, chosen, contract, count, chosen_first=False):
    total = None
    for part in pieces(value, count):
        operands = (chosen, part) if chosen_first else (part, chosen)
        term = lax.dot_general(
            *operands, (contract, ((), ())), preferred_element_type=jnp.float32
        )
        total = term if total is None else total + term
    return total


def head_columns():
    head = lax.broadcasted_iota(jnp.int32, (HEADS, QUERIES), 0) * HEAD_DIM
    lane = lax.broadcasted_iota(jnp.int32, (HEADS, QUERIES), 1)
    return ((lane >= head) & (lane < head + HEAD_DIM)).astype(jnp.float32).astype(jnp.bfloat16)


def own_kernel(rows_ref, score_ref, value_ref, query_ref, pair_ref):
    scale = HEAD_DIM ** (-0.5)
    share = rows_ref.shape[1]
    piece = HEAD_DIM // 2
    for holder in range(HOLDERS):
        rows = slice(holder * share, (holder + 1) * share)
        for half in range(2):
            block = held(rows_ref, holder, half, pl.ds(0, HALF_COLUMNS))
            for k in range(2):
                at = (2 * k + half) * KEYS
                query_ref[rows, at : at + KEYS] = block[:, k * KEYS : (k + 1) * KEYS]
            pair_ref[half, rows, :] = block[:, QUERIES // 2 :]
    keys, values = [], []
    for g in range(KV_HEADS):
        for half in range(2):
            keys.append(pair_ref[half, :, g * piece : (g + 1) * piece])
            at = KEYS // 2 + g * piece
            values.append(pair_ref[half, :, at : at + piece])
    key = jnp.concatenate(keys, axis=1)
    value_ref[...] = jnp.concatenate(values, axis=1)
    product = query_ref[...] * jnp.concatenate([key] * REPEAT, axis=1)
    score_ref[...] = scale * spread_dot(product, head_columns(), ((1,), (1,)), 3)


def own_part(rows):
    requests = HOLDERS * rows.shape[1]
    return pl.pallas_call(
        own_kernel,
        out_shape=(
            jax.ShapeDtypeStruct((requests, HEADS), jnp.float32),
            jax.ShapeDtypeStruct((requests, KEYS), jnp.float32),
        ),
        in_specs=[VMEM],
        out_specs=(VMEM, VMEM),
        scratch_shapes=[
            pltpu.VMEM((requests, QUERIES), jnp.float32),
            pltpu.VMEM((2, requests, KEYS), jnp.float32),
        ],
        name="own_part",
    )(rows)


def combine_kernel(part_ref, own_ref, value_ref, out_ref):
    requests = out_ref.shape[0]
    slots = part_ref.shape[0]
    extra = part_ref[:, QUERIES:].astype(jnp.float32)
    column = [extra[:, i * HEADS : (i + 1) * HEADS] for i in range(7)]
    peaks = column[0] + column[1] + column[2]
    totals = column[3] + column[4] + column[5]
    tag = column[6][:, :1]
    row = lax.broadcasted_iota(jnp.int32, (requests, 1), 0).astype(jnp.float32)
    member = (
        tag == lax.broadcasted_iota(jnp.int32, (slots, requests), 1).astype(jnp.float32)
    ).astype(jnp.float32).astype(jnp.bfloat16)
    expand = head_columns()
    own = own_ref[...]
    tops = [own] + [jnp.full(own.shape, NEGATIVE, jnp.float32)] * 3
    for s in range(slots):
        tops[s % 4] = jnp.maximum(
            tops[s % 4], jnp.where(tag[s : s + 1] == row, peaks[s : s + 1], NEGATIVE)
        )
    top = jnp.maximum(jnp.maximum(tops[0], tops[1]), jnp.maximum(tops[2], tops[3]))
    own_weight = jnp.exp(own - top)
    weight = jnp.exp(peaks - spread_dot(top, member, ((1,), (0,)), 3, True))
    total = spread_dot(weight * totals, member, ((0,), (0,)), 3, True) + own_weight
    inverse = 1.0 / total
    weight = weight * spread_dot(inverse, member, ((1,), (0,)), 3, True)
    scaled = part_ref[:, :QUERIES].astype(jnp.float32) * spread_dot(weight, expand, ((1,), (0,)), 2)
    mixed = spread_dot(scaled, member, ((0,), (0,)), 2, True)
    own_share = spread_dot(own_weight * inverse, expand, ((1,), (0,)), 2)
    mixed = mixed + own_share * jnp.concatenate([value_ref[...]] * REPEAT, axis=1)
    mixed = mixed.astype(jnp.bfloat16)
    for h in range(HEADS):
        at = (h % REPEAT * KV_HEADS + h // REPEAT) * HEAD_DIM
        out_ref[:, h * HEAD_DIM : (h + 1) * HEAD_DIM] = mixed[:, at : at + HEAD_DIM]


def combine(parts, own, value):
    return pl.pallas_call(
        combine_kernel,
        out_shape=jax.ShapeDtypeStruct((own.shape[0], QUERIES), jnp.bfloat16),
        in_specs=[VMEM] * 3,
        out_specs=VMEM,
        compiler_params=pltpu.CompilerParams(vmem_limit_bytes=48 * 1024 * 1024),
        name="combine",
    )(parts, own, value)


def per_device(
    tokens, norm_gain, w_query, w_keyvalue, cache, page_count, page_owner, keep_rows, dest_slot
):
    holder = lax.axis_index("page")
    half = lax.axis_index("tensor") % 2
    share = tokens.shape[0] // HOLDERS

    def normalise(rows):
        widened = rows.astype(jnp.float32)
        return (
            widened
            * lax.rsqrt(jnp.mean(widened * widened, axis=-1, keepdims=True) + EPSILON)
            * norm_gain
        ).astype(jnp.bfloat16)

    page_count = page_count.reshape(1)
    page_owner = page_owner.reshape(SOURCES)
    compact, kept = select_rows(page_count, dest_slot.reshape(SOURCES), keep_rows, cache)

    mine = normalise(lax.dynamic_slice_in_dim(tokens, holder * share, share, 0))
    across = lax.ppermute(mine, ("page", "tensor"), OTHER_HALF)
    got = [compact[0]] + [None] * (CHIPS - 1)

    def send(after, steps):
        blocks, after = lax.optimization_barrier(([compact[d] for d in steps], after))
        for d, block in zip(steps, blocks):
            got[d] = lax.ppermute(block, "page", OTHER_CHIP[d])
        return after

    def receive(before, steps):
        blocks, before = lax.optimization_barrier(([got[d] for d in steps], before))
        for d, block in zip(steps, blocks):
            got[d] = block
        return before

    across = send(across, (4, 5, 1))
    both = jnp.where(
        half == 0,
        jnp.concatenate([mine, across], axis=0),
        jnp.concatenate([across, mine], axis=0),
    )
    rows = lax.all_to_all(
        jnp.broadcast_to(both[None], (PLANE,) + both.shape),
        "tensor",
        0,
        0,
        axis_index_groups=PLANE_GROUPS,
        tiled=True,
    ).reshape(PLANE * both.shape[0], -1)
    rows = send(rows, (2,))
    projected = project(rows, w_query, w_keyvalue).reshape(PLANE, both.shape[0], -1)
    back = lax.all_to_all(
        projected, "tensor", 0, 0, axis_index_groups=PLANE_GROUPS, tiled=True
    )
    halves = receive(pick(back), (4, 5, 1))
    halves = send(halves, (6, 3))
    quarter = lax.all_to_all(
        halves, ("page", "tensor"), 0, 0, axis_index_groups=FOUR_GROUPS, tiled=True
    )
    rows = lax.all_gather(quarter, "page", axis=0, axis_index_groups=QUAD_GROUPS, tiled=True)
    rows = receive(rows, (2,))
    part = attend(page_count, page_owner, kept, rows)
    far = lax.ppermute(part, "page", OTHER_QUAD)
    own, value = own_part(rows)
    own = send(own, (7,))
    far, own, value = lax.optimization_barrier((far, own, value))
    far = receive(far, (6, 3))
    parts = lax.all_gather(
        jnp.concatenate([part, far], axis=0),
        "page",
        axis=0,
        axis_index_groups=QUAD_GROUPS,
        tiled=True,
    )
    parts = receive(parts, (7,))
    cross = lax.ppermute(pack(got), "page", OTHER_CORE)
    attended = combine(parts, own, value)
    return attended, place_pages(got, cross)[:, None]


def solution(mesh):
    return jax.shard_map(
        per_device,
        mesh=mesh,
        in_specs=(
            P("tensor", None),
            P(),
            P(None, "tensor"),
            P(None, "tensor"),
            P("page", "tensor", None, None),
            P("page", "tensor"),
            P("page", "tensor"),
            P("page", "tensor", None),
            P("page", "tensor"),
        ),
        out_specs=(P("tensor", None), P("page", "tensor", None, None)),
        check_vma=False,
    )
```

```python
import jax
import jax.numpy as jnp
from jax import lax
from jax.experimental import pallas as pl
from jax.experimental.pallas import tpu as pltpu
from jax.sharding import PartitionSpec as P

HEADS = 32
KV_HEADS = 8
REPEAT = HEADS // KV_HEADS
HEAD_DIM = 80
KEYS = KV_HEADS * HEAD_DIM
QUERIES = HEADS * HEAD_DIM
EPSILON = 1e-05
NEGATIVE = -1e30

PLANE = 16
HOLDERS = 16
SOURCES = 8
KEEP = 32
EXTRA = 256

CHIPS = 8
PLANE_GROUPS = [[2 * i + half for i in range(PLANE)] for half in range(2)]
OTHER_HALF = [
    (p * 2 * PLANE + t, (p ^ 8) * 2 * PLANE + (t ^ 1)) for p in range(HOLDERS) for t in range(2 * PLANE)
]

FOUR_GROUPS = [
    [
        (2 * (4 * quad + z) + core) * 2 * PLANE + 2 * xy + half
        for half in range(2)
        for quad in range(2)
    ]
    for xy in range(PLANE)
    for z in range(CHIPS // 2)
    for core in range(2)
]
QUAD_GROUPS = [[CHIPS * quad + i for i in range(CHIPS)] for quad in range(2)]
OTHER_QUAD = [(i, i ^ CHIPS) for i in range(HOLDERS)]
HALF_COLUMNS = (QUERIES + 2 * KEYS) // 2
STEP = 4

VMEM = pl.BlockSpec(memory_space=pltpu.VMEM)
SMEM = pl.BlockSpec(memory_space=pltpu.SMEM)


def select_kernel(count_ref, dest_ref, keep_ref, page_ref, near_ref, far_ref, kept_ref):
    grid_step = pl.program_id(0)
    quad = lax.axis_index("page") // CHIPS

    @pl.when(grid_step == 0)
    def _():
        near_ref[...] = jnp.zeros_like(near_ref)
        far_ref[...] = jnp.zeros_like(far_ref)

    rows = page_ref.shape[1]
    for i in range(STEP):
        slot = grid_step * STEP + i
        picks = jnp.broadcast_to(keep_ref[i], (rows, KEEP))
        chosen = (picks == lax.broadcasted_iota(jnp.int32, (rows, KEEP), 0)).astype(jnp.float32)
        kept = jnp.dot(
            chosen.T.astype(jnp.bfloat16), page_ref[i], preferred_element_type=jnp.float32
        ).astype(jnp.bfloat16)
        kept_ref[i * KEEP : (i + 1) * KEEP] = kept
        target = dest_ref[slot]
        live = slot < count_ref[0]
        same = target // CHIPS == quad

        @pl.when(live & same)
        def _():
            near_ref[target % CHIPS] = kept

        @pl.when(live & jnp.logical_not(same))
        def _():
            far_ref[target % CHIPS] = kept


def select_rows(page_count, dest_slot, keep_rows, cache):
    sources, _, rows, width = cache.shape
    block = jax.ShapeDtypeStruct((CHIPS, KEEP, width), cache.dtype)
    whole = pl.BlockSpec(block.shape, lambda s, *_: (0, 0, 0))
    return pl.pallas_call(
        select_kernel,
        out_shape=(block, block, jax.ShapeDtypeStruct((sources * KEEP, width), cache.dtype)),
        grid_spec=pltpu.PrefetchScalarGridSpec(
            num_scalar_prefetch=2,
            grid=(sources // STEP,),
            in_specs=[
                pl.BlockSpec((STEP, 1, KEEP), lambda s, *_: (s, 0, 0)),
                pl.BlockSpec((STEP, rows, width), lambda s, *_: (s, 0, 0)),
            ],
            out_specs=(whole, whole, pl.BlockSpec((STEP * KEEP, width), lambda s, *_: (s, 0))),
        ),
        name="select_rows",
    )(page_count, dest_slot, keep_rows, cache.reshape(sources, rows, width))


def join_kernel(near_ref, far_ref, out_ref):
    quad = lax.axis_index("page") // CHIPS
    for i in range(near_ref.shape[0]):
        out_ref[i, quad] = near_ref[i]
        out_ref[i, 1 - quad] = far_ref[i]


def join(near, far):
    count, keep, width = near.shape
    block = pl.BlockSpec((STEP, keep, width), lambda i: (i, 0, 0))
    return pl.pallas_call(
        join_kernel,
        out_shape=jax.ShapeDtypeStruct((count, 2, keep, width), near.dtype),
        grid=(count // STEP,),
        in_specs=[block, block],
        out_specs=pl.BlockSpec((STEP, 2, keep, width), lambda i: (i, 0, 0, 0)),
        name="join",
    )(near, far)


def project_kernel(rows_ref, query_ref, pair_ref, out_ref):
    rows = rows_ref[...]
    for ref, low, high in ((query_ref, 0, HEAD_DIM), (pair_ref, HEAD_DIM, HEAD_DIM * 3 // 2)):
        out_ref[:, low:high] = lax.dot_general(
            rows, ref[...], (((1,), (1,)), ((), ())), preferred_element_type=jnp.float32
        ).astype(jnp.bfloat16)


def project(rows, w_query, w_keyvalue):
    return pl.pallas_call(
        project_kernel,
        out_shape=jax.ShapeDtypeStruct((rows.shape[0], HEAD_DIM * 3 // 2), jnp.bfloat16),
        in_specs=[VMEM] * 3,
        out_specs=VMEM,
        name="project",
    )(rows, w_query.T, w_keyvalue.T)


def pick_kernel(all_ref, out_ref, rows_ref):
    half = HEAD_DIM // 2
    for i in range(PLANE):
        block = all_ref[i].astype(jnp.float32)
        at = (i % 2 * KV_HEADS + i // 2) * HEAD_DIM
        rows_ref[:, at : at + HEAD_DIM] = block[:, :HEAD_DIM]
        at = QUERIES // 2 + i * half
        rows_ref[:, at : at + half] = block[:, HEAD_DIM:]
    share = out_ref.shape[1]
    for h in range(2):
        piece = rows_ref[h * share : (h + 1) * share].astype(jnp.bfloat16)
        for quad in range(2):
            out_ref[2 * h + quad] = piece


def pick(block):
    count, both, _ = block.shape
    return pl.pallas_call(
        pick_kernel,
        out_shape=jax.ShapeDtypeStruct((4, both // 2, HALF_COLUMNS), block.dtype),
        in_specs=[VMEM],
        out_specs=VMEM,
        scratch_shapes=[pltpu.VMEM((both, HALF_COLUMNS), jnp.float32)],
        name="pick",
    )(block)


def held(rows_ref, holder, half, columns):
    quad, inside = holder // CHIPS, holder % CHIPS
    same = lax.axis_index("tensor") % 2 == half
    spot = inside * 4 + 2 * half + jnp.where(same, quad, 1 - quad)
    return rows_ref[spot, :, columns].astype(jnp.float32)


def pieces(value, count):
    parts = []
    for _ in range(count):
        part = value.astype(jnp.bfloat16)
        parts.append(part)
        value = value - part.astype(jnp.float32)
    return parts


def attend_kernel(
    count_ref, owner_ref, kept_ref, rows_ref, out_ref, sum_ref, peak_ref, total_ref
):
    scale = HEAD_DIM ** (-0.5)
    share = rows_ref.shape[1]
    line = lax.broadcasted_iota(jnp.int32, (share, QUERIES // 2), 0)
    head = lax.broadcasted_iota(jnp.int32, (KV_HEADS, KEYS), 0) * HEAD_DIM
    lane = lax.broadcasted_iota(jnp.int32, (KV_HEADS, KEYS), 1)
    mask = ((lane >= head) & (lane < head + HEAD_DIM)).astype(jnp.float32)
    for s in range(SOURCES):
        request = owner_ref[s]
        holder = request // share
        query = []
        for half in range(2):
            block = held(rows_ref, holder, half, pl.ds(0, QUERIES // 2))
            query.append(
                jnp.sum(jnp.where(line == request % share, block, 0.0), axis=0, keepdims=True)
            )
        spread = jnp.concatenate(
            [
                query[k % 2][:, k // 2 * KEYS : (k // 2 + 1) * KEYS] * mask
                for k in range(REPEAT)
            ],
            axis=0,
        ).astype(jnp.bfloat16)
        keys = kept_ref[s * KEEP : (s + 1) * KEEP, :KEYS]
        values = kept_ref[s * KEEP : (s + 1) * KEEP, KEYS:]
        score = scale * lax.dot_general(
            keys, spread, (((1,), (1,)), ((), ())), preferred_element_type=jnp.float32
        )
        peak = jnp.max(score, axis=0, keepdims=True)
        weight = jnp.exp(score - peak)
        total_ref[s : s + 1, :] = jnp.sum(weight, axis=0, keepdims=True)
        peak_ref[s : s + 1, :] = jnp.where(s < count_ref[0], peak, NEGATIVE)
        mixed = lax.dot_general(
            weight.astype(jnp.bfloat16),
            values,
            (((0,), (0,)), ((), ())),
            preferred_element_type=jnp.float32,
        )
        for k in range(REPEAT):
            sum_ref[s : s + 1, k * KEYS : (k + 1) * KEYS] = jnp.sum(
                mixed[k * KV_HEADS : (k + 1) * KV_HEADS] * mask, axis=0, keepdims=True
            )
    sums = sum_ref[...].astype(jnp.bfloat16)
    slots = lax.broadcasted_iota(jnp.int32, (SOURCES, HEADS), 0)
    tag = jnp.full((SOURCES, HEADS), -1, jnp.int32)
    for s in range(SOURCES):
        tag = jnp.where((slots == s) & (s < count_ref[0]), owner_ref[s], tag)
    tag = tag.astype(jnp.float32).astype(jnp.bfloat16)
    columns = pieces(peak_ref[...], 3) + pieces(total_ref[...], 3) + [tag, tag]
    columns = [column.astype(jnp.float32) for column in columns]
    columns = jnp.concatenate(columns, axis=1).astype(jnp.bfloat16)
    out_ref[:, :QUERIES] = sums
    out_ref[:, QUERIES:] = columns


def attend(page_count, page_owner, kept, rows):
    return pl.pallas_call(
        attend_kernel,
        out_shape=jax.ShapeDtypeStruct((SOURCES, QUERIES + EXTRA), jnp.bfloat16),
        in_specs=[SMEM] * 2 + [VMEM] * 2,
        out_specs=VMEM,
        scratch_shapes=[
            pltpu.VMEM((SOURCES, QUERIES), jnp.float32),
            pltpu.VMEM((SOURCES, HEADS), jnp.float32),
            pltpu.VMEM((SOURCES, HEADS), jnp.float32),
        ],
        name="attend",
    )(page_count, page_owner, kept, rows)


def spread_dot(value, chosen, contract, count, chosen_first=False):
    total = None
    for part in pieces(value, count):
        operands = (chosen, part) if chosen_first else (part, chosen)
        term = lax.dot_general(
            *operands, (contract, ((), ())), preferred_element_type=jnp.float32
        )
        total = term if total is None else total + term
    return total


def head_columns():
    head = lax.broadcasted_iota(jnp.int32, (HEADS, QUERIES), 0) * HEAD_DIM
    lane = lax.broadcasted_iota(jnp.int32, (HEADS, QUERIES), 1)
    return ((lane >= head) & (lane < head + HEAD_DIM)).astype(jnp.float32).astype(jnp.bfloat16)


def own_kernel(rows_ref, score_ref, value_ref, query_ref, pair_ref):
    scale = HEAD_DIM ** (-0.5)
    share = rows_ref.shape[1]
    piece = HEAD_DIM // 2
    for holder in range(HOLDERS):
        rows = slice(holder * share, (holder + 1) * share)
        for half in range(2):
            block = held(rows_ref, holder, half, pl.ds(0, HALF_COLUMNS))
            for k in range(2):
                at = (2 * k + half) * KEYS
                query_ref[rows, at : at + KEYS] = block[:, k * KEYS : (k + 1) * KEYS]
            pair_ref[half, rows, :] = block[:, QUERIES // 2 :]
    keys, values = [], []
    for g in range(KV_HEADS):
        for half in range(2):
            keys.append(pair_ref[half, :, g * piece : (g + 1) * piece])
            at = KEYS // 2 + g * piece
            values.append(pair_ref[half, :, at : at + piece])
    key = jnp.concatenate(keys, axis=1)
    value_ref[...] = jnp.concatenate(values, axis=1)
    product = query_ref[...] * jnp.concatenate([key] * REPEAT, axis=1)
    score_ref[...] = scale * spread_dot(product, head_columns(), ((1,), (1,)), 3)


def own_part(rows):
    requests = HOLDERS * rows.shape[1]
    return pl.pallas_call(
        own_kernel,
        out_shape=(
            jax.ShapeDtypeStruct((requests, HEADS), jnp.float32),
            jax.ShapeDtypeStruct((requests, KEYS), jnp.float32),
        ),
        in_specs=[VMEM],
        out_specs=(VMEM, VMEM),
        scratch_shapes=[
            pltpu.VMEM((requests, QUERIES), jnp.float32),
            pltpu.VMEM((2, requests, KEYS), jnp.float32),
        ],
        name="own_part",
    )(rows)


def combine_kernel(part_ref, own_ref, value_ref, out_ref):
    requests = out_ref.shape[0]
    slots = part_ref.shape[0]
    extra = part_ref[:, QUERIES:].astype(jnp.float32)
    column = [extra[:, i * HEADS : (i + 1) * HEADS] for i in range(7)]
    peaks = column[0] + column[1] + column[2]
    totals = column[3] + column[4] + column[5]
    tag = column[6][:, :1]
    row = lax.broadcasted_iota(jnp.int32, (requests, 1), 0).astype(jnp.float32)
    member = (
        tag == lax.broadcasted_iota(jnp.int32, (slots, requests), 1).astype(jnp.float32)
    ).astype(jnp.float32).astype(jnp.bfloat16)
    expand = head_columns()
    own = own_ref[...]
    tops = [own] + [jnp.full(own.shape, NEGATIVE, jnp.float32)] * 3
    for s in range(slots):
        tops[s % 4] = jnp.maximum(
            tops[s % 4], jnp.where(tag[s : s + 1] == row, peaks[s : s + 1], NEGATIVE)
        )
    top = jnp.maximum(jnp.maximum(tops[0], tops[1]), jnp.maximum(tops[2], tops[3]))
    own_weight = jnp.exp(own - top)
    weight = jnp.exp(peaks - spread_dot(top, member, ((1,), (0,)), 3, True))
    total = spread_dot(weight * totals, member, ((0,), (0,)), 3, True) + own_weight
    inverse = 1.0 / total
    weight = weight * spread_dot(inverse, member, ((1,), (0,)), 3, True)
    scaled = part_ref[:, :QUERIES].astype(jnp.float32) * spread_dot(weight, expand, ((1,), (0,)), 2)
    mixed = spread_dot(scaled, member, ((0,), (0,)), 2, True)
    own_share = spread_dot(own_weight * inverse, expand, ((1,), (0,)), 2)
    mixed = mixed + own_share * jnp.concatenate([value_ref[...]] * REPEAT, axis=1)
    mixed = mixed.astype(jnp.bfloat16)
    for h in range(HEADS):
        at = (h % REPEAT * KV_HEADS + h // REPEAT) * HEAD_DIM
        out_ref[:, h * HEAD_DIM : (h + 1) * HEAD_DIM] = mixed[:, at : at + HEAD_DIM]


def combine(parts, own, value):
    return pl.pallas_call(
        combine_kernel,
        out_shape=jax.ShapeDtypeStruct((own.shape[0], QUERIES), jnp.bfloat16),
        in_specs=[VMEM] * 3,
        out_specs=VMEM,
        compiler_params=pltpu.CompilerParams(vmem_limit_bytes=48 * 1024 * 1024),
        name="combine",
    )(parts, own, value)


def per_device(
    tokens, norm_gain, w_query, w_keyvalue, cache, page_count, page_owner, keep_rows, dest_slot
):
    holder = lax.axis_index("page")
    half = lax.axis_index("tensor") % 2
    share = tokens.shape[0] // HOLDERS

    def normalise(rows):
        widened = rows.astype(jnp.float32)
        return (
            widened
            * lax.rsqrt(jnp.mean(widened * widened, axis=-1, keepdims=True) + EPSILON)
            * norm_gain
        ).astype(jnp.bfloat16)

    page_count = page_count.reshape(1)
    page_owner = page_owner.reshape(SOURCES)
    near_pages, far_pages, kept = select_rows(page_count, dest_slot.reshape(SOURCES), keep_rows, cache)

    mine = normalise(lax.dynamic_slice_in_dim(tokens, holder * share, share, 0))
    across = lax.ppermute(mine, ("page", "tensor"), OTHER_HALF)
    across, far_pages = lax.optimization_barrier((across, far_pages))
    relayed = lax.ppermute(far_pages, "page", OTHER_QUAD)
    both = jnp.where(
        half == 0,
        jnp.concatenate([mine, across], axis=0),
        jnp.concatenate([across, mine], axis=0),
    )
    rows = lax.all_to_all(
        jnp.broadcast_to(both[None], (PLANE,) + both.shape),
        "tensor",
        0,
        0,
        axis_index_groups=PLANE_GROUPS,
        tiled=True,
    ).reshape(PLANE * both.shape[0], -1)
    projected = project(rows, w_query, w_keyvalue).reshape(PLANE, both.shape[0], -1)
    back = lax.all_to_all(
        projected, "tensor", 0, 0, axis_index_groups=PLANE_GROUPS, tiled=True
    )
    halves = pick(back)
    quarter = lax.all_to_all(
        halves, ("page", "tensor"), 0, 0, axis_index_groups=FOUR_GROUPS, tiled=True
    )
    rows = lax.all_gather(quarter, "page", axis=0, axis_index_groups=QUAD_GROUPS, tiled=True)
    rows, relayed = lax.optimization_barrier((rows, relayed))
    pages = lax.all_to_all(
        join(near_pages, relayed), "page", 0, 0, axis_index_groups=QUAD_GROUPS, tiled=True
    )
    part = attend(page_count, page_owner, kept, rows)
    far = lax.ppermute(part, "page", OTHER_QUAD)
    own, value = own_part(rows)
    far, own, value = lax.optimization_barrier((far, own, value))
    parts = lax.all_gather(
        jnp.concatenate([part, far], axis=0),
        "page",
        axis=0,
        axis_index_groups=QUAD_GROUPS,
        tiled=True,
    )
    arrived = jnp.swapaxes(pages, 0, 1).reshape((HOLDERS, 1) + pages.shape[2:])
    return combine(parts, own, value), arrived


def solution(mesh):
    return jax.shard_map(
        per_device,
        mesh=mesh,
        in_specs=(
            P("tensor", None),
            P(),
            P(None, "tensor"),
            P(None, "tensor"),
            P("page", "tensor", None, None),
            P("page", "tensor"),
            P("page", "tensor"),
            P("page", "tensor", None),
            P("page", "tensor"),
        ),
        out_specs=(P("tensor", None), P("page", "tensor", None, None)),
        check_vma=False,
    )
```

```python
import jax
import jax.numpy as jnp
from jax import lax
from jax.experimental import pallas as pl
from jax.experimental.pallas import tpu as pltpu
from jax.sharding import PartitionSpec as P

HEADS = 32
KV_HEADS = 8
REPEAT = HEADS // KV_HEADS
HEAD_DIM = 80
KEYS = KV_HEADS * HEAD_DIM
QUERIES = HEADS * HEAD_DIM
EPSILON = 1e-05
NEGATIVE = -1e30

PLANE = 16
HOLDERS = 16
SOURCES = 8
KEEP = 32
EXTRA = 256

CHIPS = 8
PLANE_GROUPS = [[2 * i + half for i in range(PLANE)] for half in range(2)]
OTHER_HALF = [
    (p * 2 * PLANE + t, (p ^ 8) * 2 * PLANE + (t ^ 1)) for p in range(HOLDERS) for t in range(2 * PLANE)
]

FOUR_GROUPS = [
    [
        (2 * (4 * quad + z) + core) * 2 * PLANE + 2 * xy + half
        for half in range(2)
        for quad in range(2)
    ]
    for xy in range(PLANE)
    for z in range(CHIPS // 2)
    for core in range(2)
]
QUAD_GROUPS = [[CHIPS * quad + i for i in range(CHIPS)] for quad in range(2)]
OTHER_QUAD = [(i, i ^ CHIPS) for i in range(HOLDERS)]
HALF_COLUMNS = (QUERIES + 2 * KEYS) // 2
STEP = 4

VMEM = pl.BlockSpec(memory_space=pltpu.VMEM)
SMEM = pl.BlockSpec(memory_space=pltpu.SMEM)


def select_kernel(count_ref, dest_ref, keep_ref, page_ref, out_ref, kept_ref):
    step = pl.program_id(0)

    @pl.when(step == 0)
    def _():
        out_ref[...] = jnp.zeros_like(out_ref)

    rows = page_ref.shape[1]
    for i in range(STEP):
        slot = step * STEP + i
        picks = jnp.broadcast_to(keep_ref[i], (rows, KEEP))
        chosen = (picks == lax.broadcasted_iota(jnp.int32, (rows, KEEP), 0)).astype(jnp.float32)
        kept = jnp.dot(
            chosen.T.astype(jnp.bfloat16), page_ref[i], preferred_element_type=jnp.float32
        ).astype(jnp.bfloat16)
        kept_ref[i * KEEP : (i + 1) * KEEP] = kept

        @pl.when(slot < count_ref[0])
        def _():
            out_ref[dest_ref[slot]] = kept


def select_rows(page_count, dest_slot, keep_rows, cache):
    sources, _, rows, width = cache.shape
    return pl.pallas_call(
        select_kernel,
        out_shape=(
            jax.ShapeDtypeStruct((HOLDERS, KEEP, width), cache.dtype),
            jax.ShapeDtypeStruct((sources * KEEP, width), cache.dtype),
        ),
        grid_spec=pltpu.PrefetchScalarGridSpec(
            num_scalar_prefetch=2,
            grid=(sources // STEP,),
            in_specs=[
                pl.BlockSpec((STEP, 1, KEEP), lambda s, *_: (s, 0, 0)),
                pl.BlockSpec((STEP, rows, width), lambda s, *_: (s, 0, 0)),
            ],
            out_specs=[
                pl.BlockSpec((HOLDERS, KEEP, width), lambda s, *_: (0, 0, 0)),
                pl.BlockSpec((STEP * KEEP, width), lambda s, *_: (s, 0)),
            ],
        ),
        name="select_rows",
    )(page_count, dest_slot, keep_rows, cache.reshape(sources, rows, width))


def project_kernel(rows_ref, query_ref, pair_ref, out_ref):
    rows = rows_ref[...]
    for ref, low, high in ((query_ref, 0, HEAD_DIM), (pair_ref, HEAD_DIM, HEAD_DIM * 3 // 2)):
        out_ref[:, low:high] = lax.dot_general(
            rows, ref[...], (((1,), (1,)), ((), ())), preferred_element_type=jnp.float32
        ).astype(jnp.bfloat16)


def project(rows, w_query, w_keyvalue):
    return pl.pallas_call(
        project_kernel,
        out_shape=jax.ShapeDtypeStruct((rows.shape[0], HEAD_DIM * 3 // 2), jnp.bfloat16),
        in_specs=[VMEM] * 3,
        out_specs=VMEM,
        name="project",
    )(rows, w_query.T, w_keyvalue.T)


def pick_kernel(plane_ref, all_ref, out_ref, rows_ref):
    half = HEAD_DIM // 2
    for i in range(PLANE):
        block = all_ref[i].astype(jnp.float32)
        at = (i % 2 * KV_HEADS + i // 2) * HEAD_DIM
        rows_ref[:, at : at + HEAD_DIM] = block[:, :HEAD_DIM]
        at = QUERIES // 2 + i * half
        rows_ref[:, at : at + half] = block[:, HEAD_DIM:]
    share = out_ref.shape[1]
    for h in range(2):
        piece = rows_ref[h * share : (h + 1) * share].astype(jnp.bfloat16)
        for quad in range(2):
            out_ref[2 * h + quad] = piece


def pick(plane, everyone):
    count, rows, width = everyone.shape
    both = rows // PLANE
    piece = jax.ShapeDtypeStruct((4, both // 2, HALF_COLUMNS), everyone.dtype)
    return pl.pallas_call(
        pick_kernel,
        out_shape=piece,
        grid_spec=pltpu.PrefetchScalarGridSpec(
            num_scalar_prefetch=1,
            grid=(1,),
            in_specs=[pl.BlockSpec((count, both, width), lambda i, plane: (0, plane[0], 0))],
            out_specs=pl.BlockSpec(piece.shape, lambda i, *_: (0, 0, 0)),
            scratch_shapes=[pltpu.VMEM((both, HALF_COLUMNS), jnp.float32)],
        ),
        name="pick",
    )(plane, everyone)


def held(rows_ref, holder, half, columns):
    quad, inside = holder // CHIPS, holder % CHIPS
    same = lax.axis_index("tensor") % 2 == half
    spot = inside * 4 + 2 * half + jnp.where(same, quad, 1 - quad)
    return rows_ref[spot, :, columns].astype(jnp.float32)


def pieces(value, count):
    parts = []
    for _ in range(count):
        part = value.astype(jnp.bfloat16)
        parts.append(part)
        value = value - part.astype(jnp.float32)
    return parts


def attend_kernel(
    count_ref, owner_ref, kept_ref, rows_ref, out_ref, sum_ref, peak_ref, total_ref
):
    scale = HEAD_DIM ** (-0.5)
    share = rows_ref.shape[1]
    line = lax.broadcasted_iota(jnp.int32, (share, QUERIES // 2), 0)
    head = lax.broadcasted_iota(jnp.int32, (KV_HEADS, KEYS), 0) * HEAD_DIM
    lane = lax.broadcasted_iota(jnp.int32, (KV_HEADS, KEYS), 1)
    mask = ((lane >= head) & (lane < head + HEAD_DIM)).astype(jnp.float32)
    for s in range(SOURCES):
        request = owner_ref[s]
        holder = request // share
        query = []
        for half in range(2):
            block = held(rows_ref, holder, half, pl.ds(0, QUERIES // 2))
            query.append(
                jnp.sum(jnp.where(line == request % share, block, 0.0), axis=0, keepdims=True)
            )
        spread = jnp.concatenate(
            [
                query[k % 2][:, k // 2 * KEYS : (k // 2 + 1) * KEYS] * mask
                for k in range(REPEAT)
            ],
            axis=0,
        ).astype(jnp.bfloat16)
        keys = kept_ref[s * KEEP : (s + 1) * KEEP, :KEYS]
        values = kept_ref[s * KEEP : (s + 1) * KEEP, KEYS:]
        score = scale * lax.dot_general(
            keys, spread, (((1,), (1,)), ((), ())), preferred_element_type=jnp.float32
        )
        peak = jnp.max(score, axis=0, keepdims=True)
        weight = jnp.exp(score - peak)
        total_ref[s : s + 1, :] = jnp.sum(weight, axis=0, keepdims=True)
        peak_ref[s : s + 1, :] = jnp.where(s < count_ref[0], peak, NEGATIVE)
        mixed = lax.dot_general(
            weight.astype(jnp.bfloat16),
            values,
            (((0,), (0,)), ((), ())),
            preferred_element_type=jnp.float32,
        )
        for k in range(REPEAT):
            sum_ref[s : s + 1, k * KEYS : (k + 1) * KEYS] = jnp.sum(
                mixed[k * KV_HEADS : (k + 1) * KV_HEADS] * mask, axis=0, keepdims=True
            )
    sums = sum_ref[...].astype(jnp.bfloat16)
    slots = lax.broadcasted_iota(jnp.int32, (SOURCES, HEADS), 0)
    tag = jnp.full((SOURCES, HEADS), -1, jnp.int32)
    for s in range(SOURCES):
        tag = jnp.where((slots == s) & (s < count_ref[0]), owner_ref[s], tag)
    tag = tag.astype(jnp.float32).astype(jnp.bfloat16)
    columns = pieces(peak_ref[...], 3) + pieces(total_ref[...], 3) + [tag, tag]
    columns = [column.astype(jnp.float32) for column in columns]
    columns = jnp.concatenate(columns, axis=1).astype(jnp.bfloat16)
    out_ref[:, :QUERIES] = sums
    out_ref[:, QUERIES:] = columns


def attend(page_count, page_owner, kept, rows):
    return pl.pallas_call(
        attend_kernel,
        out_shape=jax.ShapeDtypeStruct((SOURCES, QUERIES + EXTRA), jnp.bfloat16),
        in_specs=[SMEM] * 2 + [VMEM] * 2,
        out_specs=VMEM,
        scratch_shapes=[
            pltpu.VMEM((SOURCES, QUERIES), jnp.float32),
            pltpu.VMEM((SOURCES, HEADS), jnp.float32),
            pltpu.VMEM((SOURCES, HEADS), jnp.float32),
        ],
        name="attend",
    )(page_count, page_owner, kept, rows)


def spread_dot(value, chosen, contract, count, chosen_first=False):
    total = None
    for part in pieces(value, count):
        operands = (chosen, part) if chosen_first else (part, chosen)
        term = lax.dot_general(
            *operands, (contract, ((), ())), preferred_element_type=jnp.float32
        )
        total = term if total is None else total + term
    return total


def head_columns():
    head = lax.broadcasted_iota(jnp.int32, (HEADS, QUERIES), 0) * HEAD_DIM
    lane = lax.broadcasted_iota(jnp.int32, (HEADS, QUERIES), 1)
    return ((lane >= head) & (lane < head + HEAD_DIM)).astype(jnp.float32).astype(jnp.bfloat16)


def own_kernel(rows_ref, own_ref, query_ref, pair_ref):
    scale = HEAD_DIM ** (-0.5)
    share = rows_ref.shape[1]
    piece = HEAD_DIM // 2
    for holder in range(HOLDERS):
        rows = slice(holder * share, (holder + 1) * share)
        for half in range(2):
            block = held(rows_ref, holder, half, pl.ds(0, HALF_COLUMNS))
            for k in range(2):
                at = (2 * k + half) * KEYS
                query_ref[rows, at : at + KEYS] = block[:, k * KEYS : (k + 1) * KEYS]
            pair_ref[half, rows, :] = block[:, QUERIES // 2 :]
    keys, values = [], []
    for g in range(KV_HEADS):
        for half in range(2):
            keys.append(pair_ref[half, :, g * piece : (g + 1) * piece])
            at = KEYS // 2 + g * piece
            values.append(pair_ref[half, :, at : at + piece])
    key = jnp.concatenate(keys, axis=1)
    own_ref[:, :KEYS] = jnp.concatenate(values, axis=1)
    product = query_ref[...] * jnp.concatenate([key] * REPEAT, axis=1)
    own_ref[:, KEYS:] = jnp.concatenate(
        [scale * spread_dot(product, head_columns(), ((1,), (1,)), 3)] * 4, axis=1
    )


def own_part(rows):
    requests = HOLDERS * rows.shape[1]
    return pl.pallas_call(
        own_kernel,
        out_shape=jax.ShapeDtypeStruct((requests, KEYS + 4 * HEADS), jnp.float32),
        in_specs=[VMEM],
        out_specs=VMEM,
        scratch_shapes=[
            pltpu.VMEM((requests, QUERIES), jnp.float32),
            pltpu.VMEM((2, requests, KEYS), jnp.float32),
        ],
        name="own_part",
    )(rows)


def combine_kernel(part_ref, own_ref, out_ref):
    requests = out_ref.shape[0]
    slots = part_ref.shape[0]
    extra = part_ref[:, QUERIES:].astype(jnp.float32)
    column = [extra[:, i * HEADS : (i + 1) * HEADS] for i in range(7)]
    peaks = column[0] + column[1] + column[2]
    totals = column[3] + column[4] + column[5]
    tag = column[6][:, :1]
    member = (
        tag == lax.broadcasted_iota(jnp.int32, (slots, requests), 1).astype(jnp.float32)
    ).astype(jnp.float32).astype(jnp.bfloat16)
    expand = head_columns()
    own = own_ref[:, KEYS : KEYS + HEADS]
    quarter = slots // 4
    beside = [
        jnp.concatenate([block[i * quarter : (i + 1) * quarter] for i in range(4)], axis=1)
        for block in (peaks, column[6])
    ]
    row = lax.broadcasted_iota(jnp.int32, (requests, 4 * HEADS), 0).astype(jnp.float32)
    tops = [jnp.full(row.shape, NEGATIVE, jnp.float32)] * 2
    for s in range(quarter):
        tops[s % 2] = jnp.maximum(
            tops[s % 2],
            jnp.where(beside[1][s : s + 1] == row, beside[0][s : s + 1], NEGATIVE),
        )
    wide = jnp.maximum(tops[0], tops[1])
    top = own
    for i in range(4):
        top = jnp.maximum(top, wide[:, i * HEADS : (i + 1) * HEADS])
    own_weight = jnp.exp(own - top)
    weight = jnp.exp(peaks - spread_dot(top, member, ((1,), (0,)), 3, True))
    total = spread_dot(weight * totals, member, ((0,), (0,)), 3, True) + own_weight
    inverse = 1.0 / total
    weight = weight * spread_dot(inverse, member, ((1,), (0,)), 3, True)
    scaled = part_ref[:, :QUERIES].astype(jnp.float32) * spread_dot(weight, expand, ((1,), (0,)), 2)
    mixed = spread_dot(scaled, member, ((0,), (0,)), 2, True)
    own_share = spread_dot(own_weight * inverse, expand, ((1,), (0,)), 2)
    mixed = mixed + own_share * jnp.concatenate([own_ref[:, :KEYS]] * REPEAT, axis=1)
    mixed = mixed.astype(jnp.bfloat16)
    for h in range(HEADS):
        at = (h % REPEAT * KV_HEADS + h // REPEAT) * HEAD_DIM
        out_ref[:, h * HEAD_DIM : (h + 1) * HEAD_DIM] = mixed[:, at : at + HEAD_DIM]


def combine(parts, own):
    return pl.pallas_call(
        combine_kernel,
        out_shape=jax.ShapeDtypeStruct((own.shape[0], QUERIES), jnp.bfloat16),
        in_specs=[VMEM] * 2,
        out_specs=VMEM,
        compiler_params=pltpu.CompilerParams(vmem_limit_bytes=48 * 1024 * 1024),
        name="combine",
    )(parts, own)


def normalise_kernel(holder_ref, tokens_ref, gain_ref, out_ref, rows_ref):
    share = out_ref.shape[0]
    widened = tokens_ref[...].astype(jnp.float32)
    mean = jnp.mean(widened * widened, axis=-1, keepdims=True)
    normed = widened * lax.rsqrt(mean + EPSILON) * gain_ref[...]
    for i in range(rows_ref.shape[0]):
        rows_ref[i] = normed[i * share : (i + 1) * share]
    out_ref[...] = rows_ref[holder_ref[0] % rows_ref.shape[0]].astype(jnp.bfloat16)


def normalise(holder, tokens, norm_gain):
    requests, width = tokens.shape
    share = requests // HOLDERS
    shares = 4
    return pl.pallas_call(
        normalise_kernel,
        out_shape=jax.ShapeDtypeStruct((share, width), jnp.bfloat16),
        grid_spec=pltpu.PrefetchScalarGridSpec(
            num_scalar_prefetch=1,
            grid=(1,),
            in_specs=[
                pl.BlockSpec((shares * share, width), lambda i, holder: (holder[0] // shares, 0)),
                pl.BlockSpec((1, width), lambda i, *_: (0, 0)),
            ],
            out_specs=pl.BlockSpec((share, width), lambda i, *_: (0, 0)),
            scratch_shapes=[pltpu.VMEM((shares, share, width), jnp.float32)],
        ),
        name="normalise",
    )(holder.reshape(1), tokens, norm_gain.reshape(1, width))


def per_device(
    tokens, norm_gain, w_query, w_keyvalue, cache, page_count, page_owner, keep_rows, dest_slot
):
    holder = lax.axis_index("page")
    group = lax.axis_index("tensor")
    half = group % 2
    page_count = page_count.reshape(1)
    page_owner = page_owner.reshape(SOURCES)
    compact, kept = select_rows(page_count, dest_slot.reshape(SOURCES), keep_rows, cache)

    mine = normalise(holder, tokens, norm_gain)
    across = lax.ppermute(mine, ("page", "tensor"), OTHER_HALF)
    across, compact = lax.optimization_barrier((across, compact))
    arrived = lax.all_to_all(compact, "page", 0, 0, tiled=True)

    both = jnp.where(
        half == 0,
        jnp.concatenate([mine, across], axis=0),
        jnp.concatenate([across, mine], axis=0),
    )
    rows = lax.all_gather(
        both, "tensor", axis=0, axis_index_groups=PLANE_GROUPS, tiled=True
    )
    projected = project(rows, w_query, w_keyvalue)
    everyone = lax.all_gather(
        projected, "tensor", axis=0, axis_index_groups=PLANE_GROUPS, tiled=False
    )
    halves = pick((group // 2).reshape(1), everyone)
    halves, arrived = lax.optimization_barrier((halves, arrived))
    quarter = lax.all_to_all(
        halves, ("page", "tensor"), 0, 0, axis_index_groups=FOUR_GROUPS, tiled=True
    )
    rows = lax.all_gather(quarter, "page", axis=0, axis_index_groups=QUAD_GROUPS, tiled=True)
    part = attend(page_count, page_owner, kept, rows)
    far = lax.ppermute(part, "page", OTHER_QUAD)
    own = own_part(rows)
    far, own = lax.optimization_barrier((far, own))
    parts = lax.all_gather(
        jnp.concatenate([part, far], axis=0),
        "page",
        axis=0,
        axis_index_groups=QUAD_GROUPS,
        tiled=True,
    )
    return combine(parts, own), arrived[:, None]


def solution(mesh):
    return jax.shard_map(
        per_device,
        mesh=mesh,
        in_specs=(
            P("tensor", None),
            P(),
            P(None, "tensor"),
            P(None, "tensor"),
            P("page", "tensor", None, None),
            P("page", "tensor"),
            P("page", "tensor"),
            P("page", "tensor", None),
            P("page", "tensor"),
        ),
        out_specs=(P("tensor", None), P("page", "tensor", None, None)),
        check_vma=False,
    )
```

```python
import jax
import jax.numpy as jnp
from jax import lax
from jax.experimental import pallas as pl
from jax.experimental.pallas import tpu as pltpu
from jax.sharding import PartitionSpec as P

HEADS = 32
KV_HEADS = 8
REPEAT = HEADS // KV_HEADS
HEAD_DIM = 80
KEYS = KV_HEADS * HEAD_DIM
QUERIES = HEADS * HEAD_DIM
EPSILON = 1e-05
NEGATIVE = -1e30

PLANE = 16
HOLDERS = 16
SOURCES = 8
KEEP = 32
EXTRA = 256

CHIPS = 8
PLANE_GROUPS = [[2 * i + half for i in range(PLANE)] for half in range(2)]
OTHER_HALF = [
    (p * 2 * PLANE + t, (p ^ 8) * 2 * PLANE + (t ^ 1)) for p in range(HOLDERS) for t in range(2 * PLANE)
]

FOUR_GROUPS = [
    [
        (2 * (4 * quad + z) + core) * 2 * PLANE + 2 * xy + half
        for half in range(2)
        for quad in range(2)
    ]
    for xy in range(PLANE)
    for z in range(CHIPS // 2)
    for core in range(2)
]
QUAD_GROUPS = [[CHIPS * quad + i for i in range(CHIPS)] for quad in range(2)]
OTHER_CORE = [(i, i ^ 1) for i in range(HOLDERS)]
OTHER_CHIP = [[(i, i ^ (2 * d)) for i in range(HOLDERS)] for d in range(CHIPS)]
OTHER_QUAD = [(i, i ^ CHIPS) for i in range(HOLDERS)]
HALF_COLUMNS = (QUERIES + 2 * KEYS) // 2
STEP = 4

VMEM = pl.BlockSpec(memory_space=pltpu.VMEM)
SMEM = pl.BlockSpec(memory_space=pltpu.SMEM)


def select_kernel(count_ref, dest_ref, keep_ref, page_ref, *refs):
    out_refs, kept_ref = refs[:CHIPS], refs[CHIPS]
    grid_step = pl.program_id(0)
    holder = lax.axis_index("page")

    @pl.when(grid_step == 0)
    def _():
        for ref in out_refs:
            ref[...] = jnp.zeros_like(ref)

    rows = page_ref.shape[1]
    for i in range(STEP):
        slot = grid_step * STEP + i
        picks = jnp.broadcast_to(keep_ref[i], (rows, KEEP))
        chosen = (picks == lax.broadcasted_iota(jnp.int32, (rows, KEEP), 0)).astype(jnp.float32)
        kept = jnp.dot(
            chosen.T.astype(jnp.bfloat16), page_ref[i], preferred_element_type=jnp.float32
        ).astype(jnp.bfloat16)
        kept_ref[i * KEEP : (i + 1) * KEEP] = kept
        target = dest_ref[slot] ^ holder
        live = slot < count_ref[0]
        for d in range(CHIPS):

            @pl.when(live & (target // 2 == d))
            def _():
                out_refs[d][target % 2] = kept_ref[i * KEEP : (i + 1) * KEEP]


def select_rows(page_count, dest_slot, keep_rows, cache):
    sources, _, rows, width = cache.shape
    block = jax.ShapeDtypeStruct((2, KEEP, width), cache.dtype)
    results = pl.pallas_call(
        select_kernel,
        out_shape=[block] * CHIPS + [jax.ShapeDtypeStruct((sources * KEEP, width), cache.dtype)],
        grid_spec=pltpu.PrefetchScalarGridSpec(
            num_scalar_prefetch=2,
            grid=(sources // STEP,),
            in_specs=[
                pl.BlockSpec((STEP, 1, KEEP), lambda s, *_: (s, 0, 0)),
                pl.BlockSpec((STEP, rows, width), lambda s, *_: (s, 0, 0)),
            ],
            out_specs=[pl.BlockSpec(block.shape, lambda s, *_: (0, 0, 0))] * CHIPS
            + [pl.BlockSpec((STEP * KEEP, width), lambda s, *_: (s, 0))],
        ),
        name="select_rows",
    )(page_count, dest_slot, keep_rows, cache.reshape(sources, rows, width))
    return results[:CHIPS], results[CHIPS]


def pack_kernel(*refs):
    for d in range(CHIPS):
        refs[CHIPS][d] = refs[d][1]


def pack(got):
    return pl.pallas_call(
        pack_kernel,
        out_shape=jax.ShapeDtypeStruct((CHIPS,) + got[0].shape[1:], got[0].dtype),
        in_specs=[VMEM] * CHIPS,
        out_specs=VMEM,
        name="pack",
    )(*got)


def place_kernel(*refs):
    got_refs, cross_ref, out_ref = refs[:CHIPS], refs[CHIPS], refs[CHIPS + 1]
    holder = lax.axis_index("page")
    for d in range(CHIPS):
        out_ref[holder ^ (2 * d)] = got_refs[d][0]
        out_ref[holder ^ (2 * d + 1)] = cross_ref[d]


def place_pages(got, cross):
    return pl.pallas_call(
        place_kernel,
        out_shape=jax.ShapeDtypeStruct((HOLDERS,) + cross.shape[1:], cross.dtype),
        in_specs=[VMEM] * (CHIPS + 1),
        out_specs=VMEM,
        name="place_pages",
    )(*got, cross)


def project_kernel(rows_ref, query_ref, pair_ref, out_ref):
    rows = rows_ref[...]
    for ref, low, high in ((query_ref, 0, HEAD_DIM), (pair_ref, HEAD_DIM, HEAD_DIM * 3 // 2)):
        out_ref[:, low:high] = lax.dot_general(
            rows, ref[...], (((1,), (1,)), ((), ())), preferred_element_type=jnp.float32
        ).astype(jnp.bfloat16)


def project(rows, w_query, w_keyvalue):
    return pl.pallas_call(
        project_kernel,
        out_shape=jax.ShapeDtypeStruct((rows.shape[0], HEAD_DIM * 3 // 2), jnp.bfloat16),
        in_specs=[VMEM] * 3,
        out_specs=VMEM,
        name="project",
    )(rows, w_query.T, w_keyvalue.T)


def pick_kernel(all_ref, out_ref, rows_ref):
    half = HEAD_DIM // 2
    for i in range(PLANE):
        block = all_ref[i].astype(jnp.float32)
        at = (i % 2 * KV_HEADS + i // 2) * HEAD_DIM
        rows_ref[:, at : at + HEAD_DIM] = block[:, :HEAD_DIM]
        at = QUERIES // 2 + i * half
        rows_ref[:, at : at + half] = block[:, HEAD_DIM:]
    share = out_ref.shape[1]
    for h in range(2):
        piece = rows_ref[h * share : (h + 1) * share].astype(jnp.bfloat16)
        for quad in range(2):
            out_ref[2 * h + quad] = piece


def pick(block):
    count, both, _ = block.shape
    return pl.pallas_call(
        pick_kernel,
        out_shape=jax.ShapeDtypeStruct((4, both // 2, HALF_COLUMNS), block.dtype),
        in_specs=[VMEM],
        out_specs=VMEM,
        scratch_shapes=[pltpu.VMEM((both, HALF_COLUMNS), jnp.float32)],
        name="pick",
    )(block)


def held(rows_ref, holder, half, columns):
    quad, inside = holder // CHIPS, holder % CHIPS
    same = lax.axis_index("tensor") % 2 == half
    spot = inside * 4 + 2 * half + jnp.where(same, quad, 1 - quad)
    return rows_ref[spot, :, columns].astype(jnp.float32)


def pieces(value, count):
    parts = []
    for _ in range(count):
        part = value.astype(jnp.bfloat16)
        parts.append(part)
        value = value - part.astype(jnp.float32)
    return parts


def attend_kernel(
    count_ref, owner_ref, kept_ref, rows_ref, out_ref, sum_ref, peak_ref, total_ref
):
    scale = HEAD_DIM ** (-0.5)
    share = rows_ref.shape[1]
    line = lax.broadcasted_iota(jnp.int32, (share, QUERIES // 2), 0)
    head = lax.broadcasted_iota(jnp.int32, (KV_HEADS, KEYS), 0) * HEAD_DIM
    lane = lax.broadcasted_iota(jnp.int32, (KV_HEADS, KEYS), 1)
    mask = ((lane >= head) & (lane < head + HEAD_DIM)).astype(jnp.float32)
    for s in range(SOURCES):
        request = owner_ref[s]
        holder = request // share
        query = []
        for half in range(2):
            block = held(rows_ref, holder, half, pl.ds(0, QUERIES // 2))
            query.append(
                jnp.sum(jnp.where(line == request % share, block, 0.0), axis=0, keepdims=True)
            )
        spread = jnp.concatenate(
            [
                query[k % 2][:, k // 2 * KEYS : (k // 2 + 1) * KEYS] * mask
                for k in range(REPEAT)
            ],
            axis=0,
        ).astype(jnp.bfloat16)
        keys = kept_ref[s * KEEP : (s + 1) * KEEP, :KEYS]
        values = kept_ref[s * KEEP : (s + 1) * KEEP, KEYS:]
        score = scale * lax.dot_general(
            keys, spread, (((1,), (1,)), ((), ())), preferred_element_type=jnp.float32
        )
        peak = jnp.max(score, axis=0, keepdims=True)
        weight = jnp.exp(score - peak)
        total_ref[s : s + 1, :] = jnp.sum(weight, axis=0, keepdims=True)
        peak_ref[s : s + 1, :] = jnp.where(s < count_ref[0], peak, NEGATIVE)
        mixed = lax.dot_general(
            weight.astype(jnp.bfloat16),
            values,
            (((0,), (0,)), ((), ())),
            preferred_element_type=jnp.float32,
        )
        for k in range(REPEAT):
            sum_ref[s : s + 1, k * KEYS : (k + 1) * KEYS] = jnp.sum(
                mixed[k * KV_HEADS : (k + 1) * KV_HEADS] * mask, axis=0, keepdims=True
            )
    sums = sum_ref[...].astype(jnp.bfloat16)
    slots = lax.broadcasted_iota(jnp.int32, (SOURCES, HEADS), 0)
    tag = jnp.full((SOURCES, HEADS), -1, jnp.int32)
    for s in range(SOURCES):
        tag = jnp.where((slots == s) & (s < count_ref[0]), owner_ref[s], tag)
    tag = tag.astype(jnp.float32).astype(jnp.bfloat16)
    columns = pieces(peak_ref[...], 3) + pieces(total_ref[...], 3) + [tag, tag]
    columns = [column.astype(jnp.float32) for column in columns]
    columns = jnp.concatenate(columns, axis=1).astype(jnp.bfloat16)
    out_ref[:, :QUERIES] = sums
    out_ref[:, QUERIES:] = columns


def attend(page_count, page_owner, kept, rows):
    return pl.pallas_call(
        attend_kernel,
        out_shape=jax.ShapeDtypeStruct((SOURCES, QUERIES + EXTRA), jnp.bfloat16),
        in_specs=[SMEM] * 2 + [VMEM] * 2,
        out_specs=VMEM,
        scratch_shapes=[
            pltpu.VMEM((SOURCES, QUERIES), jnp.float32),
            pltpu.VMEM((SOURCES, HEADS), jnp.float32),
            pltpu.VMEM((SOURCES, HEADS), jnp.float32),
        ],
        name="attend",
    )(page_count, page_owner, kept, rows)


def spread_dot(value, chosen, contract, count, chosen_first=False):
    total = None
    for part in pieces(value, count):
        operands = (chosen, part) if chosen_first else (part, chosen)
        term = lax.dot_general(
            *operands, (contract, ((), ())), preferred_element_type=jnp.float32
        )
        total = term if total is None else total + term
    return total


def head_columns():
    head = lax.broadcasted_iota(jnp.int32, (HEADS, QUERIES), 0) * HEAD_DIM
    lane = lax.broadcasted_iota(jnp.int32, (HEADS, QUERIES), 1)
    return ((lane >= head) & (lane < head + HEAD_DIM)).astype(jnp.float32).astype(jnp.bfloat16)


def own_kernel(rows_ref, own_ref, query_ref, pair_ref):
    scale = HEAD_DIM ** (-0.5)
    share = rows_ref.shape[1]
    piece = HEAD_DIM // 2
    for holder in range(HOLDERS):
        rows = slice(holder * share, (holder + 1) * share)
        for half in range(2):
            block = held(rows_ref, holder, half, pl.ds(0, HALF_COLUMNS))
            for k in range(2):
                at = (2 * k + half) * KEYS
                query_ref[rows, at : at + KEYS] = block[:, k * KEYS : (k + 1) * KEYS]
            pair_ref[half, rows, :] = block[:, QUERIES // 2 :]
    keys, values = [], []
    for g in range(KV_HEADS):
        for half in range(2):
            keys.append(pair_ref[half, :, g * piece : (g + 1) * piece])
            at = KEYS // 2 + g * piece
            values.append(pair_ref[half, :, at : at + piece])
    key = jnp.concatenate(keys, axis=1)
    own_ref[:, :KEYS] = jnp.concatenate(values, axis=1)
    product = query_ref[...] * jnp.concatenate([key] * REPEAT, axis=1)
    own_ref[:, KEYS:] = jnp.concatenate(
        [scale * spread_dot(product, head_columns(), ((1,), (1,)), 3)] * 4, axis=1
    )


def own_part(rows):
    requests = HOLDERS * rows.shape[1]
    return pl.pallas_call(
        own_kernel,
        out_shape=jax.ShapeDtypeStruct((requests, KEYS + 4 * HEADS), jnp.float32),
        in_specs=[VMEM],
        out_specs=VMEM,
        scratch_shapes=[
            pltpu.VMEM((requests, QUERIES), jnp.float32),
            pltpu.VMEM((2, requests, KEYS), jnp.float32),
        ],
        name="own_part",
    )(rows)


def combine_kernel(part_ref, own_ref, out_ref):
    requests = out_ref.shape[0]
    slots = part_ref.shape[0]
    extra = part_ref[:, QUERIES:].astype(jnp.float32)
    column = [extra[:, i * HEADS : (i + 1) * HEADS] for i in range(7)]
    peaks = column[0] + column[1] + column[2]
    totals = column[3] + column[4] + column[5]
    tag = column[6][:, :1]
    member = (
        tag == lax.broadcasted_iota(jnp.int32, (slots, requests), 1).astype(jnp.float32)
    ).astype(jnp.float32).astype(jnp.bfloat16)
    expand = head_columns()
    own = own_ref[:, KEYS : KEYS + HEADS]
    quarter = slots // 4
    beside = [
        jnp.concatenate([block[i * quarter : (i + 1) * quarter] for i in range(4)], axis=1)
        for block in (peaks, column[6])
    ]
    row = lax.broadcasted_iota(jnp.int32, (requests, 4 * HEADS), 0).astype(jnp.float32)
    tops = [jnp.full(row.shape, NEGATIVE, jnp.float32)] * 2
    for s in range(quarter):
        tops[s % 2] = jnp.maximum(
            tops[s % 2],
            jnp.where(beside[1][s : s + 1] == row, beside[0][s : s + 1], NEGATIVE),
        )
    wide = jnp.maximum(tops[0], tops[1])
    top = own
    for i in range(4):
        top = jnp.maximum(top, wide[:, i * HEADS : (i + 1) * HEADS])
    own_weight = jnp.exp(own - top)
    weight = jnp.exp(peaks - spread_dot(top, member, ((1,), (0,)), 3, True))
    total = spread_dot(weight * totals, member, ((0,), (0,)), 3, True) + own_weight
    inverse = 1.0 / total
    weight = weight * spread_dot(inverse, member, ((1,), (0,)), 3, True)
    scaled = part_ref[:, :QUERIES].astype(jnp.float32) * spread_dot(weight, expand, ((1,), (0,)), 2)
    mixed = spread_dot(scaled, member, ((0,), (0,)), 2, True)
    own_share = spread_dot(own_weight * inverse, expand, ((1,), (0,)), 2)
    mixed = mixed + own_share * jnp.concatenate([own_ref[:, :KEYS]] * REPEAT, axis=1)
    mixed = mixed.astype(jnp.bfloat16)
    for h in range(HEADS):
        at = (h % REPEAT * KV_HEADS + h // REPEAT) * HEAD_DIM
        out_ref[:, h * HEAD_DIM : (h + 1) * HEAD_DIM] = mixed[:, at : at + HEAD_DIM]


def combine(parts, own):
    return pl.pallas_call(
        combine_kernel,
        out_shape=jax.ShapeDtypeStruct((own.shape[0], QUERIES), jnp.bfloat16),
        in_specs=[VMEM] * 2,
        out_specs=VMEM,
        compiler_params=pltpu.CompilerParams(vmem_limit_bytes=48 * 1024 * 1024),
        name="combine",
    )(parts, own)


def per_device(
    tokens, norm_gain, w_query, w_keyvalue, cache, page_count, page_owner, keep_rows, dest_slot
):
    holder = lax.axis_index("page")
    half = lax.axis_index("tensor") % 2
    share = tokens.shape[0] // HOLDERS

    def normalise(rows):
        widened = rows.astype(jnp.float32)
        return (
            widened
            * lax.rsqrt(jnp.mean(widened * widened, axis=-1, keepdims=True) + EPSILON)
            * norm_gain
        ).astype(jnp.bfloat16)

    page_count = page_count.reshape(1)
    page_owner = page_owner.reshape(SOURCES)
    compact, kept = select_rows(page_count, dest_slot.reshape(SOURCES), keep_rows, cache)

    mine = normalise(lax.dynamic_slice_in_dim(tokens, holder * share, share, 0))
    across = lax.ppermute(mine, ("page", "tensor"), OTHER_HALF)
    got = [compact[0]] + [None] * (CHIPS - 1)

    def send(after, steps):
        blocks, after = lax.optimization_barrier(([compact[d] for d in steps], after))
        for d, block in zip(steps, blocks):
            got[d] = lax.ppermute(block, "page", OTHER_CHIP[d])
        return after

    def receive(before, steps):
        blocks, before = lax.optimization_barrier(([got[d] for d in steps], before))
        for d, block in zip(steps, blocks):
            got[d] = block
        return before

    across = send(across, (4, 5, 1))
    both = jnp.where(
        half == 0,
        jnp.concatenate([mine, across], axis=0),
        jnp.concatenate([across, mine], axis=0),
    )
    rows = lax.all_to_all(
        jnp.broadcast_to(both[None], (PLANE,) + both.shape),
        "tensor",
        0,
        0,
        axis_index_groups=PLANE_GROUPS,
        tiled=True,
    ).reshape(PLANE * both.shape[0], -1)
    projected = project(rows, w_query, w_keyvalue).reshape(PLANE, both.shape[0], -1)
    projected = send(projected, (2, 3))
    back = lax.all_to_all(
        projected, "tensor", 0, 0, axis_index_groups=PLANE_GROUPS, tiled=True
    )
    halves = receive(pick(back), (4, 5, 1, 2, 3))
    halves = send(halves, (6,))
    quarter = lax.all_to_all(
        halves, ("page", "tensor"), 0, 0, axis_index_groups=FOUR_GROUPS, tiled=True
    )
    rows = lax.all_gather(quarter, "page", axis=0, axis_index_groups=QUAD_GROUPS, tiled=True)
    part = attend(page_count, page_owner, kept, rows)
    far = lax.ppermute(part, "page", OTHER_QUAD)
    own = send(own_part(rows), (7,))
    far, own = lax.optimization_barrier((far, own))
    far = receive(far, (6,))
    parts = lax.all_gather(
        jnp.concatenate([part, far], axis=0),
        "page",
        axis=0,
        axis_index_groups=QUAD_GROUPS,
        tiled=True,
    )
    parts = receive(parts, (7,))
    cross = lax.ppermute(pack(got), "page", OTHER_CORE)
    attended = combine(parts, own)
    return attended, place_pages(got, cross)[:, None]


def solution(mesh):
    return jax.shard_map(
        per_device,
        mesh=mesh,
        in_specs=(
            P("tensor", None),
            P(),
            P(None, "tensor"),
            P(None, "tensor"),
            P("page", "tensor", None, None),
            P("page", "tensor"),
            P("page", "tensor"),
            P("page", "tensor", None),
            P("page", "tensor"),
        ),
        out_specs=(P("tensor", None), P("page", "tensor", None, None)),
        check_vma=False,
    )
```

```python
import jax
import jax.numpy as jnp
from jax import lax
from jax.experimental import pallas as pl
from jax.experimental.pallas import tpu as pltpu
from jax.sharding import PartitionSpec as P

HEADS = 32
KV_HEADS = 8
REPEAT = HEADS // KV_HEADS
HEAD_DIM = 80
KEYS = KV_HEADS * HEAD_DIM
QUERIES = HEADS * HEAD_DIM
EPSILON = 1e-05
NEGATIVE = -1e30

PLANE = 16
HOLDERS = 16
SOURCES = 8
KEEP = 32
EXTRA = 256

CHIPS = 8
PLANE_GROUPS = [[2 * i + half for i in range(PLANE)] for half in range(2)]
OTHER_HALF = [
    (p * 2 * PLANE + t, (p ^ 8) * 2 * PLANE + (t ^ 1)) for p in range(HOLDERS) for t in range(2 * PLANE)
]

COLUMN_GROUPS = [
    [(2 * z + core) * 2 * PLANE + 2 * xy + half for half in range(2) for z in range(CHIPS)]
    for xy in range(PLANE)
    for core in range(2)
]
QUAD_GROUPS = [[CHIPS * quad + i for i in range(CHIPS)] for quad in range(2)]
OTHER_CORE = [(i, i ^ 1) for i in range(HOLDERS)]
OTHER_QUAD = [(i, i ^ CHIPS) for i in range(HOLDERS)]
HALF_COLUMNS = (QUERIES + 2 * KEYS) // 2
STEP = 4

VMEM = pl.BlockSpec(memory_space=pltpu.VMEM)
SMEM = pl.BlockSpec(memory_space=pltpu.SMEM)


def select_kernel(count_ref, dest_ref, keep_ref, page_ref, out_ref, kept_ref):
    step = pl.program_id(0)

    @pl.when(step == 0)
    def _():
        out_ref[...] = jnp.zeros_like(out_ref)

    rows = page_ref.shape[1]
    for i in range(STEP):
        slot = step * STEP + i
        picks = jnp.broadcast_to(keep_ref[i], (rows, KEEP))
        chosen = (picks == lax.broadcasted_iota(jnp.int32, (rows, KEEP), 0)).astype(jnp.float32)
        kept = jnp.dot(
            chosen.T.astype(jnp.bfloat16), page_ref[i], preferred_element_type=jnp.float32
        ).astype(jnp.bfloat16)
        kept_ref[i * KEEP : (i + 1) * KEEP] = kept

        @pl.when(slot < count_ref[0])
        def _():
            out_ref[dest_ref[slot]] = kept


def select_rows(page_count, dest_slot, keep_rows, cache):
    sources, _, rows, width = cache.shape
    return pl.pallas_call(
        select_kernel,
        out_shape=(
            jax.ShapeDtypeStruct((HOLDERS, KEEP, width), cache.dtype),
            jax.ShapeDtypeStruct((sources * KEEP, width), cache.dtype),
        ),
        grid_spec=pltpu.PrefetchScalarGridSpec(
            num_scalar_prefetch=2,
            grid=(sources // STEP,),
            in_specs=[
                pl.BlockSpec((STEP, 1, KEEP), lambda s, *_: (s, 0, 0)),
                pl.BlockSpec((STEP, rows, width), lambda s, *_: (s, 0, 0)),
            ],
            out_specs=[
                pl.BlockSpec((HOLDERS, KEEP, width), lambda s, *_: (0, 0, 0)),
                pl.BlockSpec((STEP * KEEP, width), lambda s, *_: (s, 0)),
            ],
        ),
        name="select_rows",
    )(page_count, dest_slot, keep_rows, cache.reshape(sources, rows, width))


def project_kernel(rows_ref, query_ref, pair_ref, out_ref):
    rows = rows_ref[...]
    for ref, low, high in ((query_ref, 0, HEAD_DIM), (pair_ref, HEAD_DIM, HEAD_DIM * 3 // 2)):
        out_ref[:, low:high] = lax.dot_general(
            rows, ref[...], (((1,), (1,)), ((), ())), preferred_element_type=jnp.float32
        ).astype(jnp.bfloat16)


def project(rows, w_query, w_keyvalue):
    return pl.pallas_call(
        project_kernel,
        out_shape=jax.ShapeDtypeStruct((rows.shape[0], HEAD_DIM * 3 // 2), jnp.bfloat16),
        in_specs=[VMEM] * 3,
        out_specs=VMEM,
        name="project",
    )(rows, w_query.T, w_keyvalue.T)


def pick_kernel(plane_ref, all_ref, out_ref, rows_ref):
    half = HEAD_DIM // 2
    for i in range(PLANE):
        block = all_ref[i].astype(jnp.float32)
        at = (i % 2 * KV_HEADS + i // 2) * HEAD_DIM
        rows_ref[:, at : at + HEAD_DIM] = block[:, :HEAD_DIM]
        at = QUERIES // 2 + i * half
        rows_ref[:, at : at + half] = block[:, HEAD_DIM:]
    share = out_ref.shape[1]
    for h in range(2):
        piece = rows_ref[h * share : (h + 1) * share].astype(jnp.bfloat16)
        for z in range(CHIPS):
            out_ref[h * CHIPS + z] = piece


def pick(plane, everyone):
    count, rows, width = everyone.shape
    both = rows // PLANE
    piece = jax.ShapeDtypeStruct((2 * CHIPS, both // 2, HALF_COLUMNS), everyone.dtype)
    return pl.pallas_call(
        pick_kernel,
        out_shape=piece,
        grid_spec=pltpu.PrefetchScalarGridSpec(
            num_scalar_prefetch=1,
            grid=(1,),
            in_specs=[pl.BlockSpec((count, both, width), lambda i, plane: (0, plane[0], 0))],
            out_specs=pl.BlockSpec(piece.shape, lambda i, *_: (0, 0, 0)),
            scratch_shapes=[pltpu.VMEM((both, HALF_COLUMNS), jnp.float32)],
        ),
        name="pick",
    )(plane, everyone)


def held(near_ref, far_ref, holder, half, columns):
    chip = holder // 2
    spot = half * CHIPS + jnp.where(lax.axis_index("tensor") % 2 == half, chip, chip ^ 4)
    near = near_ref[spot, :, columns].astype(jnp.float32)
    far = far_ref[spot, :, columns].astype(jnp.float32)
    return jnp.where(lax.axis_index("page") % 2 == holder % 2, near, far)


def pieces(value, count):
    parts = []
    for _ in range(count):
        part = value.astype(jnp.bfloat16)
        parts.append(part)
        value = value - part.astype(jnp.float32)
    return parts


def attend_kernel(
    count_ref, owner_ref, kept_ref, near_ref, far_ref, out_ref, sum_ref, peak_ref, total_ref
):
    scale = HEAD_DIM ** (-0.5)
    share = near_ref.shape[1]
    line = lax.broadcasted_iota(jnp.int32, (share, QUERIES // 2), 0)
    head = lax.broadcasted_iota(jnp.int32, (KV_HEADS, KEYS), 0) * HEAD_DIM
    lane = lax.broadcasted_iota(jnp.int32, (KV_HEADS, KEYS), 1)
    mask = ((lane >= head) & (lane < head + HEAD_DIM)).astype(jnp.float32)
    for s in range(SOURCES):
        request = owner_ref[s]
        holder = request // share
        query = []
        for half in range(2):
            block = held(near_ref, far_ref, holder, half, pl.ds(0, QUERIES // 2))
            query.append(
                jnp.sum(jnp.where(line == request % share, block, 0.0), axis=0, keepdims=True)
            )
        spread = jnp.concatenate(
            [
                query[k % 2][:, k // 2 * KEYS : (k // 2 + 1) * KEYS] * mask
                for k in range(REPEAT)
            ],
            axis=0,
        ).astype(jnp.bfloat16)
        keys = kept_ref[s * KEEP : (s + 1) * KEEP, :KEYS]
        values = kept_ref[s * KEEP : (s + 1) * KEEP, KEYS:]
        score = scale * lax.dot_general(
            keys, spread, (((1,), (1,)), ((), ())), preferred_element_type=jnp.float32
        )
        peak = jnp.max(score, axis=0, keepdims=True)
        weight = jnp.exp(score - peak)
        total_ref[s : s + 1, :] = jnp.sum(weight, axis=0, keepdims=True)
        peak_ref[s : s + 1, :] = jnp.where(s < count_ref[0], peak, NEGATIVE)
        mixed = lax.dot_general(
            weight.astype(jnp.bfloat16),
            values,
            (((0,), (0,)), ((), ())),
            preferred_element_type=jnp.float32,
        )
        for k in range(REPEAT):
            sum_ref[s : s + 1, k * KEYS : (k + 1) * KEYS] = jnp.sum(
                mixed[k * KV_HEADS : (k + 1) * KV_HEADS] * mask, axis=0, keepdims=True
            )
    sums = sum_ref[...].astype(jnp.bfloat16)
    slots = lax.broadcasted_iota(jnp.int32, (SOURCES, HEADS), 0)
    tag = jnp.full((SOURCES, HEADS), -1, jnp.int32)
    for s in range(SOURCES):
        tag = jnp.where((slots == s) & (s < count_ref[0]), owner_ref[s], tag)
    tag = tag.astype(jnp.float32).astype(jnp.bfloat16)
    columns = pieces(peak_ref[...], 3) + pieces(total_ref[...], 3) + [tag, tag]
    columns = [column.astype(jnp.float32) for column in columns]
    columns = jnp.concatenate(columns, axis=1).astype(jnp.bfloat16)
    out_ref[:, :QUERIES] = sums
    out_ref[:, QUERIES:] = columns


def attend(page_count, page_owner, kept, near, far):
    return pl.pallas_call(
        attend_kernel,
        out_shape=jax.ShapeDtypeStruct((SOURCES, QUERIES + EXTRA), jnp.bfloat16),
        in_specs=[SMEM] * 2 + [VMEM] * 3,
        out_specs=VMEM,
        scratch_shapes=[
            pltpu.VMEM((SOURCES, QUERIES), jnp.float32),
            pltpu.VMEM((SOURCES, HEADS), jnp.float32),
            pltpu.VMEM((SOURCES, HEADS), jnp.float32),
        ],
        name="attend",
    )(page_count, page_owner, kept, near, far)


def spread_dot(value, chosen, contract, count, chosen_first=False):
    total = None
    for part in pieces(value, count):
        operands = (chosen, part) if chosen_first else (part, chosen)
        term = lax.dot_general(
            *operands, (contract, ((), ())), preferred_element_type=jnp.float32
        )
        total = term if total is None else total + term
    return total


def head_columns():
    head = lax.broadcasted_iota(jnp.int32, (HEADS, QUERIES), 0) * HEAD_DIM
    lane = lax.broadcasted_iota(jnp.int32, (HEADS, QUERIES), 1)
    return ((lane >= head) & (lane < head + HEAD_DIM)).astype(jnp.float32).astype(jnp.bfloat16)


def own_kernel(near_ref, far_ref, own_ref, query_ref, pair_ref):
    scale = HEAD_DIM ** (-0.5)
    share = near_ref.shape[1]
    piece = HEAD_DIM // 2
    for holder in range(HOLDERS):
        rows = slice(holder * share, (holder + 1) * share)
        for half in range(2):
            block = held(near_ref, far_ref, holder, half, pl.ds(0, HALF_COLUMNS))
            for k in range(2):
                at = (2 * k + half) * KEYS
                query_ref[rows, at : at + KEYS] = block[:, k * KEYS : (k + 1) * KEYS]
            pair_ref[half, rows, :] = block[:, QUERIES // 2 :]
    keys, values = [], []
    for g in range(KV_HEADS):
        for half in range(2):
            keys.append(pair_ref[half, :, g * piece : (g + 1) * piece])
            at = KEYS // 2 + g * piece
            values.append(pair_ref[half, :, at : at + piece])
    key = jnp.concatenate(keys, axis=1)
    own_ref[:, :KEYS] = jnp.concatenate(values, axis=1)
    product = query_ref[...] * jnp.concatenate([key] * REPEAT, axis=1)
    own_ref[:, KEYS:] = jnp.concatenate(
        [scale * spread_dot(product, head_columns(), ((1,), (1,)), 3)] * 4, axis=1
    )


def own_part(near, far):
    requests = HOLDERS * near.shape[1]
    return pl.pallas_call(
        own_kernel,
        out_shape=jax.ShapeDtypeStruct((requests, KEYS + 4 * HEADS), jnp.float32),
        in_specs=[VMEM, VMEM],
        out_specs=VMEM,
        scratch_shapes=[
            pltpu.VMEM((requests, QUERIES), jnp.float32),
            pltpu.VMEM((2, requests, KEYS), jnp.float32),
        ],
        name="own_part",
    )(near, far)


def combine_kernel(part_ref, own_ref, out_ref):
    requests = out_ref.shape[0]
    slots = part_ref.shape[0]
    extra = part_ref[:, QUERIES:].astype(jnp.float32)
    column = [extra[:, i * HEADS : (i + 1) * HEADS] for i in range(7)]
    peaks = column[0] + column[1] + column[2]
    totals = column[3] + column[4] + column[5]
    tag = column[6][:, :1]
    member = (
        tag == lax.broadcasted_iota(jnp.int32, (slots, requests), 1).astype(jnp.float32)
    ).astype(jnp.float32).astype(jnp.bfloat16)
    expand = head_columns()
    own = own_ref[:, KEYS : KEYS + HEADS]
    quarter = slots // 4
    beside = [
        jnp.concatenate([block[i * quarter : (i + 1) * quarter] for i in range(4)], axis=1)
        for block in (peaks, column[6])
    ]
    row = lax.broadcasted_iota(jnp.int32, (requests, 4 * HEADS), 0).astype(jnp.float32)
    tops = [jnp.full(row.shape, NEGATIVE, jnp.float32)] * 2
    for s in range(quarter):
        tops[s % 2] = jnp.maximum(
            tops[s % 2],
            jnp.where(beside[1][s : s + 1] == row, beside[0][s : s + 1], NEGATIVE),
        )
    wide = jnp.maximum(tops[0], tops[1])
    top = own
    for i in range(4):
        top = jnp.maximum(top, wide[:, i * HEADS : (i + 1) * HEADS])
    own_weight = jnp.exp(own - top)
    weight = jnp.exp(peaks - spread_dot(top, member, ((1,), (0,)), 3, True))
    total = spread_dot(weight * totals, member, ((0,), (0,)), 3, True) + own_weight
    inverse = 1.0 / total
    weight = weight * spread_dot(inverse, member, ((1,), (0,)), 3, True)
    scaled = part_ref[:, :QUERIES].astype(jnp.float32) * spread_dot(weight, expand, ((1,), (0,)), 2)
    mixed = spread_dot(scaled, member, ((0,), (0,)), 2, True)
    own_share = spread_dot(own_weight * inverse, expand, ((1,), (0,)), 2)
    mixed = mixed + own_share * jnp.concatenate([own_ref[:, :KEYS]] * REPEAT, axis=1)
    mixed = mixed.astype(jnp.bfloat16)
    for h in range(HEADS):
        at = (h % REPEAT * KV_HEADS + h // REPEAT) * HEAD_DIM
        out_ref[:, h * HEAD_DIM : (h + 1) * HEAD_DIM] = mixed[:, at : at + HEAD_DIM]


def combine(parts, own):
    return pl.pallas_call(
        combine_kernel,
        out_shape=jax.ShapeDtypeStruct((own.shape[0], QUERIES), jnp.bfloat16),
        in_specs=[VMEM] * 2,
        out_specs=VMEM,
        compiler_params=pltpu.CompilerParams(vmem_limit_bytes=48 * 1024 * 1024),
        name="combine",
    )(parts, own)


def per_device(
    tokens, norm_gain, w_query, w_keyvalue, cache, page_count, page_owner, keep_rows, dest_slot
):
    holder = lax.axis_index("page")
    group = lax.axis_index("tensor")
    half = group % 2
    share = tokens.shape[0] // HOLDERS

    def normalise(rows):
        widened = rows.astype(jnp.float32)
        return (
            widened
            * lax.rsqrt(jnp.mean(widened * widened, axis=-1, keepdims=True) + EPSILON)
            * norm_gain
        ).astype(jnp.bfloat16)

    page_count = page_count.reshape(1)
    page_owner = page_owner.reshape(SOURCES)
    compact, kept = select_rows(page_count, dest_slot.reshape(SOURCES), keep_rows, cache)

    mine = normalise(lax.dynamic_slice_in_dim(tokens, holder * share, share, 0))
    across = lax.ppermute(mine, ("page", "tensor"), OTHER_HALF)
    across, compact = lax.optimization_barrier((across, compact))
    arrived = lax.all_to_all(compact, "page", 0, 0, tiled=True)

    both = jnp.where(
        half == 0,
        jnp.concatenate([mine, across], axis=0),
        jnp.concatenate([across, mine], axis=0),
    )
    rows = lax.all_gather(
        both, "tensor", axis=0, axis_index_groups=PLANE_GROUPS, tiled=True
    )
    projected = project(rows, w_query, w_keyvalue)
    everyone = lax.all_gather(
        projected, "tensor", axis=0, axis_index_groups=PLANE_GROUPS, tiled=False
    )
    halves = pick((group // 2).reshape(1), everyone)
    halves, arrived = lax.optimization_barrier((halves, arrived))
    near = lax.all_to_all(
        halves, ("page", "tensor"), 0, 0, axis_index_groups=COLUMN_GROUPS, tiled=True
    )
    far = lax.ppermute(near, "page", OTHER_CORE)
    part = attend(page_count, page_owner, kept, near, far)
    own = own_part(near, far)
    far = lax.ppermute(part, "page", OTHER_QUAD)
    far, own = lax.optimization_barrier((far, own))
    parts = lax.all_gather(
        jnp.concatenate([part, far], axis=0),
        "page",
        axis=0,
        axis_index_groups=QUAD_GROUPS,
        tiled=True,
    )
    return combine(parts, own), arrived[:, None]


def solution(mesh):
    return jax.shard_map(
        per_device,
        mesh=mesh,
        in_specs=(
            P("tensor", None),
            P(),
            P(None, "tensor"),
            P(None, "tensor"),
            P("page", "tensor", None, None),
            P("page", "tensor"),
            P("page", "tensor"),
            P("page", "tensor", None),
            P("page", "tensor"),
        ),
        out_specs=(P("tensor", None), P("page", "tensor", None, None)),
        check_vma=False,
    )
```

```python
import jax
import jax.numpy as jnp
from jax import lax
from jax.experimental import pallas as pl
from jax.experimental.pallas import tpu as pltpu
from jax.sharding import PartitionSpec as P

HEADS = 32
KV_HEADS = 8
REPEAT = HEADS // KV_HEADS
HEAD_DIM = 80
KEYS = KV_HEADS * HEAD_DIM
QUERIES = HEADS * HEAD_DIM
EPSILON = 1e-05
NEGATIVE = -1e30

PLANE = 16
HOLDERS = 16
SOURCES = 8
KEEP = 32
EXTRA = 256

CHIPS = 8
PLANE_GROUPS = [[2 * i + half for i in range(PLANE)] for half in range(2)]
OTHER_HALF = [
    (p * 2 * PLANE + t, (p ^ 8) * 2 * PLANE + (t ^ 1)) for p in range(HOLDERS) for t in range(2 * PLANE)
]

COLUMN_GROUPS = [
    [(2 * z + core) * 2 * PLANE + 2 * xy + half for half in range(2) for z in range(CHIPS)]
    for xy in range(PLANE)
    for core in range(2)
]
QUAD_GROUPS = [[CHIPS * quad + i for i in range(CHIPS)] for quad in range(2)]
OTHER_CORE = [(i, i ^ 1) for i in range(HOLDERS)]
OTHER_QUAD = [(i, i ^ CHIPS) for i in range(HOLDERS)]
HALF_COLUMNS = (QUERIES + 2 * KEYS) // 2
STEP = 8

VMEM = pl.BlockSpec(memory_space=pltpu.VMEM)
SMEM = pl.BlockSpec(memory_space=pltpu.SMEM)


def select_kernel(count_ref, dest_ref, keep_ref, page_ref, out_ref, kept_ref):
    step = pl.program_id(0)

    @pl.when(step == 0)
    def _():
        out_ref[...] = jnp.zeros_like(out_ref)

    rows = page_ref.shape[1]
    for i in range(STEP):
        slot = step * STEP + i
        chosen = keep_ref[i] == lax.broadcasted_iota(jnp.int32, (rows, KEEP), 0)
        kept = lax.dot_general(
            chosen.astype(jnp.float32).astype(jnp.bfloat16),
            page_ref[i],
            (((0,), (0,)), ((), ())),
            preferred_element_type=jnp.float32,
        ).astype(jnp.bfloat16)
        kept_ref[i * KEEP : (i + 1) * KEEP] = kept

        @pl.when(slot < count_ref[0])
        def _():
            out_ref[dest_ref[slot]] = kept


def select_rows(page_count, dest_slot, keep_rows, cache):
    sources, _, rows, width = cache.shape
    return pl.pallas_call(
        select_kernel,
        out_shape=(
            jax.ShapeDtypeStruct((HOLDERS, KEEP, width), cache.dtype),
            jax.ShapeDtypeStruct((sources * KEEP, width), cache.dtype),
        ),
        grid_spec=pltpu.PrefetchScalarGridSpec(
            num_scalar_prefetch=2,
            grid=(sources // STEP,),
            in_specs=[
                pl.BlockSpec((STEP, 1, KEEP), lambda s, *_: (s, 0, 0)),
                pl.BlockSpec((STEP, rows, width), lambda s, *_: (s, 0, 0)),
            ],
            out_specs=[
                pl.BlockSpec((HOLDERS, KEEP, width), lambda s, *_: (0, 0, 0)),
                pl.BlockSpec((STEP * KEEP, width), lambda s, *_: (s, 0)),
            ],
        ),
        compiler_params=pltpu.CompilerParams(vmem_limit_bytes=48 * 1024 * 1024),
        name="select_rows",
    )(page_count, dest_slot, keep_rows, cache.reshape(sources, rows, width))


def project_kernel(rows_ref, query_ref, pair_ref, out_ref):
    rows = rows_ref[...]
    for ref, low, high in ((query_ref, 0, HEAD_DIM), (pair_ref, HEAD_DIM, HEAD_DIM * 3 // 2)):
        out_ref[:, low:high] = lax.dot_general(
            rows, ref[...], (((1,), (1,)), ((), ())), preferred_element_type=jnp.float32
        ).astype(jnp.bfloat16)


def project(rows, w_query, w_keyvalue):
    return pl.pallas_call(
        project_kernel,
        out_shape=jax.ShapeDtypeStruct((rows.shape[0], HEAD_DIM * 3 // 2), jnp.bfloat16),
        in_specs=[VMEM] * 3,
        out_specs=VMEM,
        name="project",
    )(rows, w_query.T, w_keyvalue.T)


def pick_kernel(plane_ref, all_ref, out_ref, rows_ref):
    half = HEAD_DIM // 2
    for i in range(PLANE):
        block = all_ref[i].astype(jnp.float32)
        at = (i % 2 * KV_HEADS + i // 2) * HEAD_DIM
        rows_ref[:, at : at + HEAD_DIM] = block[:, :HEAD_DIM]
        at = QUERIES // 2 + i * half
        rows_ref[:, at : at + half] = block[:, HEAD_DIM:]
    share = out_ref.shape[1]
    for h in range(2):
        piece = rows_ref[h * share : (h + 1) * share].astype(jnp.bfloat16)
        for z in range(CHIPS):
            out_ref[h * CHIPS + z] = piece


def pick(plane, everyone):
    count, rows, width = everyone.shape
    both = rows // PLANE
    piece = jax.ShapeDtypeStruct((2 * CHIPS, both // 2, HALF_COLUMNS), everyone.dtype)
    return pl.pallas_call(
        pick_kernel,
        out_shape=piece,
        grid_spec=pltpu.PrefetchScalarGridSpec(
            num_scalar_prefetch=1,
            grid=(1,),
            in_specs=[pl.BlockSpec((count, both, width), lambda i, plane: (0, plane[0], 0))],
            out_specs=pl.BlockSpec(piece.shape, lambda i, *_: (0, 0, 0)),
            scratch_shapes=[pltpu.VMEM((both, HALF_COLUMNS), jnp.float32)],
        ),
        name="pick",
    )(plane, everyone)


def held(near_ref, far_ref, holder, half, columns):
    chip = holder // 2
    spot = half * CHIPS + jnp.where(lax.axis_index("tensor") % 2 == half, chip, chip ^ 4)
    near = near_ref[spot, :, columns].astype(jnp.float32)
    far = far_ref[spot, :, columns].astype(jnp.float32)
    return jnp.where(lax.axis_index("page") % 2 == holder % 2, near, far)


def pieces(value, count):
    parts = []
    for _ in range(count):
        part = value.astype(jnp.bfloat16)
        parts.append(part)
        value = value - part.astype(jnp.float32)
    return parts


def attend_kernel(
    count_ref, owner_ref, kept_ref, near_ref, far_ref, out_ref, sum_ref, peak_ref, total_ref
):
    scale = HEAD_DIM ** (-0.5)
    share = near_ref.shape[1]
    line = lax.broadcasted_iota(jnp.int32, (share, QUERIES // 2), 0)
    head = lax.broadcasted_iota(jnp.int32, (KV_HEADS, KEYS), 0) * HEAD_DIM
    lane = lax.broadcasted_iota(jnp.int32, (KV_HEADS, KEYS), 1)
    mask = ((lane >= head) & (lane < head + HEAD_DIM)).astype(jnp.float32)
    for s in range(SOURCES):
        request = owner_ref[s]
        holder = request // share
        query = []
        for half in range(2):
            block = held(near_ref, far_ref, holder, half, pl.ds(0, QUERIES // 2))
            query.append(
                jnp.sum(jnp.where(line == request % share, block, 0.0), axis=0, keepdims=True)
            )
        spread = jnp.concatenate(
            [
                query[k % 2][:, k // 2 * KEYS : (k // 2 + 1) * KEYS] * mask
                for k in range(REPEAT)
            ],
            axis=0,
        ).astype(jnp.bfloat16)
        keys = kept_ref[s * KEEP : (s + 1) * KEEP, :KEYS]
        values = kept_ref[s * KEEP : (s + 1) * KEEP, KEYS:]
        score = scale * lax.dot_general(
            keys, spread, (((1,), (1,)), ((), ())), preferred_element_type=jnp.float32
        )
        peak = jnp.max(score, axis=0, keepdims=True)
        weight = jnp.exp(score - peak)
        total_ref[s : s + 1, :] = jnp.sum(weight, axis=0, keepdims=True)
        peak_ref[s : s + 1, :] = jnp.where(s < count_ref[0], peak, NEGATIVE)
        mixed = lax.dot_general(
            weight.astype(jnp.bfloat16),
            values,
            (((0,), (0,)), ((), ())),
            preferred_element_type=jnp.float32,
        )
        for k in range(REPEAT):
            sum_ref[s : s + 1, k * KEYS : (k + 1) * KEYS] = jnp.sum(
                mixed[k * KV_HEADS : (k + 1) * KV_HEADS] * mask, axis=0, keepdims=True
            )
    sums = sum_ref[...].astype(jnp.bfloat16)
    slots = lax.broadcasted_iota(jnp.int32, (SOURCES, HEADS), 0)
    tag = jnp.full((SOURCES, HEADS), -1, jnp.int32)
    for s in range(SOURCES):
        tag = jnp.where((slots == s) & (s < count_ref[0]), owner_ref[s], tag)
    tag = tag.astype(jnp.float32).astype(jnp.bfloat16)
    columns = pieces(peak_ref[...], 3) + pieces(total_ref[...], 3) + [tag, tag]
    columns = [column.astype(jnp.float32) for column in columns]
    columns = jnp.concatenate(columns, axis=1).astype(jnp.bfloat16)
    out_ref[:, :QUERIES] = sums
    out_ref[:, QUERIES:] = columns


def attend(page_count, page_owner, kept, near, far):
    return pl.pallas_call(
        attend_kernel,
        out_shape=jax.ShapeDtypeStruct((SOURCES, QUERIES + EXTRA), jnp.bfloat16),
        in_specs=[SMEM] * 2 + [VMEM] * 3,
        out_specs=VMEM,
        scratch_shapes=[
            pltpu.VMEM((SOURCES, QUERIES), jnp.float32),
            pltpu.VMEM((SOURCES, HEADS), jnp.float32),
            pltpu.VMEM((SOURCES, HEADS), jnp.float32),
        ],
        name="attend",
    )(page_count, page_owner, kept, near, far)


def spread_dot(value, chosen, contract, count, chosen_first=False):
    total = None
    for part in pieces(value, count):
        operands = (chosen, part) if chosen_first else (part, chosen)
        term = lax.dot_general(
            *operands, (contract, ((), ())), preferred_element_type=jnp.float32
        )
        total = term if total is None else total + term
    return total


def head_columns():
    head = lax.broadcasted_iota(jnp.int32, (HEADS, QUERIES), 0) * HEAD_DIM
    lane = lax.broadcasted_iota(jnp.int32, (HEADS, QUERIES), 1)
    return ((lane >= head) & (lane < head + HEAD_DIM)).astype(jnp.float32).astype(jnp.bfloat16)


def own_kernel(near_ref, far_ref, own_ref, query_ref, pair_ref):
    scale = HEAD_DIM ** (-0.5)
    share = near_ref.shape[1]
    piece = HEAD_DIM // 2
    for holder in range(HOLDERS):
        rows = slice(holder * share, (holder + 1) * share)
        for half in range(2):
            block = held(near_ref, far_ref, holder, half, pl.ds(0, HALF_COLUMNS))
            for k in range(2):
                at = (2 * k + half) * KEYS
                query_ref[rows, at : at + KEYS] = block[:, k * KEYS : (k + 1) * KEYS]
            pair_ref[half, rows, :] = block[:, QUERIES // 2 :]
    keys, values = [], []
    for g in range(KV_HEADS):
        for half in range(2):
            keys.append(pair_ref[half, :, g * piece : (g + 1) * piece])
            at = KEYS // 2 + g * piece
            values.append(pair_ref[half, :, at : at + piece])
    key = jnp.concatenate(keys, axis=1)
    own_ref[:, :KEYS] = jnp.concatenate(values, axis=1)
    product = query_ref[...] * jnp.concatenate([key] * REPEAT, axis=1)
    own_ref[:, KEYS:] = jnp.concatenate(
        [scale * spread_dot(product, head_columns(), ((1,), (1,)), 3)] * 4, axis=1
    )


def own_part(near, far):
    requests = HOLDERS * near.shape[1]
    return pl.pallas_call(
        own_kernel,
        out_shape=jax.ShapeDtypeStruct((requests, KEYS + 4 * HEADS), jnp.float32),
        in_specs=[VMEM, VMEM],
        out_specs=VMEM,
        scratch_shapes=[
            pltpu.VMEM((requests, QUERIES), jnp.float32),
            pltpu.VMEM((2, requests, KEYS), jnp.float32),
        ],
        name="own_part",
    )(near, far)


def combine_kernel(part_ref, own_ref, out_ref):
    requests = out_ref.shape[0]
    slots = part_ref.shape[0]
    extra = part_ref[:, QUERIES:].astype(jnp.float32)
    column = [extra[:, i * HEADS : (i + 1) * HEADS] for i in range(7)]
    peaks = column[0] + column[1] + column[2]
    totals = column[3] + column[4] + column[5]
    tag = column[6][:, :1]
    member = (
        tag == lax.broadcasted_iota(jnp.int32, (slots, requests), 1).astype(jnp.float32)
    ).astype(jnp.float32).astype(jnp.bfloat16)
    expand = head_columns()
    own = own_ref[:, KEYS : KEYS + HEADS]
    quarter = slots // 4
    beside = [
        jnp.concatenate([block[i * quarter : (i + 1) * quarter] for i in range(4)], axis=1)
        for block in (peaks, column[6])
    ]
    row = lax.broadcasted_iota(jnp.int32, (requests, 4 * HEADS), 0).astype(jnp.float32)
    tops = [jnp.full(row.shape, NEGATIVE, jnp.float32)] * 2
    for s in range(quarter):
        tops[s % 2] = jnp.maximum(
            tops[s % 2],
            jnp.where(beside[1][s : s + 1] == row, beside[0][s : s + 1], NEGATIVE),
        )
    wide = jnp.maximum(tops[0], tops[1])
    top = own
    for i in range(4):
        top = jnp.maximum(top, wide[:, i * HEADS : (i + 1) * HEADS])
    own_weight = jnp.exp(own - top)
    weight = jnp.exp(peaks - spread_dot(top, member, ((1,), (0,)), 3, True))
    total = spread_dot(weight * totals, member, ((0,), (0,)), 3, True) + own_weight
    inverse = 1.0 / total
    weight = weight * spread_dot(inverse, member, ((1,), (0,)), 3, True)
    scaled = part_ref[:, :QUERIES].astype(jnp.float32) * spread_dot(weight, expand, ((1,), (0,)), 2)
    mixed = spread_dot(scaled, member, ((0,), (0,)), 2, True)
    own_share = spread_dot(own_weight * inverse, expand, ((1,), (0,)), 2)
    mixed = mixed + own_share * jnp.concatenate([own_ref[:, :KEYS]] * REPEAT, axis=1)
    mixed = mixed.astype(jnp.bfloat16)
    for h in range(HEADS):
        at = (h % REPEAT * KV_HEADS + h // REPEAT) * HEAD_DIM
        out_ref[:, h * HEAD_DIM : (h + 1) * HEAD_DIM] = mixed[:, at : at + HEAD_DIM]


def combine(parts, own):
    return pl.pallas_call(
        combine_kernel,
        out_shape=jax.ShapeDtypeStruct((own.shape[0], QUERIES), jnp.bfloat16),
        in_specs=[VMEM] * 2,
        out_specs=VMEM,
        compiler_params=pltpu.CompilerParams(vmem_limit_bytes=48 * 1024 * 1024),
        name="combine",
    )(parts, own)


def settle_kernel(in_ref, out_ref):
    out_ref[...] = in_ref[...]


def settle(pages):
    block = pl.BlockSpec((4,) + pages.shape[1:], lambda i: (i, 0, 0))
    return pl.pallas_call(
        settle_kernel,
        out_shape=jax.ShapeDtypeStruct(pages.shape, pages.dtype),
        grid=(pages.shape[0] // 4,),
        in_specs=[block],
        out_specs=block,
        name="settle",
    )(pages)


def per_device(
    tokens, norm_gain, w_query, w_keyvalue, cache, page_count, page_owner, keep_rows, dest_slot
):
    holder = lax.axis_index("page")
    group = lax.axis_index("tensor")
    half = group % 2
    share = tokens.shape[0] // HOLDERS

    def normalise(rows):
        widened = rows.astype(jnp.float32)
        return (
            widened
            * lax.rsqrt(jnp.mean(widened * widened, axis=-1, keepdims=True) + EPSILON)
            * norm_gain
        ).astype(jnp.bfloat16)

    page_count = page_count.reshape(1)
    page_owner = page_owner.reshape(SOURCES)
    compact, kept = select_rows(page_count, dest_slot.reshape(SOURCES), keep_rows, cache)

    mine = normalise(lax.dynamic_slice_in_dim(tokens, holder * share, share, 0))
    across = lax.ppermute(mine, ("page", "tensor"), OTHER_HALF)
    across, compact = lax.optimization_barrier((across, compact))
    arrived = lax.all_to_all(compact, "page", 0, 0, tiled=True)

    both = jnp.where(
        half == 0,
        jnp.concatenate([mine, across], axis=0),
        jnp.concatenate([across, mine], axis=0),
    )
    rows = lax.all_gather(
        both, "tensor", axis=0, axis_index_groups=PLANE_GROUPS, tiled=True
    )
    projected = project(rows, w_query, w_keyvalue)
    everyone = lax.all_gather(
        projected, "tensor", axis=0, axis_index_groups=PLANE_GROUPS, tiled=False
    )
    halves = pick((group // 2).reshape(1), everyone)
    halves, arrived = lax.optimization_barrier((halves, arrived))
    near = lax.all_to_all(
        halves, ("page", "tensor"), 0, 0, axis_index_groups=COLUMN_GROUPS, tiled=True
    )
    near, settled = lax.optimization_barrier((near, settle(arrived)))
    far = lax.ppermute(near, "page", OTHER_CORE)
    part = attend(page_count, page_owner, kept, near, far)
    own = own_part(near, far)
    far = lax.ppermute(part, "page", OTHER_QUAD)
    far, own = lax.optimization_barrier((far, own))
    parts = lax.all_gather(
        jnp.concatenate([part, far], axis=0),
        "page",
        axis=0,
        axis_index_groups=QUAD_GROUPS,
        tiled=True,
    )
    return combine(parts, own), settled[:, None]


def solution(mesh):
    return jax.shard_map(
        per_device,
        mesh=mesh,
        in_specs=(
            P("tensor", None),
            P(),
            P(None, "tensor"),
            P(None, "tensor"),
            P("page", "tensor", None, None),
            P("page", "tensor"),
            P("page", "tensor"),
            P("page", "tensor", None),
            P("page", "tensor"),
        ),
        out_specs=(P("tensor", None), P("page", "tensor", None, None)),
        check_vma=False,
    )
```

```python
import jax
import jax.numpy as jnp
from jax import lax
from jax.experimental import pallas as pl
from jax.experimental.pallas import tpu as pltpu
from jax.sharding import PartitionSpec as P

HEADS = 32
KV_HEADS = 8
REPEAT = HEADS // KV_HEADS
HEAD_DIM = 80
KEYS = KV_HEADS * HEAD_DIM
QUERIES = HEADS * HEAD_DIM
EPSILON = 1e-05
NEGATIVE = -1e30

PLANE = 16
HOLDERS = 16
SOURCES = 8
KEEP = 32
EXTRA = 256

CHIPS = 8
PLANE_GROUPS = [[2 * i + half for i in range(PLANE)] for half in range(2)]
OTHER_HALF = [
    (p * 2 * PLANE + t, (p ^ 8) * 2 * PLANE + (t ^ 1)) for p in range(HOLDERS) for t in range(2 * PLANE)
]

COLUMN_GROUPS = [
    [(2 * z + core) * 2 * PLANE + 2 * xy + half for half in range(2) for z in range(CHIPS)]
    for xy in range(PLANE)
    for core in range(2)
]
QUAD_GROUPS = [[CHIPS * quad + i for i in range(CHIPS)] for quad in range(2)]
OTHER_CORE = [(i, i ^ 1) for i in range(HOLDERS)]
OTHER_QUAD = [(i, i ^ CHIPS) for i in range(HOLDERS)]
HALF_COLUMNS = (QUERIES + 2 * KEYS) // 2
STEP = 4

VMEM = pl.BlockSpec(memory_space=pltpu.VMEM)
SMEM = pl.BlockSpec(memory_space=pltpu.SMEM)


def select_kernel(count_ref, dest_ref, keep_ref, page_ref, out_ref, kept_ref):
    step = pl.program_id(0)

    @pl.when(step == 0)
    def _():
        out_ref[...] = jnp.zeros_like(out_ref)

    rows = page_ref.shape[1]
    for i in range(STEP):
        slot = step * STEP + i
        chosen = keep_ref[i] == lax.broadcasted_iota(jnp.int32, (rows, KEEP), 0)
        kept = lax.dot_general(
            chosen.astype(jnp.float32).astype(jnp.bfloat16),
            page_ref[i],
            (((0,), (0,)), ((), ())),
            preferred_element_type=jnp.float32,
        ).astype(jnp.bfloat16)
        kept_ref[i * KEEP : (i + 1) * KEEP] = kept

        @pl.when(slot < count_ref[0])
        def _():
            out_ref[dest_ref[slot]] = kept


def select_rows(page_count, dest_slot, keep_rows, cache):
    sources, _, rows, width = cache.shape
    return pl.pallas_call(
        select_kernel,
        out_shape=(
            jax.ShapeDtypeStruct((HOLDERS, KEEP, width), cache.dtype),
            jax.ShapeDtypeStruct((sources * KEEP, width), cache.dtype),
        ),
        grid_spec=pltpu.PrefetchScalarGridSpec(
            num_scalar_prefetch=2,
            grid=(sources // STEP,),
            in_specs=[
                pl.BlockSpec((STEP, 1, KEEP), lambda s, *_: (s, 0, 0)),
                pl.BlockSpec((STEP, rows, width), lambda s, *_: (s, 0, 0)),
            ],
            out_specs=[
                pl.BlockSpec((HOLDERS, KEEP, width), lambda s, *_: (0, 0, 0)),
                pl.BlockSpec((STEP * KEEP, width), lambda s, *_: (s, 0)),
            ],
        ),
        name="select_rows",
    )(page_count, dest_slot, keep_rows, cache.reshape(sources, rows, width))


def project_kernel(rows_ref, query_ref, pair_ref, out_ref):
    rows = rows_ref[...]
    for ref, low, high in ((query_ref, 0, HEAD_DIM), (pair_ref, HEAD_DIM, HEAD_DIM * 3 // 2)):
        out_ref[:, low:high] = lax.dot_general(
            rows, ref[...], (((1,), (1,)), ((), ())), preferred_element_type=jnp.float32
        ).astype(jnp.bfloat16)


def project(rows, w_query, w_keyvalue):
    return pl.pallas_call(
        project_kernel,
        out_shape=jax.ShapeDtypeStruct((rows.shape[0], HEAD_DIM * 3 // 2), jnp.bfloat16),
        in_specs=[VMEM] * 3,
        out_specs=VMEM,
        name="project",
    )(rows, w_query.T, w_keyvalue.T)


def pick_kernel(plane_ref, all_ref, out_ref, rows_ref):
    half = HEAD_DIM // 2
    for i in range(PLANE):
        block = all_ref[i].astype(jnp.float32)
        at = (i % 2 * KV_HEADS + i // 2) * HEAD_DIM
        rows_ref[:, at : at + HEAD_DIM] = block[:, :HEAD_DIM]
        at = QUERIES // 2 + i * half
        rows_ref[:, at : at + half] = block[:, HEAD_DIM:]
    share = out_ref.shape[1]
    for h in range(2):
        piece = rows_ref[h * share : (h + 1) * share].astype(jnp.bfloat16)
        for z in range(CHIPS):
            out_ref[h * CHIPS + z] = piece


def pick(plane, everyone):
    count, rows, width = everyone.shape
    both = rows // PLANE
    piece = jax.ShapeDtypeStruct((2 * CHIPS, both // 2, HALF_COLUMNS), everyone.dtype)
    return pl.pallas_call(
        pick_kernel,
        out_shape=piece,
        grid_spec=pltpu.PrefetchScalarGridSpec(
            num_scalar_prefetch=1,
            grid=(1,),
            in_specs=[pl.BlockSpec((count, both, width), lambda i, plane: (0, plane[0], 0))],
            out_specs=pl.BlockSpec(piece.shape, lambda i, *_: (0, 0, 0)),
            scratch_shapes=[pltpu.VMEM((both, HALF_COLUMNS), jnp.float32)],
        ),
        name="pick",
    )(plane, everyone)


def held(near_ref, far_ref, holder, half, columns):
    chip = holder // 2
    spot = half * CHIPS + jnp.where(lax.axis_index("tensor") % 2 == half, chip, chip ^ 4)
    near = near_ref[spot, :, columns].astype(jnp.float32)
    far = far_ref[spot, :, columns].astype(jnp.float32)
    return jnp.where(lax.axis_index("page") % 2 == holder % 2, near, far)


def pieces(value, count):
    parts = []
    for _ in range(count):
        part = value.astype(jnp.bfloat16)
        parts.append(part)
        value = value - part.astype(jnp.float32)
    return parts


def attend_kernel(
    count_ref, owner_ref, kept_ref, near_ref, far_ref, out_ref, sum_ref, peak_ref, total_ref
):
    scale = HEAD_DIM ** (-0.5)
    share = near_ref.shape[1]
    line = lax.broadcasted_iota(jnp.int32, (share, QUERIES // 2), 0)
    head = lax.broadcasted_iota(jnp.int32, (KV_HEADS, KEYS), 0) * HEAD_DIM
    lane = lax.broadcasted_iota(jnp.int32, (KV_HEADS, KEYS), 1)
    mask = ((lane >= head) & (lane < head + HEAD_DIM)).astype(jnp.float32)
    for s in range(SOURCES):
        request = owner_ref[s]
        holder = request // share
        query = []
        for half in range(2):
            block = held(near_ref, far_ref, holder, half, pl.ds(0, QUERIES // 2))
            query.append(
                jnp.sum(jnp.where(line == request % share, block, 0.0), axis=0, keepdims=True)
            )
        spread = jnp.concatenate(
            [
                query[k % 2][:, k // 2 * KEYS : (k // 2 + 1) * KEYS] * mask
                for k in range(REPEAT)
            ],
            axis=0,
        ).astype(jnp.bfloat16)
        keys = kept_ref[s * KEEP : (s + 1) * KEEP, :KEYS]
        values = kept_ref[s * KEEP : (s + 1) * KEEP, KEYS:]
        score = scale * lax.dot_general(
            keys, spread, (((1,), (1,)), ((), ())), preferred_element_type=jnp.float32
        )
        peak = jnp.max(score, axis=0, keepdims=True)
        weight = jnp.exp(score - peak)
        total_ref[s : s + 1, :] = jnp.sum(weight, axis=0, keepdims=True)
        peak_ref[s : s + 1, :] = jnp.where(s < count_ref[0], peak, NEGATIVE)
        mixed = lax.dot_general(
            weight.astype(jnp.bfloat16),
            values,
            (((0,), (0,)), ((), ())),
            preferred_element_type=jnp.float32,
        )
        for k in range(REPEAT):
            sum_ref[s : s + 1, k * KEYS : (k + 1) * KEYS] = jnp.sum(
                mixed[k * KV_HEADS : (k + 1) * KV_HEADS] * mask, axis=0, keepdims=True
            )
    sums = sum_ref[...].astype(jnp.bfloat16)
    slots = lax.broadcasted_iota(jnp.int32, (SOURCES, HEADS), 0)
    tag = jnp.full((SOURCES, HEADS), -1, jnp.int32)
    for s in range(SOURCES):
        tag = jnp.where((slots == s) & (s < count_ref[0]), owner_ref[s], tag)
    tag = tag.astype(jnp.float32).astype(jnp.bfloat16)
    columns = pieces(peak_ref[...], 3) + pieces(total_ref[...], 3) + [tag, tag]
    columns = [column.astype(jnp.float32) for column in columns]
    columns = jnp.concatenate(columns, axis=1).astype(jnp.bfloat16)
    out_ref[:, :QUERIES] = sums
    out_ref[:, QUERIES:] = columns


def attend(page_count, page_owner, kept, near, far):
    return pl.pallas_call(
        attend_kernel,
        out_shape=jax.ShapeDtypeStruct((SOURCES, QUERIES + EXTRA), jnp.bfloat16),
        in_specs=[SMEM] * 2 + [VMEM] * 3,
        out_specs=VMEM,
        scratch_shapes=[
            pltpu.VMEM((SOURCES, QUERIES), jnp.float32),
            pltpu.VMEM((SOURCES, HEADS), jnp.float32),
            pltpu.VMEM((SOURCES, HEADS), jnp.float32),
        ],
        name="attend",
    )(page_count, page_owner, kept, near, far)


def spread_dot(value, chosen, contract, count, chosen_first=False):
    total = None
    for part in pieces(value, count):
        operands = (chosen, part) if chosen_first else (part, chosen)
        term = lax.dot_general(
            *operands, (contract, ((), ())), preferred_element_type=jnp.float32
        )
        total = term if total is None else total + term
    return total


def head_columns():
    head = lax.broadcasted_iota(jnp.int32, (HEADS, QUERIES), 0) * HEAD_DIM
    lane = lax.broadcasted_iota(jnp.int32, (HEADS, QUERIES), 1)
    return ((lane >= head) & (lane < head + HEAD_DIM)).astype(jnp.float32).astype(jnp.bfloat16)


def own_kernel(near_ref, far_ref, own_ref, query_ref, pair_ref):
    scale = HEAD_DIM ** (-0.5)
    share = near_ref.shape[1]
    piece = HEAD_DIM // 2
    for holder in range(HOLDERS):
        rows = slice(holder * share, (holder + 1) * share)
        for half in range(2):
            block = held(near_ref, far_ref, holder, half, pl.ds(0, HALF_COLUMNS))
            for k in range(2):
                at = (2 * k + half) * KEYS
                query_ref[rows, at : at + KEYS] = block[:, k * KEYS : (k + 1) * KEYS]
            pair_ref[half, rows, :] = block[:, QUERIES // 2 :]
    keys, values = [], []
    for g in range(KV_HEADS):
        for half in range(2):
            keys.append(pair_ref[half, :, g * piece : (g + 1) * piece])
            at = KEYS // 2 + g * piece
            values.append(pair_ref[half, :, at : at + piece])
    key = jnp.concatenate(keys, axis=1)
    own_ref[:, :KEYS] = jnp.concatenate(values, axis=1)
    product = query_ref[...] * jnp.concatenate([key] * REPEAT, axis=1)
    own_ref[:, KEYS:] = jnp.concatenate(
        [scale * spread_dot(product, head_columns(), ((1,), (1,)), 3)] * 4, axis=1
    )


def own_part(near, far):
    requests = HOLDERS * near.shape[1]
    return pl.pallas_call(
        own_kernel,
        out_shape=jax.ShapeDtypeStruct((requests, KEYS + 4 * HEADS), jnp.float32),
        in_specs=[VMEM, VMEM],
        out_specs=VMEM,
        scratch_shapes=[
            pltpu.VMEM((requests, QUERIES), jnp.float32),
            pltpu.VMEM((2, requests, KEYS), jnp.float32),
        ],
        name="own_part",
    )(near, far)


def combine_kernel(part_ref, own_ref, out_ref):
    requests = out_ref.shape[0]
    slots = part_ref.shape[0]
    extra = part_ref[:, QUERIES:].astype(jnp.float32)
    column = [extra[:, i * HEADS : (i + 1) * HEADS] for i in range(7)]
    peaks = column[0] + column[1] + column[2]
    totals = column[3] + column[4] + column[5]
    tag = column[6][:, :1]
    member = (
        tag == lax.broadcasted_iota(jnp.int32, (slots, requests), 1).astype(jnp.float32)
    ).astype(jnp.float32).astype(jnp.bfloat16)
    expand = head_columns()
    own = own_ref[:, KEYS : KEYS + HEADS]
    quarter = slots // 4
    beside = [
        jnp.concatenate([block[i * quarter : (i + 1) * quarter] for i in range(4)], axis=1)
        for block in (peaks, column[6])
    ]
    row = lax.broadcasted_iota(jnp.int32, (requests, 4 * HEADS), 0).astype(jnp.float32)
    tops = [jnp.full(row.shape, NEGATIVE, jnp.float32)] * 2
    for s in range(quarter):
        tops[s % 2] = jnp.maximum(
            tops[s % 2],
            jnp.where(beside[1][s : s + 1] == row, beside[0][s : s + 1], NEGATIVE),
        )
    wide = jnp.maximum(tops[0], tops[1])
    top = own
    for i in range(4):
        top = jnp.maximum(top, wide[:, i * HEADS : (i + 1) * HEADS])
    own_weight = jnp.exp(own - top)
    weight = jnp.exp(peaks - spread_dot(top, member, ((1,), (0,)), 3, True))
    total = spread_dot(weight * totals, member, ((0,), (0,)), 3, True) + own_weight
    inverse = 1.0 / total
    weight = weight * spread_dot(inverse, member, ((1,), (0,)), 3, True)
    scaled = part_ref[:, :QUERIES].astype(jnp.float32) * spread_dot(weight, expand, ((1,), (0,)), 2)
    mixed = spread_dot(scaled, member, ((0,), (0,)), 2, True)
    own_share = spread_dot(own_weight * inverse, expand, ((1,), (0,)), 2)
    mixed = mixed + own_share * jnp.concatenate([own_ref[:, :KEYS]] * REPEAT, axis=1)
    mixed = mixed.astype(jnp.bfloat16)
    for h in range(HEADS):
        at = (h % REPEAT * KV_HEADS + h // REPEAT) * HEAD_DIM
        out_ref[:, h * HEAD_DIM : (h + 1) * HEAD_DIM] = mixed[:, at : at + HEAD_DIM]


def combine(parts, own):
    return pl.pallas_call(
        combine_kernel,
        out_shape=jax.ShapeDtypeStruct((own.shape[0], QUERIES), jnp.bfloat16),
        in_specs=[VMEM] * 2,
        out_specs=VMEM,
        compiler_params=pltpu.CompilerParams(vmem_limit_bytes=48 * 1024 * 1024),
        name="combine",
    )(parts, own)


def settle_kernel(in_ref, out_ref):
    out_ref[...] = in_ref[...]


def settle(pages):
    block = pl.BlockSpec((4,) + pages.shape[1:], lambda i: (i, 0, 0))
    return pl.pallas_call(
        settle_kernel,
        out_shape=jax.ShapeDtypeStruct(pages.shape, pages.dtype),
        grid=(pages.shape[0] // 4,),
        in_specs=[block],
        out_specs=block,
        name="settle",
    )(pages)


def per_device(
    tokens, norm_gain, w_query, w_keyvalue, cache, page_count, page_owner, keep_rows, dest_slot
):
    holder = lax.axis_index("page")
    group = lax.axis_index("tensor")
    half = group % 2
    share = tokens.shape[0] // HOLDERS

    def normalise(rows):
        widened = rows.astype(jnp.float32)
        return (
            widened
            * lax.rsqrt(jnp.mean(widened * widened, axis=-1, keepdims=True) + EPSILON)
            * norm_gain
        ).astype(jnp.bfloat16)

    page_count = page_count.reshape(1)
    page_owner = page_owner.reshape(SOURCES)
    compact, kept = select_rows(page_count, dest_slot.reshape(SOURCES), keep_rows, cache)

    mine = normalise(lax.dynamic_slice_in_dim(tokens, holder * share, share, 0))
    across = lax.ppermute(mine, ("page", "tensor"), OTHER_HALF)
    across, compact = lax.optimization_barrier((across, compact))
    arrived = lax.all_to_all(compact, "page", 0, 0, tiled=True)

    both = jnp.where(
        half == 0,
        jnp.concatenate([mine, across], axis=0),
        jnp.concatenate([across, mine], axis=0),
    )
    rows = lax.all_gather(
        both, "tensor", axis=0, axis_index_groups=PLANE_GROUPS, tiled=True
    )
    projected = project(rows, w_query, w_keyvalue)
    everyone = lax.all_gather(
        projected, "tensor", axis=0, axis_index_groups=PLANE_GROUPS, tiled=False
    )
    halves = pick((group // 2).reshape(1), everyone)
    halves, arrived = lax.optimization_barrier((halves, arrived))
    near = lax.all_to_all(
        halves, ("page", "tensor"), 0, 0, axis_index_groups=COLUMN_GROUPS, tiled=True
    )
    near, settled = lax.optimization_barrier((near, settle(arrived)))
    far = lax.ppermute(near, "page", OTHER_CORE)
    part = attend(page_count, page_owner, kept, near, far)
    own = own_part(near, far)
    far = lax.ppermute(part, "page", OTHER_QUAD)
    far, own = lax.optimization_barrier((far, own))
    parts = lax.all_gather(
        jnp.concatenate([part, far], axis=0),
        "page",
        axis=0,
        axis_index_groups=QUAD_GROUPS,
        tiled=True,
    )
    return combine(parts, own), settled[:, None]


def solution(mesh):
    return jax.shard_map(
        per_device,
        mesh=mesh,
        in_specs=(
            P("tensor", None),
            P(),
            P(None, "tensor"),
            P(None, "tensor"),
            P("page", "tensor", None, None),
            P("page", "tensor"),
            P("page", "tensor"),
            P("page", "tensor", None),
            P("page", "tensor"),
        ),
        out_specs=(P("tensor", None), P("page", "tensor", None, None)),
        check_vma=False,
    )
```

```python
import jax
import jax.numpy as jnp
from jax import lax
from jax.experimental import pallas as pl
from jax.experimental.pallas import tpu as pltpu
from jax.sharding import PartitionSpec as P

HEADS = 32
KV_HEADS = 8
REPEAT = HEADS // KV_HEADS
HEAD_DIM = 80
KEYS = KV_HEADS * HEAD_DIM
QUERIES = HEADS * HEAD_DIM
EPSILON = 1e-05
NEGATIVE = -1e30

PLANE = 16
HOLDERS = 16
SOURCES = 8
KEEP = 32
EXTRA = 256

CHIPS = 8
ROW_GROUPS = [[(x * 4 + y) * 2 + half for y in range(4)] for x in range(4) for half in range(2)]
LINE_GROUPS = [[(x * 4 + y) * 2 + half for x in range(4)] for y in range(4) for half in range(2)]
PLANE_GROUPS = [[2 * i + half for i in range(PLANE)] for half in range(2)]
OTHER_HALF = [
    (p * 2 * PLANE + t, (p ^ 8) * 2 * PLANE + (t ^ 1)) for p in range(HOLDERS) for t in range(2 * PLANE)
]

COLUMN_GROUPS = [
    [(2 * z + core) * 2 * PLANE + 2 * xy + half for half in range(2) for z in range(CHIPS)]
    for xy in range(PLANE)
    for core in range(2)
]
QUAD_GROUPS = [[CHIPS * quad + i for i in range(CHIPS)] for quad in range(2)]
OTHER_CORE = [(i, i ^ 1) for i in range(HOLDERS)]
OTHER_QUAD = [(i, i ^ CHIPS) for i in range(HOLDERS)]
HALF_COLUMNS = (QUERIES + 2 * KEYS) // 2
STEP = 4

VMEM = pl.BlockSpec(memory_space=pltpu.VMEM)
SMEM = pl.BlockSpec(memory_space=pltpu.SMEM)


def select_kernel(count_ref, dest_ref, keep_ref, page_ref, out_ref, kept_ref):
    step = pl.program_id(0)

    @pl.when(step == 0)
    def _():
        out_ref[...] = jnp.zeros_like(out_ref)

    rows = page_ref.shape[1]
    for i in range(STEP):
        slot = step * STEP + i
        chosen = keep_ref[i] == lax.broadcasted_iota(jnp.int32, (rows, KEEP), 0)
        kept = lax.dot_general(
            chosen.astype(jnp.float32).astype(jnp.bfloat16),
            page_ref[i],
            (((0,), (0,)), ((), ())),
            preferred_element_type=jnp.float32,
        ).astype(jnp.bfloat16)
        kept_ref[i * KEEP : (i + 1) * KEEP] = kept

        @pl.when(slot < count_ref[0])
        def _():
            out_ref[dest_ref[slot]] = kept


def select_rows(page_count, dest_slot, keep_rows, cache):
    sources, _, rows, width = cache.shape
    return pl.pallas_call(
        select_kernel,
        out_shape=(
            jax.ShapeDtypeStruct((HOLDERS, KEEP, width), cache.dtype),
            jax.ShapeDtypeStruct((sources * KEEP, width), cache.dtype),
        ),
        grid_spec=pltpu.PrefetchScalarGridSpec(
            num_scalar_prefetch=2,
            grid=(sources // STEP,),
            in_specs=[
                pl.BlockSpec((STEP, 1, KEEP), lambda s, *_: (s, 0, 0)),
                pl.BlockSpec((STEP, rows, width), lambda s, *_: (s, 0, 0)),
            ],
            out_specs=[
                pl.BlockSpec((HOLDERS, KEEP, width), lambda s, *_: (0, 0, 0)),
                pl.BlockSpec((STEP * KEEP, width), lambda s, *_: (s, 0)),
            ],
        ),
        name="select_rows",
    )(page_count, dest_slot, keep_rows, cache.reshape(sources, rows, width))


def project_kernel(rows_ref, query_ref, pair_ref, out_ref):
    rows = rows_ref[...]
    for ref, low, high in ((query_ref, 0, HEAD_DIM), (pair_ref, HEAD_DIM, HEAD_DIM * 3 // 2)):
        out_ref[:, low:high] = lax.dot_general(
            rows, ref[...], (((1,), (1,)), ((), ())), preferred_element_type=jnp.float32
        ).astype(jnp.bfloat16)


def project(rows, w_query, w_keyvalue):
    return pl.pallas_call(
        project_kernel,
        out_shape=jax.ShapeDtypeStruct((rows.shape[0], HEAD_DIM * 3 // 2), jnp.bfloat16),
        in_specs=[VMEM] * 3,
        out_specs=VMEM,
        name="project",
    )(rows, w_query.T, w_keyvalue.T)


def pick_kernel(plane_ref, all_ref, out_ref, rows_ref):
    half = HEAD_DIM // 2
    for i in range(PLANE):
        block = all_ref[i].astype(jnp.float32)
        at = (i % 2 * KV_HEADS + i // 2) * HEAD_DIM
        rows_ref[:, at : at + HEAD_DIM] = block[:, :HEAD_DIM]
        at = QUERIES // 2 + i * half
        rows_ref[:, at : at + half] = block[:, HEAD_DIM:]
    share = out_ref.shape[1]
    for h in range(2):
        piece = rows_ref[h * share : (h + 1) * share].astype(jnp.bfloat16)
        for z in range(CHIPS):
            out_ref[h * CHIPS + z] = piece


def pick(plane, everyone):
    count, rows, width = everyone.shape
    both = rows // PLANE
    piece = jax.ShapeDtypeStruct((2 * CHIPS, both // 2, HALF_COLUMNS), everyone.dtype)
    return pl.pallas_call(
        pick_kernel,
        out_shape=piece,
        grid_spec=pltpu.PrefetchScalarGridSpec(
            num_scalar_prefetch=1,
            grid=(1,),
            in_specs=[pl.BlockSpec((count, both, width), lambda i, plane: (0, plane[0], 0))],
            out_specs=pl.BlockSpec(piece.shape, lambda i, *_: (0, 0, 0)),
            scratch_shapes=[pltpu.VMEM((both, HALF_COLUMNS), jnp.float32)],
        ),
        name="pick",
    )(plane, everyone)


def held(near_ref, far_ref, holder, half, columns):
    chip = holder // 2
    spot = half * CHIPS + jnp.where(lax.axis_index("tensor") % 2 == half, chip, chip ^ 4)
    near = near_ref[spot, :, columns].astype(jnp.float32)
    far = far_ref[spot, :, columns].astype(jnp.float32)
    return jnp.where(lax.axis_index("page") % 2 == holder % 2, near, far)


def pieces(value, count):
    parts = []
    for _ in range(count):
        part = value.astype(jnp.bfloat16)
        parts.append(part)
        value = value - part.astype(jnp.float32)
    return parts


def attend_kernel(
    count_ref, owner_ref, kept_ref, near_ref, far_ref, out_ref, sum_ref, peak_ref, total_ref
):
    scale = HEAD_DIM ** (-0.5)
    share = near_ref.shape[1]
    line = lax.broadcasted_iota(jnp.int32, (share, QUERIES // 2), 0)
    head = lax.broadcasted_iota(jnp.int32, (KV_HEADS, KEYS), 0) * HEAD_DIM
    lane = lax.broadcasted_iota(jnp.int32, (KV_HEADS, KEYS), 1)
    mask = ((lane >= head) & (lane < head + HEAD_DIM)).astype(jnp.float32)
    for s in range(SOURCES):
        request = owner_ref[s]
        holder = request // share
        query = []
        for half in range(2):
            block = held(near_ref, far_ref, holder, half, pl.ds(0, QUERIES // 2))
            query.append(
                jnp.sum(jnp.where(line == request % share, block, 0.0), axis=0, keepdims=True)
            )
        spread = jnp.concatenate(
            [
                query[k % 2][:, k // 2 * KEYS : (k // 2 + 1) * KEYS] * mask
                for k in range(REPEAT)
            ],
            axis=0,
        ).astype(jnp.bfloat16)
        keys = kept_ref[s * KEEP : (s + 1) * KEEP, :KEYS]
        values = kept_ref[s * KEEP : (s + 1) * KEEP, KEYS:]
        score = scale * lax.dot_general(
            keys, spread, (((1,), (1,)), ((), ())), preferred_element_type=jnp.float32
        )
        peak = jnp.max(score, axis=0, keepdims=True)
        weight = jnp.exp(score - peak)
        total_ref[s : s + 1, :] = jnp.sum(weight, axis=0, keepdims=True)
        peak_ref[s : s + 1, :] = jnp.where(s < count_ref[0], peak, NEGATIVE)
        mixed = lax.dot_general(
            weight.astype(jnp.bfloat16),
            values,
            (((0,), (0,)), ((), ())),
            preferred_element_type=jnp.float32,
        )
        for k in range(REPEAT):
            sum_ref[s : s + 1, k * KEYS : (k + 1) * KEYS] = jnp.sum(
                mixed[k * KV_HEADS : (k + 1) * KV_HEADS] * mask, axis=0, keepdims=True
            )
    sums = sum_ref[...].astype(jnp.bfloat16)
    slots = lax.broadcasted_iota(jnp.int32, (SOURCES, HEADS), 0)
    tag = jnp.full((SOURCES, HEADS), -1, jnp.int32)
    for s in range(SOURCES):
        tag = jnp.where((slots == s) & (s < count_ref[0]), owner_ref[s], tag)
    tag = tag.astype(jnp.float32).astype(jnp.bfloat16)
    columns = pieces(peak_ref[...], 3) + pieces(total_ref[...], 3) + [tag, tag]
    columns = [column.astype(jnp.float32) for column in columns]
    columns = jnp.concatenate(columns, axis=1).astype(jnp.bfloat16)
    out_ref[:, :QUERIES] = sums
    out_ref[:, QUERIES:] = columns


def attend(page_count, page_owner, kept, near, far):
    return pl.pallas_call(
        attend_kernel,
        out_shape=jax.ShapeDtypeStruct((SOURCES, QUERIES + EXTRA), jnp.bfloat16),
        in_specs=[SMEM] * 2 + [VMEM] * 3,
        out_specs=VMEM,
        scratch_shapes=[
            pltpu.VMEM((SOURCES, QUERIES), jnp.float32),
            pltpu.VMEM((SOURCES, HEADS), jnp.float32),
            pltpu.VMEM((SOURCES, HEADS), jnp.float32),
        ],
        name="attend",
    )(page_count, page_owner, kept, near, far)


def spread_dot(value, chosen, contract, count, chosen_first=False):
    total = None
    for part in pieces(value, count):
        operands = (chosen, part) if chosen_first else (part, chosen)
        term = lax.dot_general(
            *operands, (contract, ((), ())), preferred_element_type=jnp.float32
        )
        total = term if total is None else total + term
    return total


def head_columns():
    head = lax.broadcasted_iota(jnp.int32, (HEADS, QUERIES), 0) * HEAD_DIM
    lane = lax.broadcasted_iota(jnp.int32, (HEADS, QUERIES), 1)
    return ((lane >= head) & (lane < head + HEAD_DIM)).astype(jnp.float32).astype(jnp.bfloat16)


def own_kernel(near_ref, far_ref, own_ref, query_ref, pair_ref):
    scale = HEAD_DIM ** (-0.5)
    share = near_ref.shape[1]
    piece = HEAD_DIM // 2
    for holder in range(HOLDERS):
        rows = slice(holder * share, (holder + 1) * share)
        for half in range(2):
            block = held(near_ref, far_ref, holder, half, pl.ds(0, HALF_COLUMNS))
            for k in range(2):
                at = (2 * k + half) * KEYS
                query_ref[rows, at : at + KEYS] = block[:, k * KEYS : (k + 1) * KEYS]
            pair_ref[half, rows, :] = block[:, QUERIES // 2 :]
    keys, values = [], []
    for g in range(KV_HEADS):
        for half in range(2):
            keys.append(pair_ref[half, :, g * piece : (g + 1) * piece])
            at = KEYS // 2 + g * piece
            values.append(pair_ref[half, :, at : at + piece])
    key = jnp.concatenate(keys, axis=1)
    own_ref[:, :KEYS] = jnp.concatenate(values, axis=1)
    product = query_ref[...] * jnp.concatenate([key] * REPEAT, axis=1)
    own_ref[:, KEYS:] = jnp.concatenate(
        [scale * spread_dot(product, head_columns(), ((1,), (1,)), 3)] * 4, axis=1
    )


def own_part(near, far):
    requests = HOLDERS * near.shape[1]
    return pl.pallas_call(
        own_kernel,
        out_shape=jax.ShapeDtypeStruct((requests, KEYS + 4 * HEADS), jnp.float32),
        in_specs=[VMEM, VMEM],
        out_specs=VMEM,
        scratch_shapes=[
            pltpu.VMEM((requests, QUERIES), jnp.float32),
            pltpu.VMEM((2, requests, KEYS), jnp.float32),
        ],
        name="own_part",
    )(near, far)


def combine_kernel(part_ref, own_ref, out_ref):
    requests = out_ref.shape[0]
    slots = part_ref.shape[0]
    extra = part_ref[:, QUERIES:].astype(jnp.float32)
    column = [extra[:, i * HEADS : (i + 1) * HEADS] for i in range(7)]
    peaks = column[0] + column[1] + column[2]
    totals = column[3] + column[4] + column[5]
    tag = column[6][:, :1]
    member = (
        tag == lax.broadcasted_iota(jnp.int32, (slots, requests), 1).astype(jnp.float32)
    ).astype(jnp.float32).astype(jnp.bfloat16)
    expand = head_columns()
    own = own_ref[:, KEYS : KEYS + HEADS]
    quarter = slots // 4
    beside = [
        jnp.concatenate([block[i * quarter : (i + 1) * quarter] for i in range(4)], axis=1)
        for block in (peaks, column[6])
    ]
    row = lax.broadcasted_iota(jnp.int32, (requests, 4 * HEADS), 0).astype(jnp.float32)
    tops = [jnp.full(row.shape, NEGATIVE, jnp.float32)] * 2
    for s in range(quarter):
        tops[s % 2] = jnp.maximum(
            tops[s % 2],
            jnp.where(beside[1][s : s + 1] == row, beside[0][s : s + 1], NEGATIVE),
        )
    wide = jnp.maximum(tops[0], tops[1])
    top = own
    for i in range(4):
        top = jnp.maximum(top, wide[:, i * HEADS : (i + 1) * HEADS])
    own_weight = jnp.exp(own - top)
    weight = jnp.exp(peaks - spread_dot(top, member, ((1,), (0,)), 3, True))
    total = spread_dot(weight * totals, member, ((0,), (0,)), 3, True) + own_weight
    inverse = 1.0 / total
    weight = weight * spread_dot(inverse, member, ((1,), (0,)), 3, True)
    scaled = part_ref[:, :QUERIES].astype(jnp.float32) * spread_dot(weight, expand, ((1,), (0,)), 2)
    mixed = spread_dot(scaled, member, ((0,), (0,)), 2, True)
    own_share = spread_dot(own_weight * inverse, expand, ((1,), (0,)), 2)
    mixed = mixed + own_share * jnp.concatenate([own_ref[:, :KEYS]] * REPEAT, axis=1)
    mixed = mixed.astype(jnp.bfloat16)
    for h in range(HEADS):
        at = (h % REPEAT * KV_HEADS + h // REPEAT) * HEAD_DIM
        out_ref[:, h * HEAD_DIM : (h + 1) * HEAD_DIM] = mixed[:, at : at + HEAD_DIM]


def combine(parts, own):
    return pl.pallas_call(
        combine_kernel,
        out_shape=jax.ShapeDtypeStruct((own.shape[0], QUERIES), jnp.bfloat16),
        in_specs=[VMEM] * 2,
        out_specs=VMEM,
        compiler_params=pltpu.CompilerParams(vmem_limit_bytes=48 * 1024 * 1024),
        name="combine",
    )(parts, own)


def settle_kernel(in_ref, out_ref):
    out_ref[...] = in_ref[...]


def settle(pages):
    block = pl.BlockSpec((4,) + pages.shape[1:], lambda i: (i, 0, 0))
    return pl.pallas_call(
        settle_kernel,
        out_shape=jax.ShapeDtypeStruct(pages.shape, pages.dtype),
        grid=(pages.shape[0] // 4,),
        in_specs=[block],
        out_specs=block,
        name="settle",
    )(pages)


def per_device(
    tokens, norm_gain, w_query, w_keyvalue, cache, page_count, page_owner, keep_rows, dest_slot
):
    holder = lax.axis_index("page")
    group = lax.axis_index("tensor")
    half = group % 2
    share = tokens.shape[0] // HOLDERS

    def normalise(rows):
        widened = rows.astype(jnp.float32)
        return (
            widened
            * lax.rsqrt(jnp.mean(widened * widened, axis=-1, keepdims=True) + EPSILON)
            * norm_gain
        ).astype(jnp.bfloat16)

    page_count = page_count.reshape(1)
    page_owner = page_owner.reshape(SOURCES)
    compact, kept = select_rows(page_count, dest_slot.reshape(SOURCES), keep_rows, cache)

    mine = normalise(lax.dynamic_slice_in_dim(tokens, holder * share, share, 0))
    across = lax.ppermute(mine, ("page", "tensor"), OTHER_HALF)
    across, compact = lax.optimization_barrier((across, compact))
    arrived = lax.all_to_all(compact, "page", 0, 0, tiled=True)

    both = jnp.where(
        half == 0,
        jnp.concatenate([mine, across], axis=0),
        jnp.concatenate([across, mine], axis=0),
    )
    rows = both
    for plane_groups in (ROW_GROUPS, LINE_GROUPS):
        rows = lax.all_gather(
            rows, "tensor", axis=0, axis_index_groups=plane_groups, tiled=True
        )
    projected = project(rows, w_query, w_keyvalue)
    everyone = lax.all_gather(
        projected, "tensor", axis=0, axis_index_groups=PLANE_GROUPS, tiled=False
    )
    halves = pick((group // 2).reshape(1), everyone)
    halves, arrived = lax.optimization_barrier((halves, arrived))
    near = lax.all_to_all(
        halves, ("page", "tensor"), 0, 0, axis_index_groups=COLUMN_GROUPS, tiled=True
    )
    near, settled = lax.optimization_barrier((near, settle(arrived)))
    far = lax.ppermute(near, "page", OTHER_CORE)
    part = attend(page_count, page_owner, kept, near, far)
    own = own_part(near, far)
    far = lax.ppermute(part, "page", OTHER_QUAD)
    far, own = lax.optimization_barrier((far, own))
    parts = lax.all_gather(
        jnp.concatenate([part, far], axis=0),
        "page",
        axis=0,
        axis_index_groups=QUAD_GROUPS,
        tiled=True,
    )
    return combine(parts, own), settled[:, None]


def solution(mesh):
    return jax.shard_map(
        per_device,
        mesh=mesh,
        in_specs=(
            P("tensor", None),
            P(),
            P(None, "tensor"),
            P(None, "tensor"),
            P("page", "tensor", None, None),
            P("page", "tensor"),
            P("page", "tensor"),
            P("page", "tensor", None),
            P("page", "tensor"),
        ),
        out_specs=(P("tensor", None), P("page", "tensor", None, None)),
        check_vma=False,
    )
```
